32 devices in a mesh: groups: 1, seq: 32 (over z, y, x, core).
Axes of the slice: x: 2, y: 2, z: 4, core: 2. Of those that a mesh axis runs over, the one named last changes fastest.
Arguments:
- queries: bfloat16 [8192, 1280], P(('groups', 'seq')), may hold values from -8 to 8
- key_rows: bfloat16 [8192, 1280], P(('groups', 'seq')), may hold values from -8 to 8
- value_rows: bfloat16 [8192, 1280], P(('groups', 'seq')), may hold values from -8 to 8
- step_rates: float32 [2, 8192], P(None, ('groups', 'seq')), may hold values from 0.02 to 0.2
- fast_weights: float32 [3, 1280, 640], P(None, 'seq'), may hold values from -0.25 to 0.25
- momentum: float32 [3, 1280, 640], P('groups', 'seq'), may hold values from -0.18 to 0.18
- out_gain: float32 [1280], replicated, may hold values from 0.5 to 1.5
Outputs:
- layer_out: bfloat16 [8192, 1280], P(('groups', 'seq'))
- new_weights: float32 [3, 1280, 640], P('groups', 'seq')
- new_momentum: float32 [3, 1280, 640], P('groups', 'seq')
The draws below stay inside these ranges and needn't reach their ends.
All inputs are finite; a program needn't handle non-finite values.
Results may differ from the reference program's by a relative error of at most 0.0089.
Values may be sent and summed in bfloat16 or wider, within the bound.
No kernel may reach another device: no remote copies, remote signals or barrier semaphores. Data moves between devices by JAX's collectives and lax.ppermute only.
A program may use at most 128 MiB of HBM per device.

```python
import math
import jax
import jax.numpy as jnp
from jax import lax

FAST_HEADS = 2
HEAD_DIM = 640
FAST_HIDDEN = 640
ATT_DIM = 128
WINDOW = 1024
WIDTH = 1280
ATT_HEADS = 10
ROWS = 1280
TOKENS = 8192


def pair_draw(key):
    seed_key = jax.random.fold_in(key, 11)
    query_key, row_key = jax.random.split(seed_key, 2)
    query_draw = jnp.clip(jax.random.normal(query_key, (TOKENS, WIDTH), jnp.float32), -8.0, 8.0)
    key_draw = jnp.clip(jax.random.normal(row_key, (TOKENS, WIDTH), jnp.float32), -8.0, 8.0)
    return (query_draw, key_draw)


def draw_queries(key, part):
    return pair_draw(key)[0].astype(jnp.bfloat16)


def draw_key_rows(key, part):
    return pair_draw(key)[1].astype(jnp.bfloat16)


def raised(values, rng, source, target, parts, factor):
    owner, partner = [(jnp.arange(values.shape[dim]) // (values.shape[dim] // parts)).reshape([-1 if axis == dim else 1 for axis in range(values.ndim)]) for dim in (source, target)]
    chosen = jax.random.permutation(rng, parts)[partner]
    strong = (owner == chosen) | (owner == (partner + parts // 2) % parts)
    return jnp.where(strong, factor * values, values)


def block_levels(key, dims, cuts, low, top_value):
    gain = 1.0
    for dim, parts in cuts:
        heights = jax.random.uniform(jax.random.fold_in(jax.random.fold_in(key, 6), dim), (parts,), jnp.float32, low / len(cuts), top_value / len(cuts))
        gain = gain * jnp.repeat(jnp.exp(heights), dims[dim] // parts).reshape((-1,) + (1,) * (len(dims) - 1 - dim))
    return gain


def gaussian(stream_key, extent, scale, most, shards=(), kind=jnp.bfloat16):
    result = jax.random.normal(stream_key, extent, jnp.float32) * scale
    if len(shards) > 0:
        result = block_levels(stream_key, extent, shards, -0.22, 0.18) * result
    return jnp.clip(result, min=-most, max=most).astype(kind)


def noise_with(own_key, shape, spread, limit, cuts, heavy, kind=jnp.bfloat16):
    entries = spread * jax.random.normal(own_key, shape, jnp.float32)
    if cuts:
        entries = entries * block_levels(own_key, shape, cuts, -0.22, 0.18)
    return jnp.clip(raised(entries, jax.random.fold_in(own_key, 3), *heavy), -limit, limit).astype(kind)


def setup_inputs(seed: int = 0, part: int = 0) -> dict:
    seeds = jax.random.split(jax.random.key(seed), 8)
    own_keys = jax.random.split(jax.random.fold_in(seeds[7], part), 8)
    queries = draw_queries(jax.random.fold_in(jax.random.fold_in(seeds[7], part), 71), part)
    key_rows = draw_key_rows(jax.random.fold_in(jax.random.fold_in(seeds[7], part), 71), part)
    value_rows = noise_with(own_keys[2], (TOKENS, WIDTH), 1.0, 8.0, ((0, 32),), (0, 1, 32, 2.75))
    step_rates = jnp.clip(jnp.exp(math.log(0.2) - 2.3025851 * jax.random.uniform(own_keys[3], (FAST_HEADS, TOKENS), jnp.float32) ** block_levels(own_keys[3], (FAST_HEADS, TOKENS), ((1, 32),), -0.2, 0.2)), 0.02, 0.2)
    fast_weights = gaussian(seeds[4], (3, ROWS, HEAD_DIM), HEAD_DIM ** -0.5, 0.25, ((1, 32),), jnp.float32)
    momentum = gaussian(own_keys[5], (3, ROWS, HEAD_DIM), 0.03, 0.18, ((1, 32),), jnp.float32)
    out_gain = jnp.clip(1.0 + 0.1 * jax.random.normal(seeds[6], (WIDTH,), jnp.float32), 0.5, 1.5)
    return dict(queries=queries, key_rows=key_rows, value_rows=value_rows, step_rates=step_rates, fast_weights=fast_weights, momentum=momentum, out_gain=out_gain)


def silu_slope(values_in):
    sigmoid_val = jax.nn.sigmoid(values_in)
    return sigmoid_val * (1.0 + values_in * (1.0 - sigmoid_val))

def row_product(left_side, right_side):
    return lax.dot_general(left_side, right_side, (((1,), (1,)), ((), ())), preferred_element_type=jnp.float32)

def token_product(left_side, right_side):
    return lax.dot_general(left_side, right_side, (((0,), (0,)), ((), ())), preferred_element_type=jnp.float32)

def reference(queries, key_rows, value_rows, step_rates, fast_weights, momentum, out_gain):
    weight_copy = fast_weights.astype(jnp.bfloat16)
    grad_scale = 1.0 / math.sqrt(TOKENS)
    gate_list, up_list, down_list = ([], [], [])
    for head_idx in range(FAST_HEADS):
        col_lo = head_idx * HEAD_DIM
        row_lo = head_idx * FAST_HIDDEN
        key_head = key_rows[:, col_lo:col_lo + HEAD_DIM]
        value_head = value_rows[:, col_lo:col_lo + HEAD_DIM]
        key_gate = row_product(key_head, weight_copy[0, row_lo:row_lo + FAST_HIDDEN])
        key_up = row_product(key_head, weight_copy[1, row_lo:row_lo + FAST_HIDDEN])
        key_hidden = (jax.nn.silu(key_gate) * key_up).astype(jnp.bfloat16)
        out_grad = (-grad_scale * step_rates[head_idx][:, None] * value_head.astype(jnp.float32)).astype(jnp.bfloat16)
        hidden_grad = row_product(out_grad, weight_copy[2, row_lo:row_lo + FAST_HIDDEN])
        gate_grad = (hidden_grad * key_up * silu_slope(key_gate)).astype(jnp.bfloat16)
        up_grad = (hidden_grad * jax.nn.silu(key_gate)).astype(jnp.bfloat16)
        gate_list.append(token_product(gate_grad, key_head))
        up_list.append(token_product(up_grad, key_head))
        down_list.append(token_product(key_hidden, out_grad))
    gradient = jnp.stack([jnp.concatenate(gate_list, 0), jnp.concatenate(up_list, 0), jnp.concatenate(down_list, 0)])
    new_momentum = 0.9 * momentum + gradient
    moved_rows = fast_weights - new_momentum
    keep_norm = jnp.sqrt(lax.optimization_barrier(jnp.mean(fast_weights * fast_weights, axis=-1, keepdims=True)))
    new_weights = moved_rows * keep_norm * lax.rsqrt(lax.optimization_barrier(jnp.mean(moved_rows * moved_rows, axis=-1, keepdims=True)) + 1e-06)
    applied = new_weights.astype(jnp.bfloat16)
    fast_list = []
    for head_idx in range(FAST_HEADS):
        col_lo = head_idx * HEAD_DIM
        row_lo = head_idx * FAST_HIDDEN
        query_head = queries[:, col_lo:col_lo + HEAD_DIM]
        query_gate = row_product(query_head, applied[0, row_lo:row_lo + FAST_HIDDEN])
        query_up = row_product(query_head, applied[1, row_lo:row_lo + FAST_HIDDEN])
        query_hidden = (jax.nn.silu(query_gate) * query_up).astype(jnp.bfloat16)
        fast_out = jnp.dot(query_hidden, applied[2, row_lo:row_lo + FAST_HIDDEN], preferred_element_type=jnp.float32)
        fast_normed = fast_out * lax.rsqrt(lax.optimization_barrier(jnp.mean(fast_out * fast_out, axis=-1, keepdims=True)) + 1e-06) * out_gain[col_lo:col_lo + HEAD_DIM]
        fast_list.append(fast_normed)
    fast_all = jnp.concatenate(fast_list, axis=1)
    block_rows = min(TOKENS, 512)
    key_padded = jnp.concatenate([jnp.zeros((WINDOW, WIDTH), jnp.bfloat16), key_rows], axis=0)
    value_padded = jnp.concatenate([jnp.zeros((WINDOW, WIDTH), jnp.bfloat16), value_rows], axis=0)

    def one_block(block_start):
        query_block = lax.dynamic_slice_in_dim(queries, block_start, block_rows, 0)
        key_block = lax.dynamic_slice_in_dim(key_padded, block_start, block_rows + WINDOW, 0)
        value_block = lax.dynamic_slice_in_dim(value_padded, block_start, block_rows + WINDOW, 0)
        query_heads = query_block.reshape(block_rows, ATT_HEADS, ATT_DIM).astype(jnp.float32)
        key_heads = key_block.reshape(block_rows + WINDOW, ATT_HEADS, ATT_DIM).astype(jnp.float32)
        value_heads = value_block.reshape(block_rows + WINDOW, ATT_HEADS, ATT_DIM).astype(jnp.float32)
        scores = jnp.einsum('qhd,khd->hqk', query_heads, key_heads) / math.sqrt(ATT_DIM)
        query_pos = block_start + jnp.arange(block_rows, dtype=jnp.int32)
        key_pos = block_start - WINDOW + jnp.arange(block_rows + WINDOW, dtype=jnp.int32)
        allowed = (key_pos[None, :] <= query_pos[:, None]) & (key_pos[None, :] > query_pos[:, None] - WINDOW) & (key_pos[None, :] >= 0)
        scores = jnp.where(allowed[None], scores, -jnp.inf)
        top_score = lax.optimization_barrier(jnp.max(scores, axis=-1, keepdims=True))
        exp_scores = jnp.exp(scores - top_score)
        att_probs = (exp_scores / lax.optimization_barrier(jnp.sum(exp_scores, axis=-1, keepdims=True))).astype(jnp.bfloat16)
        attended = jnp.einsum('hqk,khd->qhd', att_probs.astype(jnp.float32), value_heads)
        att_normed = attended * lax.rsqrt(lax.optimization_barrier(jnp.mean(attended * attended, axis=-1, keepdims=True)) + 1e-06)
        return att_normed.reshape(block_rows, WIDTH)
    block_starts = jnp.arange(TOKENS // block_rows, dtype=jnp.int32) * block_rows
    att_all = lax.map(one_block, block_starts).reshape(TOKENS, WIDTH)
    layer_out = (fast_all + att_all).astype(jnp.bfloat16)
    return (layer_out, new_weights, new_momentum)
```

```python
import math

import jax
import jax.numpy as jnp
from jax import lax
from jax.experimental import pallas as pl
from jax.experimental.pallas import tpu as pltpu
from jax.sharding import PartitionSpec as P

ATT_DIM = 128
WINDOW = 1024
EPS = 1e-06
MASKED = -1e30
BF16 = jnp.bfloat16
F32 = jnp.float32


class Routes:
    def __init__(self, count):
        self.count = count
        self.z_size = count // 8
        half = self.z_size // 2
        self.bits = [1 << b for b in range(half.bit_length() - 1)]
        assert count % 16 == 0 and half == 1 << len(self.bits)
        home = [dev for dev in range(count) if self.is_home(dev)]
        away = [dev for dev in range(count) if not self.is_home(dev)]
        self.partner = [(dev, dev ^ 1) for dev in range(count)]
        self.x_swap = [(dev, dev ^ 2) for dev in range(count)]
        self.y_swap = [(dev, dev ^ 4) for dev in range(count)]
        self.pair_in = [(dev ^ 1, dev) for dev in home]
        self.pair_out = [(dev, dev ^ 1) for dev in home]
        shift = half * 8
        self.cross_out = [(dev, (dev + shift) % count) for dev in home]
        self.cross_back = [(dev, (dev + shift) % count) for dev in away]
        self.home_swap = {b: [(dev, dev ^ (8 * b)) for dev in home] for b in self.bits}
        self.away_swap = {b: [(dev, dev ^ (8 * b)) for dev in away] for b in self.bits}
        self.z_swap = {b: [(dev, dev ^ (8 * b)) for dev in range(count)] for b in self.bits}
        self.next_x = [(dev, dev + 2) for dev in range(count) if dev % 4 < 2]
        self.next_two = [(dev, dev + 4) for dev in range(count - 4)]
        self.back_x = [(dev, dev - 2) for dev in range(count) if dev % 4 >= 2]

    def is_home(self, dev):
        return (dev % 2) == (2 * dev // self.count)


def send(array, route):
    return lax.ppermute(array, "seq", route)


def gather_rows(block, routes, is_home):
    unit = jnp.concatenate([block, send(block, routes.pair_in)], axis=1)
    home_list = [unit]
    away_list = [send(unit, routes.cross_out)]
    for bit in routes.bits:
        home_list = home_list + [send(part, routes.home_swap[bit]) for part in home_list]
        away_list = away_list + [send(part, routes.away_swap[bit]) for part in away_list]
    pieces = []
    for idx, (home, away) in enumerate(zip(home_list, away_list)):
        own = jnp.where(is_home, home, away)
        first, second = (
            (routes.x_swap, routes.y_swap) if idx % 2 == 0 else (routes.y_swap, routes.x_swap)
        )
        near = send(own, first)
        side = send(own, second)
        pieces += [own, near, side, send(near, second)]
    return pieces


def reduce_rows(grads, routes, is_home, owned):
    sums = []
    for idx in range(len(grads) // 4):
        own, near, side, far = grads[4 * idx : 4 * idx + 4]
        first, second = (
            (routes.x_swap, routes.y_swap) if idx % 2 == 0 else (routes.y_swap, routes.x_swap)
        )
        far_in = send(far, second)
        side_in = send(side, second)
        near_sum = (near + far_in.astype(F32)).astype(BF16)
        near_in = send(near_sum, first)
        sums.append(own + side_in.astype(F32) + near_in.astype(F32))
    for bit in reversed(routes.bits):
        half = len(sums) // 2
        arrived = [send(part.astype(BF16), routes.z_swap[bit]) for part in sums[half:]]
        sums = [low + part.astype(F32) for low, part in zip(sums[:half], arrived)]
    total = sums[0] + send(sums[0].astype(BF16), routes.cross_back).astype(F32)
    other = send(total[:, owned:], routes.pair_out)
    return jnp.where(is_home, total[:, :owned], other)


def nt_dot(left, right):
    return lax.dot_general(left, right, (((1,), (1,)), ((), ())), preferred_element_type=F32)


def nn_dot(left, right):
    return lax.dot_general(left, right, (((1,), (0,)), ((), ())), preferred_element_type=F32)


def key_kernel(count, *refs):
    ka, kb, oa, ob = refs[:4]
    pieces = refs[4 : 4 + count]
    outs = refs[4 + count : 4 + 2 * count]
    keys, ograd, weights = refs[4 + 2 * count :]
    tokens = ka.shape[0]
    rows = pieces[0].shape[1]
    keys[:tokens, :] = ka[...]
    keys[tokens:, :] = kb[...]
    ograd[:tokens, :] = oa[...]
    ograd[tokens:, :] = ob[...]
    for idx in range(count):
        weights[:, idx * rows : (idx + 1) * rows, :] = pieces[idx][...]
    step = 4
    for start in range(0, count, step):
        low, high = start * rows, (start + step) * rows
        gate = nt_dot(weights[0, low:high, :], keys[...])
        up = nt_dot(weights[1, low:high, :], keys[...])
        hidden_grad = nt_dot(weights[2, low:high, :], ograd[...])
        sig = jax.nn.sigmoid(gate)
        silu = gate * sig
        hidden = (silu * up).astype(BF16)
        gate_grad = (hidden_grad * up * (sig * (1.0 + gate * (1.0 - sig)))).astype(BF16)
        up_grad = (hidden_grad * silu).astype(BF16)
        for mat, (left, right) in enumerate(
            ((gate_grad, keys), (up_grad, keys), (hidden, ograd))
        ):
            grad = nn_dot(left, right[...])
            for idx in range(start, start + step):
                base = idx * rows - low
                outs[idx][mat] = grad[base : base + rows, :].astype(outs[idx].dtype)


def vmem():
    return pl.BlockSpec(memory_space=pltpu.VMEM)


def key_side(key_pair, ograd_pair, pieces, out_types):
    tokens, width = key_pair[0].shape
    count = len(pieces)
    rows = pieces[0].shape[1]
    total = 2 * tokens * count * rows * width
    return pl.pallas_call(
        lambda *refs: key_kernel(count, *refs),
        out_shape=[jax.ShapeDtypeStruct(p.shape, t) for p, t in zip(pieces, out_types)],
        in_specs=[vmem()] * (4 + count),
        out_specs=[vmem()] * count,
        scratch_shapes=[
            pltpu.VMEM((2 * tokens, width), BF16),
            pltpu.VMEM((2 * tokens, width), BF16),
            pltpu.VMEM((3, count * rows, width), BF16),
        ],
        cost_estimate=pl.CostEstimate(
            flops=12 * total, bytes_accessed=8 * count * rows * width, transcendentals=0
        ),
        name="key_side",
    )(*key_pair, *ograd_pair, *pieces)


def query_kernel(count, *refs):
    where, qa, qb = refs[:3]
    pieces = refs[3 : 3 + count]
    gain, att, own, other = refs[3 + count : 7 + count]
    quer, weights, result = refs[7 + count :]
    tokens = qa.shape[0]
    rows = pieces[0].shape[1]
    mine = pl.multiple_of(where[0] * tokens, tokens)
    theirs = pl.multiple_of((1 - where[0]) * tokens, tokens)
    quer[pl.ds(mine, tokens), :] = qa[...]
    quer[pl.ds(theirs, tokens), :] = qb[...]
    for idx in range(count):
        weights[:, idx * rows : (idx + 1) * rows, :] = pieces[idx][...]
    gate = nt_dot(quer[...], weights[0])
    up = nt_dot(quer[...], weights[1])
    hidden = (gate * jax.nn.sigmoid(gate) * up).astype(BF16)
    out = nn_dot(hidden, weights[2])
    scale = lax.rsqrt(jnp.mean(out * out, axis=-1, keepdims=True) + EPS)
    result[...] = out * scale * gain[...] + att[...]
    own[...] = result[pl.ds(mine, tokens), :].astype(BF16)
    other[...] = result[pl.ds(theirs, tokens), :].astype(BF16)


def query_side(where, query_pair, pieces, gain, att):
    tokens, width = query_pair[0].shape
    count = len(pieces)
    rows = pieces[0].shape[1]
    total = 2 * tokens * count * rows * width
    return pl.pallas_call(
        lambda *refs: query_kernel(count, *refs),
        out_shape=[jax.ShapeDtypeStruct((tokens, width), BF16)] * 2,
        in_specs=[pl.BlockSpec(memory_space=pltpu.SMEM)] + [vmem()] * (4 + count),
        out_specs=[vmem()] * 2,
        scratch_shapes=[
            pltpu.VMEM((2 * tokens, width), BF16),
            pltpu.VMEM((3, count * rows, width), BF16),
            pltpu.VMEM((2 * tokens, width), F32),
        ],
        cost_estimate=pl.CostEstimate(
            flops=6 * total, bytes_accessed=6 * count * rows * width, transcendentals=0
        ),
        name="query_side",
    )(where, *query_pair, *pieces, gain, att)


def att_kernel(where, *refs):
    blocks = refs[:18]
    out, quer, keys, vals, bias = refs[18:]
    tokens = blocks[0].shape[0]
    span = 2 * tokens
    tile = 128
    reach = WINDOW + tile
    core, odd, chip = where[0], where[1], where[2]
    mine = core * tokens
    theirs = (1 - core) * tokens

    def put(dest, base, pair):
        dest[pl.ds(pl.multiple_of(base + mine, tokens), tokens), :] = pair[0]
        dest[pl.ds(pl.multiple_of(base + theirs, tokens), tokens), :] = pair[1]

    def value(pair):
        return (pair[0][...], pair[1][...])

    put(quer, 0, value(blocks[0:2]))
    for dest, at in ((keys, 2), (vals, 4)):
        put(dest, 2 * span, value(blocks[at : at + 2]))
        put(dest, 0, value(blocks[at + 4 : at + 6]))

        @pl.when(odd == 1)
        def _():
            put(dest, span, value(blocks[at + 8 : at + 10]))

        @pl.when(odd == 0)
        def _():
            put(dest, span, value(blocks[at + 12 : at + 14]))

    scale = 1.0 / math.sqrt(ATT_DIM)
    row = lax.broadcasted_iota(jnp.int32, (tile, reach), 0)
    col = lax.broadcasted_iota(jnp.int32, (tile, reach), 1)

    def one_tile(idx, carry):
        first = pl.multiple_of(idx * tile, tile)
        position = chip * span - WINDOW + first + col
        seen = (col > row) & (col <= row + WINDOW) & (position >= 0)
        bias[...] = jnp.where(seen, 0.0, MASKED)
        for head in range(quer.shape[1] // ATT_DIM):
            cols = slice(head * ATT_DIM, (head + 1) * ATT_DIM)
            scores = nt_dot(quer[pl.ds(first, tile), cols], keys[pl.ds(first, reach), cols])
            scores = scores * scale + bias[...]
            top = jnp.max(scores, axis=-1, keepdims=True)
            probs = jnp.exp(scores - top)
            norm = jnp.sum(probs, axis=-1, keepdims=True)
            att = nn_dot(probs.astype(BF16), vals[pl.ds(first, reach), cols]) / norm
            att = att * lax.rsqrt(jnp.mean(att * att, axis=-1, keepdims=True) + EPS)
            out[pl.ds(first, tile), cols] = att
        return carry

    lax.fori_loop(0, span // tile, one_tile, 0)


def attention(where, blocks):
    tokens, width = blocks[0].shape
    span = 2 * tokens
    assert WINDOW == 2 * span
    return pl.pallas_call(
        att_kernel,
        out_shape=jax.ShapeDtypeStruct((span, width), F32),
        in_specs=[pl.BlockSpec(memory_space=pltpu.SMEM)] + [vmem()] * len(blocks),
        out_specs=vmem(),
        scratch_shapes=[
            pltpu.VMEM((span, width), BF16),
            pltpu.VMEM((3 * span, width), BF16),
            pltpu.VMEM((3 * span, width), BF16),
            pltpu.VMEM((128, WINDOW + 128), F32),
        ],
        cost_estimate=pl.CostEstimate(
            flops=4 * span * (WINDOW + 128) * width,
            bytes_accessed=40 * tokens * width,
            transcendentals=span * WINDOW * width // ATT_DIM,
        ),
        name="attention",
    )(where, *blocks)


def per_device(queries, key_rows, value_rows, step_rates, fast_weights, momentum, out_gain):
    count = lax.axis_size("seq")
    routes = Routes(count)
    local_tokens = queries.shape[0]
    heads, width = step_rates.shape[0], fast_weights.shape[2]
    owned = fast_weights.shape[1]
    assert heads == 2
    here = lax.axis_index("seq")
    core = here % 2
    chip = here // 2
    is_home = core == (2 * here) // count
    where = jnp.stack([core, chip % 2, chip]).astype(jnp.int32)

    start = gather_rows(fast_weights.astype(BF16), routes, is_home)

    grad_scale = 1.0 / math.sqrt(local_tokens * count)
    rates = jnp.repeat(step_rates.T, width, axis=1)
    out_grad = (-grad_scale * rates * value_rows.astype(F32)).astype(BF16)

    def by_core(array):
        kept = lax.dynamic_slice_in_dim(array, core * width, width, 1)
        sent = lax.dynamic_slice_in_dim(array, (1 - core) * width, width, 1)
        return (kept, send(sent, routes.partner))

    key_pair = by_core(key_rows)
    ograd_pair = by_core(out_grad)
    value_pair = by_core(value_rows)
    query_pair = by_core(queries)

    out_types = []
    for idx in range(len(start) // 4):
        out_types += [F32, F32, BF16, BF16]
    grads = key_side(key_pair, ograd_pair, start, out_types)

    own_blocks = key_pair + value_pair
    two_back = tuple(send(b, routes.next_two) for b in own_blocks)
    from_x = tuple(send(b, routes.next_x) for b in own_blocks)
    relayed = tuple(send(b, routes.back_x) for b in two_back)
    att = attention(where, query_pair + own_blocks + two_back + from_x + relayed)

    grad_rows = reduce_rows(grads, routes, is_home, owned)
    new_momentum = 0.9 * momentum + grad_rows
    moved_rows = fast_weights - new_momentum
    keep_norm = jnp.sqrt(jnp.mean(fast_weights * fast_weights, axis=-1, keepdims=True))
    new_weights = (
        moved_rows
        * keep_norm
        * lax.rsqrt(jnp.mean(moved_rows * moved_rows, axis=-1, keepdims=True) + EPS)
    )
    applied = gather_rows(new_weights.astype(BF16), routes, is_home)
    gain = lax.dynamic_slice_in_dim(out_gain, core * width, width, 0).reshape(1, width)
    own, other = query_side(where, query_pair, applied, gain, att)
    arrived = send(other, routes.partner)
    layer_out = jnp.where(
        core == 0,
        jnp.concatenate([own, arrived], axis=1),
        jnp.concatenate([arrived, own], axis=1),
    )
    return (layer_out, new_weights, new_momentum)


def solution(mesh):
    placed = (
        P(("groups", "seq"), None),
        P(("groups", "seq"), None),
        P(("groups", "seq"), None),
        P(None, ("groups", "seq")),
        P(None, "seq", None),
        P("groups", "seq", None),
        P(),
    )
    return jax.shard_map(
        per_device,
        mesh=mesh,
        in_specs=placed,
        out_specs=(P(("groups", "seq"), None), P("groups", "seq", None), P("groups", "seq", None)),
        check_vma=False,
    )
```

```python
import math

import jax
import jax.numpy as jnp
from jax import lax
from jax.experimental import pallas as pl
from jax.experimental.pallas import tpu as pltpu
from jax.sharding import PartitionSpec as P

ATT_DIM = 128
WINDOW = 1024
EPS = 1e-06
MASKED = -1e30
BF16 = jnp.bfloat16
F32 = jnp.float32


class Routes:
    def __init__(self, count):
        self.count = count
        half = count // 16
        self.bits = [1 << b for b in range(half.bit_length() - 1)]
        assert count % 16 == 0 and half == 1 << len(self.bits)
        home = [dev for dev in range(count) if self.is_home(dev)]
        away = [dev for dev in range(count) if not self.is_home(dev)]
        self.partner = [(dev, dev ^ 1) for dev in range(count)]
        self.x_swap = [(dev, dev ^ 2) for dev in range(count)]
        self.y_swap = [(dev, dev ^ 4) for dev in range(count)]
        self.pair_in = [(dev ^ 1, dev) for dev in home]
        self.pair_out = [(dev, dev ^ 1) for dev in home]
        shift = half * 8
        self.cross_out = [(dev, (dev + shift) % count) for dev in home]
        self.home_swap = [[(dev, dev ^ (8 * k)) for dev in home] for k in range(half)]
        self.away_swap = [[(dev, dev ^ (8 * k)) for dev in away] for k in range(half)]
        self.cross_back = [
            [(dev, ((dev ^ (8 * k)) + shift) % count) for dev in away] for k in range(half)
        ]
        self.next_two = [(dev, dev + 4) for dev in range(count - 4)]
        self.back_x = [(dev, dev - 2) for dev in range(count) if dev % 4 >= 2]

    def is_home(self, dev):
        return (dev % 2) == (2 * dev // self.count)


def send(array, route):
    return lax.ppermute(array, "seq", route)


def gather_z(unit, routes, is_home):
    home_list = [unit]
    away_list = [send(unit, routes.cross_out)]
    for bit in routes.bits:
        home_list = home_list + [send(part, routes.home_swap[bit]) for part in home_list]
        away_list = away_list + [send(part, routes.away_swap[bit]) for part in away_list]
    return [jnp.where(is_home, home, away) for home, away in zip(home_list, away_list)]


def gather_plane(units, routes):
    pieces = []
    for idx, own in enumerate(units):
        first, second = (
            (routes.x_swap, routes.y_swap) if idx % 2 == 0 else (routes.y_swap, routes.x_swap)
        )
        near = send(own, first)
        side = send(own, second)
        pieces += [own, near, side, send(near, second)]
    return pieces


def reduce_z(sums, routes):
    total = sums[0]
    for k, part in enumerate(sums):
        sent = part.astype(BF16)
        total = total + send(sent, routes.cross_back[k]).astype(F32)
        if k > 0:
            total = total + send(sent, routes.home_swap[k]).astype(F32)
    return total


def nt_dot(left, right):
    return lax.dot_general(left, right, (((1,), (1,)), ((), ())), preferred_element_type=F32)


def nn_dot(left, right):
    return lax.dot_general(left, right, (((1,), (0,)), ((), ())), preferred_element_type=F32)


def vmem():
    return pl.BlockSpec(memory_space=pltpu.VMEM)


def key_kernel(grad_scale, k_own, v_own, k_near, v_near, rates, units, out, keys, ograd, pair, down):
    tokens = k_own.shape[1]
    parts, _, step, _ = units.shape
    rows = parts * step
    for idx, (k_ref, v_ref) in enumerate(((k_own, v_own), (k_near, v_near))):
        for side in range(2):
            at = (2 * idx + side) * tokens
            keys[at : at + tokens, :] = k_ref[side]
            rate = rates[at : at + tokens, :] * (-grad_scale)
            ograd[at : at + tokens, :] = (rate * v_ref[side].astype(F32)).astype(BF16)
    for idx in range(parts):
        pair[idx * step : (idx + 1) * step, :] = units[idx, 0]
        pair[rows + idx * step : rows + (idx + 1) * step, :] = units[idx, 1]
        down[idx * step : (idx + 1) * step, :] = units[idx, 2]
    both = nt_dot(pair[...], keys[...])
    gate, up = both[:rows], both[rows:]
    hidden_grad = nt_dot(down[...], ograd[...])
    sig = jax.nn.sigmoid(gate)
    silu = gate * sig
    hidden = (silu * up).astype(BF16)
    gate_grad = (hidden_grad * up * (sig * (1.0 + gate * (1.0 - sig)))).astype(BF16)
    up_grad = (hidden_grad * silu).astype(BF16)
    first = nn_dot(jnp.concatenate([gate_grad, up_grad], axis=0), keys[...])
    second = nn_dot(hidden, ograd[...])
    for idx in range(parts):
        at = idx * step
        out[idx, 0] = first[at : at + step].astype(out.dtype)
        out[idx, 1] = first[rows + at : rows + at + step].astype(out.dtype)
        out[idx, 2] = second[at : at + step].astype(out.dtype)


def key_side(grad_scale, k_own, v_own, k_near, v_near, rates, units, kind, name):
    _, tokens, width = k_own.shape
    parts, _, step, _ = units.shape
    rows = parts * step
    return pl.pallas_call(
        lambda *refs: key_kernel(grad_scale, *refs),
        out_shape=jax.ShapeDtypeStruct(units.shape, kind),
        in_specs=[vmem()] * 6,
        out_specs=vmem(),
        scratch_shapes=[
            pltpu.VMEM((4 * tokens, width), BF16),
            pltpu.VMEM((4 * tokens, width), BF16),
            pltpu.VMEM((2 * rows, width), BF16),
            pltpu.VMEM((rows, width), BF16),
        ],
        cost_estimate=pl.CostEstimate(
            flops=12 * 4 * tokens * rows * width,
            bytes_accessed=16 * tokens * width,
            transcendentals=0,
        ),
        name=name,
    )(k_own, v_own, k_near, v_near, rates, units)


def query_kernel(count, *refs):
    where, quer_in = refs[:2]
    pieces = refs[2 : 2 + count]
    gain, att, own, other = refs[2 + count : 6 + count]
    quer, weights, result = refs[6 + count :]
    tokens = quer_in.shape[1]
    rows = pieces[0].shape[1]
    mine = pl.multiple_of(where[0] * tokens, tokens)
    theirs = pl.multiple_of((1 - where[0]) * tokens, tokens)
    quer[pl.ds(mine, tokens), :] = quer_in[0]
    quer[pl.ds(theirs, tokens), :] = quer_in[1]
    for idx in range(count):
        weights[:, idx * rows : (idx + 1) * rows, :] = pieces[idx][...]
    gate = nt_dot(quer[...], weights[0])
    up = nt_dot(quer[...], weights[1])
    hidden = (gate * jax.nn.sigmoid(gate) * up).astype(BF16)
    out = nn_dot(hidden, weights[2])
    scale = lax.rsqrt(jnp.mean(out * out, axis=-1, keepdims=True) + EPS)
    result[...] = out * scale * gain[...] + att[...]
    own[...] = result[pl.ds(mine, tokens), :].astype(BF16)
    other[...] = result[pl.ds(theirs, tokens), :].astype(BF16)


def query_side(where, quer_in, pieces, gain, att):
    _, tokens, width = quer_in.shape
    count = len(pieces)
    rows = pieces[0].shape[1]
    total = 2 * tokens * count * rows * width
    return pl.pallas_call(
        lambda *refs: query_kernel(count, *refs),
        out_shape=[jax.ShapeDtypeStruct((tokens, width), BF16)] * 2,
        in_specs=[pl.BlockSpec(memory_space=pltpu.SMEM)] + [vmem()] * (3 + count),
        out_specs=[vmem()] * 2,
        scratch_shapes=[
            pltpu.VMEM((2 * tokens, width), BF16),
            pltpu.VMEM((3, count * rows, width), BF16),
            pltpu.VMEM((2 * tokens, width), F32),
        ],
        cost_estimate=pl.CostEstimate(
            flops=6 * total, bytes_accessed=6 * count * rows * width, transcendentals=0
        ),
        name="query_side",
    )(where, quer_in, *pieces, gain, att)


def att_kernel(where, quer_in, k_own, v_own, k_two, v_two, k_near, v_near, k_back, v_back, out,
               quer, keys, vals, bias):
    tokens = quer_in.shape[1]
    span = 2 * tokens
    tile = 128
    reach = WINDOW + tile
    core, odd, chip = where[0], where[1], where[2]
    mine = core * tokens
    theirs = (1 - core) * tokens

    def put(dest, base, pair):
        dest[pl.ds(pl.multiple_of(base + mine, tokens), tokens), :] = pair[0]
        dest[pl.ds(pl.multiple_of(base + theirs, tokens), tokens), :] = pair[1]

    put(quer, 0, quer_in)
    for dest, own, two, near, back in (
        (keys, k_own, k_two, k_near, k_back),
        (vals, v_own, v_two, v_near, v_back),
    ):
        put(dest, 2 * span, own)
        put(dest, 0, two)

        @pl.when(odd == 1)
        def _():
            put(dest, span, near)

        @pl.when(odd == 0)
        def _():
            put(dest, span, back)

    scale = 1.0 / math.sqrt(ATT_DIM)
    row = lax.broadcasted_iota(jnp.int32, (tile, reach), 0)
    col = lax.broadcasted_iota(jnp.int32, (tile, reach), 1)

    def one_tile(idx, carry):
        first = pl.multiple_of(idx * tile, tile)
        position = chip * span - WINDOW + first + col
        seen = (col > row) & (col <= row + WINDOW) & (position >= 0)
        bias[...] = jnp.where(seen, 0.0, MASKED)
        for head in range(quer.shape[1] // ATT_DIM):
            cols = slice(head * ATT_DIM, (head + 1) * ATT_DIM)
            scores = nt_dot(quer[pl.ds(first, tile), cols], keys[pl.ds(first, reach), cols])
            scores = scores * scale + bias[...]
            top = jnp.max(scores, axis=-1, keepdims=True)
            probs = jnp.exp(scores - top)
            norm = jnp.sum(probs, axis=-1, keepdims=True)
            att = nn_dot(probs.astype(BF16), vals[pl.ds(first, reach), cols]) / norm
            att = att * lax.rsqrt(jnp.mean(att * att, axis=-1, keepdims=True) + EPS)
            out[pl.ds(first, tile), cols] = att
        return carry

    lax.fori_loop(0, span // tile, one_tile, 0)


def attention(where, *blocks):
    _, tokens, width = blocks[0].shape
    span = 2 * tokens
    assert WINDOW == 2 * span
    return pl.pallas_call(
        att_kernel,
        out_shape=jax.ShapeDtypeStruct((span, width), F32),
        in_specs=[pl.BlockSpec(memory_space=pltpu.SMEM)] + [vmem()] * len(blocks),
        out_specs=vmem(),
        scratch_shapes=[
            pltpu.VMEM((span, width), BF16),
            pltpu.VMEM((3 * span, width), BF16),
            pltpu.VMEM((3 * span, width), BF16),
            pltpu.VMEM((128, WINDOW + 128), F32),
        ],
        cost_estimate=pl.CostEstimate(
            flops=4 * span * (WINDOW + 128) * width,
            bytes_accessed=40 * tokens * width,
            transcendentals=span * WINDOW * width // ATT_DIM,
        ),
        name="attention",
    )(where, *blocks)


def updated(weights, momentum, grads):
    new_momentum = 0.9 * momentum + grads
    moved = weights - new_momentum
    keep_norm = jnp.sqrt(jnp.mean(weights * weights, axis=-1, keepdims=True))
    new_weights = (
        moved * keep_norm * lax.rsqrt(jnp.mean(moved * moved, axis=-1, keepdims=True) + EPS)
    )
    return new_weights, new_momentum


def per_device(queries, key_rows, value_rows, step_rates, fast_weights, momentum, out_gain):
    count = lax.axis_size("seq")
    routes = Routes(count)
    local_tokens = queries.shape[0]
    heads, width = step_rates.shape[0], fast_weights.shape[2]
    owned = fast_weights.shape[1]
    assert heads == 2
    here = lax.axis_index("seq")
    core = here % 2
    chip = here // 2
    is_home = core == (2 * here) // count
    where = jnp.stack([core, chip % 2, chip]).astype(jnp.int32)

    pair_weights = jnp.concatenate([fast_weights, send(fast_weights, routes.pair_in)], axis=1)
    pair_momentum = jnp.concatenate([momentum, send(momentum, routes.pair_in)], axis=1)

    def by_core(array):
        kept = lax.dynamic_slice_in_dim(array, core * width, width, 1)
        sent = lax.dynamic_slice_in_dim(array, (1 - core) * width, width, 1)
        return jnp.stack([kept, send(sent, routes.partner)])

    k_own = by_core(key_rows)
    v_own = by_core(value_rows)
    q_own = by_core(queries)
    my_rate = lax.dynamic_slice_in_dim(step_rates, core, 1, 0)
    their_rate = lax.dynamic_slice_in_dim(step_rates, 1 - core, 1, 0)
    rates = jnp.concatenate([my_rate, send(their_rate, routes.partner)], axis=0)
    rates = jnp.concatenate([rates, send(rates, routes.x_swap)], axis=0)
    rates = rates.reshape(4 * local_tokens, 1)

    k_near = send(k_own, routes.x_swap)
    v_near = send(v_own, routes.x_swap)
    units = gather_z(pair_weights.astype(BF16), routes, is_home)
    own_units = jnp.stack(units)
    side_units = send(own_units, routes.y_swap)
    grad_scale = 1.0 / math.sqrt(local_tokens * count)
    tokens_in = (k_own, v_own, k_near, v_near, rates)
    side_grads = key_side(grad_scale, *tokens_in, side_units, BF16, "key_sent")
    side_in = send(side_grads, routes.y_swap)
    own_grads = key_side(grad_scale, *tokens_in, own_units, F32, "key_kept")
    sums = own_grads + side_in.astype(F32)
    total = reduce_z([sums[k] for k in range(len(units))], routes)

    k_two = send(k_own, routes.next_two)
    v_two = send(v_own, routes.next_two)
    k_back = send(k_two, routes.back_x)
    v_back = send(v_two, routes.back_x)
    att = attention(where, q_own, k_own, v_own, k_two, v_two, k_near, v_near, k_back, v_back)

    pair_new, _ = updated(pair_weights, pair_momentum, total)
    applied = gather_plane(gather_z(pair_new.astype(BF16), routes, is_home), routes)
    partner_grads = send(total[:, owned:], routes.pair_out)
    grads = jnp.where(is_home, total[:, :owned], partner_grads)
    new_weights, new_momentum = updated(fast_weights, momentum, grads)
    gain = lax.dynamic_slice_in_dim(out_gain, core * width, width, 0).reshape(1, width)
    own, other = query_side(where, q_own, applied, gain, att)
    arrived = send(other, routes.partner)
    layer_out = jnp.where(
        core == 0,
        jnp.concatenate([own, arrived], axis=1),
        jnp.concatenate([arrived, own], axis=1),
    )
    return (layer_out, new_weights, new_momentum)


def solution(mesh):
    placed = (
        P(("groups", "seq"), None),
        P(("groups", "seq"), None),
        P(("groups", "seq"), None),
        P(None, ("groups", "seq")),
        P(None, "seq", None),
        P("groups", "seq", None),
        P(),
    )
    return jax.shard_map(
        per_device,
        mesh=mesh,
        in_specs=placed,
        out_specs=(P(("groups", "seq"), None), P("groups", "seq", None), P("groups", "seq", None)),
        check_vma=False,
    )
```

```python
import math

import jax
import jax.numpy as jnp
from jax import lax
from jax.experimental import pallas as pl
from jax.experimental.pallas import tpu as pltpu
from jax.sharding import PartitionSpec as P


ATT_DIM = 128
WINDOW = 1024
EPS = 1e-06
MASKED = -1e30
BF16 = jnp.bfloat16
F32 = jnp.float32


class Routes:
    def __init__(self, count):
        self.count = count
        half = count // 16
        self.bits = [1 << b for b in range(half.bit_length() - 1)]
        assert count % 16 == 0 and half == 1 << len(self.bits)
        home = [dev for dev in range(count) if self.is_home(dev)]
        away = [dev for dev in range(count) if not self.is_home(dev)]
        self.partner = [(dev, dev ^ 1) for dev in range(count)]
        self.x_swap = [(dev, dev ^ 2) for dev in range(count)]
        self.y_swap = [(dev, dev ^ 4) for dev in range(count)]
        self.pair_in = [(dev ^ 1, dev) for dev in home]
        self.pair_out = [(dev, dev ^ 1) for dev in home]
        shift = half * 8
        self.cross_out = [(dev, (dev + shift) % count) for dev in home]
        self.home_swap = [[(dev, dev ^ (8 * k)) for dev in home] for k in range(half)]
        self.away_swap = [[(dev, dev ^ (8 * k)) for dev in away] for k in range(half)]
        self.cross_back = [
            [(dev, ((dev ^ (8 * k)) + shift) % count) for dev in away] for k in range(half)
        ]
        self.z_up = [(dev, dev + 8) for dev in range(count - 8) if dev % 8 >= 4]
        self.back_x = [(dev, dev - 2) for dev in range(count) if dev % 4 >= 2]

    def is_home(self, dev):
        return (dev % 2) == (2 * dev // self.count)


def send(array, route):
    return lax.ppermute(array, "seq", route)


def gather_z(unit, routes, is_home):
    home_list = [unit]
    away_list = [send(unit, routes.cross_out)]
    for bit in routes.bits:
        home_list = home_list + [send(part, routes.home_swap[bit]) for part in home_list]
        away_list = away_list + [send(part, routes.away_swap[bit]) for part in away_list]
    return [jnp.where(is_home, home, away) for home, away in zip(home_list, away_list)]


def gather_plane(units, routes):
    pieces = []
    for idx, own in enumerate(units):
        first, second = (
            (routes.x_swap, routes.y_swap) if idx % 2 == 0 else (routes.y_swap, routes.x_swap)
        )
        near = send(own, first)
        side = send(own, second)
        pieces += [own, near, side, send(near, second)]
    return pieces


def reduce_z(sums, routes):
    total = sums[0]
    for k, part in enumerate(sums):
        sent = part.astype(BF16)
        total = total + send(sent, routes.cross_back[k]).astype(F32)
        if k > 0:
            total = total + send(sent, routes.home_swap[k]).astype(F32)
    return total


def nt_dot(left, right):
    return lax.dot_general(left, right, (((1,), (1,)), ((), ())), preferred_element_type=F32)


def nn_dot(left, right):
    return lax.dot_general(left, right, (((1,), (0,)), ((), ())), preferred_element_type=F32)


def vmem():
    return pl.BlockSpec(memory_space=pltpu.VMEM)


def key_kernel(grad_scale, k_own, v_own, k_near, v_near, rates, units, out, keys, ograd, pair, down):
    tokens = k_own.shape[1]
    parts, _, step, _ = units.shape
    rows = parts * step
    for idx, (k_ref, v_ref) in enumerate(((k_own, v_own), (k_near, v_near))):
        for side in range(2):
            at = (2 * idx + side) * tokens
            keys[at : at + tokens, :] = k_ref[side]
            rate = rates[at : at + tokens, :] * (-grad_scale)
            ograd[at : at + tokens, :] = (rate * v_ref[side].astype(F32)).astype(BF16)
    for idx in range(parts):
        pair[idx * step : (idx + 1) * step, :] = units[idx, 0]
        pair[rows + idx * step : rows + (idx + 1) * step, :] = units[idx, 1]
        down[idx * step : (idx + 1) * step, :] = units[idx, 2]
    both = nt_dot(pair[...], keys[...])
    gate, up = both[:rows], both[rows:]
    hidden_grad = nt_dot(down[...], ograd[...])
    sig = jax.nn.sigmoid(gate)
    silu = gate * sig
    hidden = (silu * up).astype(BF16)
    gate_grad = (hidden_grad * up * (sig * (1.0 + gate * (1.0 - sig)))).astype(BF16)
    up_grad = (hidden_grad * silu).astype(BF16)
    first = nn_dot(jnp.concatenate([gate_grad, up_grad], axis=0), keys[...])
    second = nn_dot(hidden, ograd[...])
    for idx in range(parts):
        at = idx * step
        out[idx, 0] = first[at : at + step].astype(out.dtype)
        out[idx, 1] = first[rows + at : rows + at + step].astype(out.dtype)
        out[idx, 2] = second[at : at + step].astype(out.dtype)


def key_side(grad_scale, k_own, v_own, k_near, v_near, rates, units, kind):
    _, tokens, width = k_own.shape
    parts, _, step, _ = units.shape
    rows = parts * step
    return pl.pallas_call(
        lambda *refs: key_kernel(grad_scale, *refs),
        out_shape=jax.ShapeDtypeStruct(units.shape, kind),
        in_specs=[vmem()] * 6,
        out_specs=vmem(),
        scratch_shapes=[
            pltpu.VMEM((4 * tokens, width), BF16),
            pltpu.VMEM((4 * tokens, width), BF16),
            pltpu.VMEM((2 * rows, width), BF16),
            pltpu.VMEM((rows, width), BF16),
        ],
        cost_estimate=pl.CostEstimate(
            flops=12 * 4 * tokens * rows * width,
            bytes_accessed=16 * tokens * width,
            transcendentals=0,
        ),
    )(k_own, v_own, k_near, v_near, rates, units)


def query_kernel(count, *refs):
    where, quer_in = refs[:2]
    pieces = refs[2 : 2 + count]
    gain, att, own, other = refs[2 + count : 6 + count]
    quer, weights, result = refs[6 + count :]
    tokens = quer_in.shape[1]
    rows = pieces[0].shape[1]
    mine = pl.multiple_of(where[0] * tokens, tokens)
    theirs = pl.multiple_of((1 - where[0]) * tokens, tokens)
    quer[pl.ds(mine, tokens), :] = quer_in[0]
    quer[pl.ds(theirs, tokens), :] = quer_in[1]
    for idx in range(count):
        weights[:, idx * rows : (idx + 1) * rows, :] = pieces[idx][...]
    gate = nt_dot(quer[...], weights[0])
    up = nt_dot(quer[...], weights[1])
    hidden = (gate * jax.nn.sigmoid(gate) * up).astype(BF16)
    out = nn_dot(hidden, weights[2])
    scale = lax.rsqrt(jnp.mean(out * out, axis=-1, keepdims=True) + EPS)
    result[...] = out * scale * gain[...] + att[...]
    own[...] = result[pl.ds(mine, tokens), :].astype(BF16)
    other[...] = result[pl.ds(theirs, tokens), :].astype(BF16)


def query_side(where, quer_in, pieces, gain, att):
    _, tokens, width = quer_in.shape
    count = len(pieces)
    rows = pieces[0].shape[1]
    total = 2 * tokens * count * rows * width
    return pl.pallas_call(
        lambda *refs: query_kernel(count, *refs),
        out_shape=[jax.ShapeDtypeStruct((tokens, width), BF16)] * 2,
        in_specs=[pl.BlockSpec(memory_space=pltpu.SMEM)] + [vmem()] * (3 + count),
        out_specs=[vmem()] * 2,
        scratch_shapes=[
            pltpu.VMEM((2 * tokens, width), BF16),
            pltpu.VMEM((3, count * rows, width), BF16),
            pltpu.VMEM((2 * tokens, width), F32),
        ],
        cost_estimate=pl.CostEstimate(
            flops=6 * total, bytes_accessed=6 * count * rows * width, transcendentals=0
        ),
        name="query_side",
    )(where, quer_in, *pieces, gain, att)


def att_kernel(where, quer_in, k_own, v_own, k_two, v_two, k_near, v_near, k_back, v_back, out,
               quer, keys, vals, bias):
    tokens = quer_in.shape[1]
    span = 2 * tokens
    tile = 128
    reach = WINDOW + tile
    core, odd, chip = where[0], where[1], where[2]
    mine = core * tokens
    theirs = (1 - core) * tokens

    def put(dest, base, pair):
        dest[pl.ds(pl.multiple_of(base + mine, tokens), tokens), :] = pair[0]
        dest[pl.ds(pl.multiple_of(base + theirs, tokens), tokens), :] = pair[1]

    put(quer, 0, quer_in)
    for dest, own, two, near, back in (
        (keys, k_own, k_two, k_near, k_back),
        (vals, v_own, v_two, v_near, v_back),
    ):
        put(dest, 2 * span, own)
        put(dest, 0, two)

        @pl.when(odd == 1)
        def _():
            put(dest, span, near)

        @pl.when(odd == 0)
        def _():
            put(dest, span, back)

    scale = 1.0 / math.sqrt(ATT_DIM)
    row = lax.broadcasted_iota(jnp.int32, (tile, reach), 0)
    col = lax.broadcasted_iota(jnp.int32, (tile, reach), 1)

    def one_tile(idx, carry):
        first = pl.multiple_of(idx * tile, tile)
        position = chip * span - WINDOW + first + col
        seen = (col > row) & (col <= row + WINDOW) & (position >= 0)
        bias[...] = jnp.where(seen, 0.0, MASKED)
        for head in range(quer.shape[1] // ATT_DIM):
            cols = slice(head * ATT_DIM, (head + 1) * ATT_DIM)
            scores = nt_dot(quer[pl.ds(first, tile), cols], keys[pl.ds(first, reach), cols])
            scores = scores * scale + bias[...]
            top = jnp.max(scores, axis=-1, keepdims=True)
            probs = jnp.exp(scores - top)
            norm = jnp.sum(probs, axis=-1, keepdims=True)
            att = nn_dot(probs.astype(BF16), vals[pl.ds(first, reach), cols]) / norm
            att = att * lax.rsqrt(jnp.mean(att * att, axis=-1, keepdims=True) + EPS)
            out[pl.ds(first, tile), cols] = att
        return carry

    lax.fori_loop(0, span // tile, one_tile, 0)


def attention(where, *blocks):
    _, tokens, width = blocks[0].shape
    span = 2 * tokens
    assert WINDOW == 2 * span
    return pl.pallas_call(
        att_kernel,
        out_shape=jax.ShapeDtypeStruct((span, width), F32),
        in_specs=[pl.BlockSpec(memory_space=pltpu.SMEM)] + [vmem()] * len(blocks),
        out_specs=vmem(),
        scratch_shapes=[
            pltpu.VMEM((span, width), BF16),
            pltpu.VMEM((3 * span, width), BF16),
            pltpu.VMEM((3 * span, width), BF16),
            pltpu.VMEM((128, WINDOW + 128), F32),
        ],
        cost_estimate=pl.CostEstimate(
            flops=4 * span * (WINDOW + 128) * width,
            bytes_accessed=40 * tokens * width,
            transcendentals=span * WINDOW * width // ATT_DIM,
        ),
        name="attention",
    )(where, *blocks)


def updated(weights, momentum, grads):
    new_momentum = 0.9 * momentum + grads
    moved = weights - new_momentum
    keep_norm = jnp.sqrt(jnp.mean(weights * weights, axis=-1, keepdims=True))
    new_weights = (
        moved * keep_norm * lax.rsqrt(jnp.mean(moved * moved, axis=-1, keepdims=True) + EPS)
    )
    return new_weights, new_momentum


def layer(queries, key_rows, value_rows, step_rates, fast_weights, momentum, out_gain):
    count = lax.axis_size("seq")
    routes = Routes(count)
    local_tokens = queries.shape[0]
    heads, width = step_rates.shape[0], fast_weights.shape[2]
    owned = fast_weights.shape[1]
    assert heads == 2
    here = lax.axis_index("seq")
    core = here % 2
    chip = here // 2
    is_home = core == (2 * here) // count
    where = jnp.stack([core, chip % 2, chip]).astype(jnp.int32)

    my_rate = lax.dynamic_slice_in_dim(step_rates, core, 1, 0)
    their_rate = lax.dynamic_slice_in_dim(step_rates, 1 - core, 1, 0)
    rates = jnp.concatenate([my_rate, send(their_rate, routes.partner)], axis=0)
    rates = jnp.concatenate([rates, send(rates, routes.x_swap)], axis=0)
    rates = rates.reshape(4 * local_tokens, 1)

    def by_core(array):
        kept = lax.dynamic_slice_in_dim(array, core * width, width, 1)
        sent = lax.dynamic_slice_in_dim(array, (1 - core) * width, width, 1)
        return jnp.stack([kept, send(sent, routes.partner)])

    k_own = by_core(key_rows)
    v_own = by_core(value_rows)
    k_own, v_own, rates = lax.optimization_barrier((k_own, v_own, rates))
    q_own = by_core(queries)

    pair_weights = jnp.concatenate([fast_weights, send(fast_weights, routes.pair_in)], axis=1)

    k_near = send(k_own, routes.x_swap)
    v_near = send(v_own, routes.x_swap)
    unit = pair_weights.astype(BF16)
    units = gather_z(unit, routes, is_home)
    own_units = jnp.stack(units)
    side_units = send(own_units, routes.y_swap)
    k_late, v_late, _ = lax.optimization_barrier((k_own, v_own, own_units))
    k_up = send(k_late, routes.z_up)
    v_up = send(v_late, routes.z_up)
    grad_scale = 1.0 / math.sqrt(local_tokens * count)
    tokens_in = (k_own, v_own, k_near, v_near, rates)
    side_grads = key_side(grad_scale, *tokens_in, side_units, BF16)
    side_in = send(side_grads, routes.y_swap)
    own_grads = key_side(grad_scale, *tokens_in, own_units, F32)
    sums = own_grads + side_in.astype(F32)
    sums, k_up, v_up = lax.optimization_barrier((sums, k_up, v_up))
    total = reduce_z([sums[k] for k in range(len(units))], routes)
    pair_momentum = jnp.concatenate([momentum, send(momentum, routes.pair_in)], axis=1)

    upper = chip // 2 % 2 == 1
    k_two = send(jnp.where(upper, k_up, k_own), routes.y_swap)
    v_two = send(jnp.where(upper, v_up, v_own), routes.y_swap)
    k_back = send(k_two, routes.back_x)
    v_back = send(v_two, routes.back_x)
    att = attention(where, q_own, k_own, v_own, k_two, v_two, k_near, v_near, k_back, v_back)

    pair_new, _ = updated(pair_weights, pair_momentum, total)
    applied = gather_plane(gather_z(pair_new.astype(BF16), routes, is_home), routes)
    partner_grads = send(total[:, owned:], routes.pair_out)
    grads = jnp.where(is_home, total[:, :owned], partner_grads)
    new_weights, new_momentum = updated(fast_weights, momentum, grads)
    gain = lax.dynamic_slice_in_dim(out_gain, core * width, width, 0).reshape(1, width)
    own, other = query_side(where, q_own, applied, gain, att)
    arrived = send(other, routes.partner)
    layer_out = jnp.where(
        core == 0,
        jnp.concatenate([own, arrived], axis=1),
        jnp.concatenate([arrived, own], axis=1),
    )
    return (layer_out, new_weights, new_momentum)


def solution(mesh):
    placed = (
        P(("groups", "seq"), None),
        P(("groups", "seq"), None),
        P(("groups", "seq"), None),
        P(None, ("groups", "seq")),
        P(None, "seq", None),
        P("groups", "seq", None),
        P(),
    )
    return jax.shard_map(
        layer,
        mesh=mesh,
        in_specs=placed,
        out_specs=(P(("groups", "seq"), None), P("groups", "seq", None), P("groups", "seq", None)),
        check_vma=False,
    )
```

```python
import math

import jax
import jax.numpy as jnp
from jax import lax
from jax.experimental import pallas as pl
from jax.experimental.pallas import tpu as pltpu
from jax.sharding import PartitionSpec as P


ATT_DIM = 128
WINDOW = 1024
EPS = 1e-06
MASKED = -1e30
BF16 = jnp.bfloat16
F32 = jnp.float32


class Routes:
    def __init__(self, count):
        self.count = count
        half = count // 16
        self.bits = [1 << b for b in range(half.bit_length() - 1)]
        assert count % 16 == 0 and half == 1 << len(self.bits)
        home = [dev for dev in range(count) if self.is_home(dev)]
        away = [dev for dev in range(count) if not self.is_home(dev)]
        self.partner = [(dev, dev ^ 1) for dev in range(count)]
        self.x_swap = [(dev, dev ^ 2) for dev in range(count)]
        self.y_swap = [(dev, dev ^ 4) for dev in range(count)]
        self.pair_in = [(dev ^ 1, dev) for dev in home]
        self.pair_out = [(dev, dev ^ 1) for dev in home]
        shift = half * 8
        self.cross_out = [(dev, (dev + shift) % count) for dev in home]
        self.home_swap = [[(dev, dev ^ (8 * k)) for dev in home] for k in range(half)]
        self.away_swap = [[(dev, dev ^ (8 * k)) for dev in away] for k in range(half)]
        self.cross_back = [(dev, (dev + shift) % count) for dev in away]
        self.z_up = [(dev, dev + 8) for dev in range(count - 8) if dev % 8 < 4]
        self.back_x = [(dev, dev - 2) for dev in range(count) if dev % 4 >= 2]

    def is_home(self, dev):
        return (dev % 2) == (2 * dev // self.count)


def send(array, route):
    return lax.ppermute(array, "seq", route)


def gather_z(unit, routes, is_home):
    home_list = [unit]
    away_list = [send(unit, routes.cross_out)]
    for bit in routes.bits:
        home_list = home_list + [send(part, routes.home_swap[bit]) for part in home_list]
        away_list = away_list + [send(part, routes.away_swap[bit]) for part in away_list]
    return [jnp.where(is_home, home, away) for home, away in zip(home_list, away_list)]


def gather_plane(units, routes):
    pieces = []
    for idx, own in enumerate(units):
        first, second = (
            (routes.x_swap, routes.y_swap) if idx % 2 == 0 else (routes.y_swap, routes.x_swap)
        )
        near = send(own, first)
        side = send(own, second)
        pieces += [own, near, side, send(near, second)]
    return pieces


def reduce_z(sums, routes):
    away, home = sums, sums
    for bit in reversed(routes.bits):
        half = len(away) // 2
        sent = [part.astype(BF16) for part in away[half:]]
        arrived = [send(part, routes.away_swap[bit]) for part in sent]
        away = [low + part.astype(F32) for low, part in zip(away[:half], arrived)]
    crossed = away[0].astype(BF16)
    home, crossed = lax.optimization_barrier((home, crossed))
    crossed = send(crossed, routes.cross_back)
    for bit in reversed(routes.bits):
        half = len(home) // 2
        arrived = [send(part.astype(BF16), routes.home_swap[bit]) for part in home[half:]]
        home = [low + part.astype(F32) for low, part in zip(home[:half], arrived)]
    return home[0] + crossed.astype(F32)


def nt_dot(left, right):
    return lax.dot_general(left, right, (((1,), (1,)), ((), ())), preferred_element_type=F32)


def nn_dot(left, right):
    return lax.dot_general(left, right, (((1,), (0,)), ((), ())), preferred_element_type=F32)


def vmem():
    return pl.BlockSpec(memory_space=pltpu.VMEM)


def key_kernel(grad_scale, *refs):
    k_own, v_own, k_near, v_near, rates = refs[:5]
    units = refs[5:-5]
    out, keys, ograd, pair, down = refs[-5:]
    tokens = k_own.shape[1]
    parts = len(units)
    step = units[0].shape[1]
    rows = parts * step
    for idx, (k_ref, v_ref) in enumerate(((k_own, v_own), (k_near, v_near))):
        for side in range(2):
            at = (2 * idx + side) * tokens
            keys[at : at + tokens, :] = k_ref[side]
            rate = rates[at : at + tokens, :] * (-grad_scale)
            ograd[at : at + tokens, :] = (rate * v_ref[side].astype(F32)).astype(BF16)
    for idx in range(parts):
        pair[idx * step : (idx + 1) * step, :] = units[idx][0]
        pair[rows + idx * step : rows + (idx + 1) * step, :] = units[idx][1]
        down[idx * step : (idx + 1) * step, :] = units[idx][2]
    both = nt_dot(pair[...], keys[...])
    gate, up = both[:rows], both[rows:]
    hidden_grad = nt_dot(down[...], ograd[...])
    sig = jax.nn.sigmoid(gate)
    silu = gate * sig
    hidden = (silu * up).astype(BF16)
    gate_grad = (hidden_grad * up * (sig * (1.0 + gate * (1.0 - sig)))).astype(BF16)
    up_grad = (hidden_grad * silu).astype(BF16)
    first = nn_dot(jnp.concatenate([gate_grad, up_grad], axis=0), keys[...])
    second = nn_dot(hidden, ograd[...])
    for idx in range(parts):
        at = idx * step
        out[idx, 0] = first[at : at + step].astype(out.dtype)
        out[idx, 1] = first[rows + at : rows + at + step].astype(out.dtype)
        out[idx, 2] = second[at : at + step].astype(out.dtype)


def key_side(grad_scale, k_own, v_own, k_near, v_near, rates, units, kind):
    _, tokens, width = k_own.shape
    parts = len(units)
    step = units[0].shape[1]
    rows = parts * step
    return pl.pallas_call(
        lambda *refs: key_kernel(grad_scale, *refs),
        out_shape=jax.ShapeDtypeStruct((parts, 3, step, width), kind),
        in_specs=[vmem()] * (5 + parts),
        out_specs=vmem(),
        scratch_shapes=[
            pltpu.VMEM((4 * tokens, width), BF16),
            pltpu.VMEM((4 * tokens, width), BF16),
            pltpu.VMEM((2 * rows, width), BF16),
            pltpu.VMEM((rows, width), BF16),
        ],
        cost_estimate=pl.CostEstimate(
            flops=12 * 4 * tokens * rows * width,
            bytes_accessed=16 * tokens * width,
            transcendentals=0,
        ),
    )(k_own, v_own, k_near, v_near, rates, *units)


def query_kernel(count, *refs):
    where, quer_in = refs[:2]
    pieces = refs[2 : 2 + count]
    gain, att_a, att_b, own, other = refs[2 + count : 7 + count]
    quer, weights, result = refs[7 + count :]
    tokens = quer_in.shape[1]
    rows = pieces[0].shape[1]
    mine = pl.multiple_of(where[0] * tokens, tokens)
    theirs = pl.multiple_of((1 - where[0]) * tokens, tokens)
    quer[pl.ds(mine, tokens), :] = quer_in[0]
    quer[pl.ds(theirs, tokens), :] = quer_in[1]
    for idx in range(count):
        weights[:, idx * rows : (idx + 1) * rows, :] = pieces[idx][...]
    gate = nt_dot(quer[...], weights[0])
    up = nt_dot(quer[...], weights[1])
    hidden = (gate * jax.nn.sigmoid(gate) * up).astype(BF16)
    out = nn_dot(hidden, weights[2])
    scale = lax.rsqrt(jnp.mean(out * out, axis=-1, keepdims=True) + EPS)
    normed = out * scale * gain[...]
    split = att_a.shape[1]
    result[:, :split] = normed[:, :split] + att_a[...]
    result[:, split:] = normed[:, split:] + att_b[...]
    own[...] = result[pl.ds(mine, tokens), :].astype(BF16)
    other[...] = result[pl.ds(theirs, tokens), :].astype(BF16)


def query_side(where, quer_in, pieces, gain, atts):
    _, tokens, width = quer_in.shape
    count = len(pieces)
    rows = pieces[0].shape[1]
    total = 2 * tokens * count * rows * width
    return pl.pallas_call(
        lambda *refs: query_kernel(count, *refs),
        out_shape=[jax.ShapeDtypeStruct((tokens, width), BF16)] * 2,
        in_specs=[pl.BlockSpec(memory_space=pltpu.SMEM)] + [vmem()] * (4 + count),
        out_specs=[vmem()] * 2,
        scratch_shapes=[
            pltpu.VMEM((2 * tokens, width), BF16),
            pltpu.VMEM((3, count * rows, width), BF16),
            pltpu.VMEM((2 * tokens, width), F32),
        ],
        cost_estimate=pl.CostEstimate(
            flops=6 * total, bytes_accessed=6 * count * rows * width, transcendentals=0
        ),
        name="query_side",
    )(where, quer_in, *pieces, gain, *atts)


def att_kernel(low, where, quer_in, k_own, v_own, k_near, v_near, two, back, out,
               quer, keys, vals, bias):
    tokens = quer_in.shape[1]
    span = 2 * tokens
    reach = WINDOW + span
    wide = out.shape[1]
    cols = slice(low, low + wide)
    core, odd, chip = where[0], where[1], where[2]
    mine = core * tokens
    theirs = (1 - core) * tokens

    def put(dest, base, first, second):
        dest[pl.ds(pl.multiple_of(base + mine, tokens), tokens), :] = first
        dest[pl.ds(pl.multiple_of(base + theirs, tokens), tokens), :] = second

    put(quer, 0, quer_in[0, :, cols], quer_in[1, :, cols])
    for idx, (dest, own, near) in enumerate(((keys, k_own, k_near), (vals, v_own, v_near))):
        put(dest, 2 * span, own[0, :, cols], own[1, :, cols])
        put(dest, 0, two[2 * idx], two[2 * idx + 1])

        @pl.when(odd == 1)
        def _():
            put(dest, span, near[0, :, cols], near[1, :, cols])

        @pl.when(odd == 0)
        def _():
            put(dest, span, back[2 * idx], back[2 * idx + 1])

    scale = 1.0 / math.sqrt(ATT_DIM)
    row = lax.broadcasted_iota(jnp.int32, (span, reach), 0)
    col = lax.broadcasted_iota(jnp.int32, (span, reach), 1)
    seen = (col > row) & (col <= row + WINDOW) & (chip * span - WINDOW + col >= 0)
    bias[...] = jnp.where(seen, 0.0, MASKED)
    for head in range(wide // ATT_DIM):
        at = slice(head * ATT_DIM, (head + 1) * ATT_DIM)
        scores = nt_dot(quer[:, at], keys[:, at]) + bias[...]
        top = jnp.max(scores, axis=-1, keepdims=True)
        probs = jnp.exp((scores - top) * scale)
        norm = jnp.sum(probs, axis=-1, keepdims=True)
        att = nn_dot(probs.astype(BF16), vals[:, at]) / norm
        out[:, at] = att * lax.rsqrt(jnp.mean(att * att, axis=-1, keepdims=True) + EPS)


def attention(where, quer_in, k_own, v_own, k_near, v_near, two, back, low):
    _, tokens, _ = quer_in.shape
    wide = two.shape[2]
    span = 2 * tokens
    reach = WINDOW + span
    assert WINDOW == 2 * span
    return pl.pallas_call(
        lambda *refs: att_kernel(low, *refs),
        out_shape=jax.ShapeDtypeStruct((span, wide), F32),
        in_specs=[pl.BlockSpec(memory_space=pltpu.SMEM)] + [vmem()] * 7,
        out_specs=vmem(),
        scratch_shapes=[
            pltpu.VMEM((span, wide), BF16),
            pltpu.VMEM((reach, wide), BF16),
            pltpu.VMEM((reach, wide), BF16),
            pltpu.VMEM((span, reach), F32),
        ],
        cost_estimate=pl.CostEstimate(
            flops=4 * span * reach * wide,
            bytes_accessed=40 * tokens * wide,
            transcendentals=span * reach * wide // ATT_DIM,
        ),
    )(where, quer_in, k_own, v_own, k_near, v_near, two, back)


def join_kernel(where, own, arrived, out):
    width = own.shape[1]
    mine = pl.multiple_of(where[0] * width, ATT_DIM)
    theirs = pl.multiple_of((1 - where[0]) * width, ATT_DIM)
    out[:, pl.ds(mine, width)] = own[...]
    out[:, pl.ds(theirs, width)] = arrived[...]


def join(where, own, arrived):
    tokens, width = own.shape
    return pl.pallas_call(
        join_kernel,
        out_shape=jax.ShapeDtypeStruct((tokens, 2 * width), own.dtype),
        in_specs=[pl.BlockSpec(memory_space=pltpu.SMEM), vmem(), vmem()],
        out_specs=vmem(),
        name="join",
    )(where, own, arrived)


def updated(weights, momentum, grads):
    new_momentum = 0.9 * momentum + grads
    moved = weights - new_momentum
    keep_norm = jnp.sqrt(jnp.mean(weights * weights, axis=-1, keepdims=True))
    new_weights = (
        moved * keep_norm * lax.rsqrt(jnp.mean(moved * moved, axis=-1, keepdims=True) + EPS)
    )
    return new_weights, new_momentum


def layer(queries, key_rows, value_rows, step_rates, fast_weights, momentum, out_gain):
    count = lax.axis_size("seq")
    routes = Routes(count)
    local_tokens = queries.shape[0]
    heads, width = step_rates.shape[0], fast_weights.shape[2]
    owned = fast_weights.shape[1]
    assert heads == 2
    here = lax.axis_index("seq")
    core = here % 2
    chip = here // 2
    is_home = core == (2 * here) // count
    where = jnp.stack([core, chip % 2, chip]).astype(jnp.int32)

    my_rate = lax.dynamic_slice_in_dim(step_rates, core, 1, 0)
    their_rate = lax.dynamic_slice_in_dim(step_rates, 1 - core, 1, 0)
    rates = jnp.concatenate([my_rate, send(their_rate, routes.partner)], axis=0)
    rates = jnp.concatenate([rates, send(rates, routes.x_swap)], axis=0)
    rates = rates.reshape(4 * local_tokens, 1)

    def by_core(array):
        kept = lax.dynamic_slice_in_dim(array, core * width, width, 1)
        sent = lax.dynamic_slice_in_dim(array, (1 - core) * width, width, 1)
        return jnp.stack([kept, send(sent, routes.partner)])

    k_own = by_core(key_rows)
    v_own = by_core(value_rows)
    k_own, v_own, rates = lax.optimization_barrier((k_own, v_own, rates))
    q_own = by_core(queries)

    pair_weights = jnp.concatenate([fast_weights, send(fast_weights, routes.pair_in)], axis=1)

    k_near = send(k_own, routes.x_swap)
    v_near = send(v_own, routes.x_swap)
    cut = 3 * ATT_DIM
    early = jnp.concatenate([k_own[:, :, :cut], v_own[:, :, :cut]], axis=0)
    late = jnp.concatenate([k_own[:, :, cut:], v_own[:, :, cut:]], axis=0)
    unit = pair_weights.astype(BF16)
    units = gather_z(unit, routes, is_home)
    side_units = [send(part, routes.y_swap) for part in units]
    grad_scale = 1.0 / math.sqrt(local_tokens * count)
    tokens_in = (k_own, v_own, k_near, v_near, rates)

    upper = chip // 2 % 2 == 1
    early_y = send(early, routes.y_swap)
    early_z = send(early_y, routes.z_up)
    early_two = jnp.where(upper, early_y, early_z)
    early_back = send(early_two, routes.back_x)
    late, _ = lax.optimization_barrier((late, side_units))
    late_y = send(late, routes.y_swap)
    late_z = send(late_y, routes.z_up)
    late_two = jnp.where(upper, late_y, late_z)
    late_back = send(late_two, routes.back_x)

    side_grads = key_side(grad_scale, *tokens_in, side_units, BF16)
    side_in = send(side_grads, routes.y_swap)
    own_grads = key_side(grad_scale, *tokens_in, units, F32)
    sums = own_grads + side_in.astype(F32)
    total = reduce_z([sums[k] for k in range(len(units))], routes)
    pair_momentum = jnp.concatenate([momentum, send(momentum, routes.pair_in)], axis=1)
    att_in = (where, q_own, k_own, v_own, k_near, v_near)
    early_att = attention(*att_in, early_two, early_back, 0)
    late_att = attention(*att_in, late_two, late_back, cut)

    pair_new, _ = updated(pair_weights, pair_momentum, total)
    applied = gather_plane(gather_z(pair_new.astype(BF16), routes, is_home), routes)
    partner_grads = send(total[:, owned:], routes.pair_out)
    grads = jnp.where(is_home, total[:, :owned], partner_grads)
    new_weights, new_momentum = updated(fast_weights, momentum, grads)
    gain = lax.dynamic_slice_in_dim(out_gain, core * width, width, 0).reshape(1, width)
    own, other = query_side(where, q_own, applied, gain, (early_att, late_att))
    arrived = send(other, routes.partner)
    layer_out = join(where, own, arrived)
    return (layer_out, new_weights, new_momentum)


def solution(mesh):
    placed = (
        P(("groups", "seq"), None),
        P(("groups", "seq"), None),
        P(("groups", "seq"), None),
        P(None, ("groups", "seq")),
        P(None, "seq", None),
        P("groups", "seq", None),
        P(),
    )
    return jax.shard_map(
        layer,
        mesh=mesh,
        in_specs=placed,
        out_specs=(P(("groups", "seq"), None), P("groups", "seq", None), P("groups", "seq", None)),
        check_vma=False,
    )
```

```python
import math

import jax
import jax.numpy as jnp
from jax import lax
from jax.experimental import pallas as pl
from jax.experimental.pallas import tpu as pltpu
from jax.sharding import PartitionSpec as P


ATT_DIM = 128
WINDOW = 1024
EPS = 1e-06
MASKED = -1e30
BF16 = jnp.bfloat16
F32 = jnp.float32


class Routes:
    def __init__(self, count):
        self.count = count
        half = count // 16
        self.bits = [1 << b for b in range(half.bit_length() - 1)]
        assert count % 16 == 0 and half == 1 << len(self.bits)
        home = [dev for dev in range(count) if self.is_home(dev)]
        away = [dev for dev in range(count) if not self.is_home(dev)]
        self.partner = [(dev, dev ^ 1) for dev in range(count)]
        self.x_swap = [(dev, dev ^ 2) for dev in range(count)]
        self.y_swap = [(dev, dev ^ 4) for dev in range(count)]
        self.pair_in = [(dev ^ 1, dev) for dev in home]
        self.pair_out = [(dev, dev ^ 1) for dev in home]
        shift = half * 8
        self.cross_out = [(dev, (dev + shift) % count) for dev in home]
        self.home_swap = [[(dev, dev ^ (8 * k)) for dev in home] for k in range(half)]
        self.away_swap = [[(dev, dev ^ (8 * k)) for dev in away] for k in range(half)]
        self.z_swap = [[(dev, dev ^ (8 * k)) for dev in range(count)] for k in range(half)]
        self.cross_back = [(dev, (dev + shift) % count) for dev in away]
        self.z_up = [(dev, dev + 8) for dev in range(count - 8) if dev % 8 < 4]
        self.back_x = [(dev, dev - 2) for dev in range(count) if dev % 4 >= 2]

    def is_home(self, dev):
        return (dev % 2) == (2 * dev // self.count)


def send(array, route):
    return lax.ppermute(array, "seq", route)


def gather_z(unit, routes, is_home):
    home_list = [unit]
    away_list = [send(unit, routes.cross_out)]
    for bit in routes.bits:
        home_list = home_list + [send(part, routes.home_swap[bit]) for part in home_list]
        away_list = away_list + [send(part, routes.away_swap[bit]) for part in away_list]
    return [jnp.where(is_home, home, away) for home, away in zip(home_list, away_list)]


def gather_plane(units, routes):
    pieces = []
    for idx, own in enumerate(units):
        first, second = (
            (routes.x_swap, routes.y_swap) if idx % 2 == 0 else (routes.y_swap, routes.x_swap)
        )
        near = send(own, first)
        side = send(own, second)
        pieces += [own, near, side, send(near, second)]
    return pieces


def fold_kernel(keep_from, send_from, low, arrived, keep, sent):
    count = keep.shape[0]
    total = low[...] + arrived[...].astype(F32)
    keep[...] = total[keep_from : keep_from + count]
    sent[...] = total[send_from : send_from + count].astype(BF16)


def fold(low, arrived):
    count = low.shape[0]
    half = max(count // 2, 1)
    shape = (half,) + low.shape[1:]
    return pl.pallas_call(
        lambda *refs: fold_kernel(0, count - half, *refs),
        out_shape=[jax.ShapeDtypeStruct(shape, F32), jax.ShapeDtypeStruct(shape, BF16)],
        in_specs=[vmem(), vmem()],
        out_specs=[vmem(), vmem()],
        cost_estimate=pl.CostEstimate(flops=low.size, bytes_accessed=12 * low.size, transcendentals=0),
    )(low, arrived)


def update_kernel(part, crossed, weights, momentum, total, applied):
    grads = part[0] + crossed[0].astype(F32)
    total[...] = grads
    applied[...] = updated(weights[...], momentum[...], grads)[0].astype(BF16)


def update_pair(part, crossed, weights, momentum):
    return pl.pallas_call(
        update_kernel,
        out_shape=[
            jax.ShapeDtypeStruct(weights.shape, F32),
            jax.ShapeDtypeStruct(weights.shape, BF16),
        ],
        in_specs=[vmem()] * 4,
        out_specs=[vmem()] * 2,
        cost_estimate=pl.CostEstimate(
            flops=10 * weights.size, bytes_accessed=20 * weights.size, transcendentals=0
        ),
        name="update",
    )(part, crossed, weights, momentum)


def nt_dot(left, right):
    return lax.dot_general(left, right, (((1,), (1,)), ((), ())), preferred_element_type=F32)


def nn_dot(left, right):
    return lax.dot_general(left, right, (((1,), (0,)), ((), ())), preferred_element_type=F32)


def vmem():
    return pl.BlockSpec(memory_space=pltpu.VMEM)


def key_kernel(grad_scale, *refs):
    k_own, v_own, k_near, v_near, rates = refs[:5]
    units = refs[5:-5]
    out, keys, ograd, pair, down = refs[-5:]
    tokens = k_own.shape[1]
    parts = len(units)
    step = units[0].shape[1]
    rows = parts * step
    by_token = jnp.transpose(rates[...] * (-grad_scale))
    for idx, (k_ref, v_ref) in enumerate(((k_own, v_own), (k_near, v_near))):
        for side in range(2):
            at = (2 * idx + side) * tokens
            keys[at : at + tokens, :] = k_ref[side]
            rate = by_token[:, 2 * idx + side : 2 * idx + side + 1]
            ograd[at : at + tokens, :] = (rate * v_ref[side].astype(F32)).astype(BF16)
    for idx in range(parts):
        pair[idx * step : (idx + 1) * step, :] = units[idx][0]
        pair[rows + idx * step : rows + (idx + 1) * step, :] = units[idx][1]
        down[idx * step : (idx + 1) * step, :] = units[idx][2]
    both = nt_dot(pair[...], keys[...])
    gate, up = both[:rows], both[rows:]
    hidden_grad = nt_dot(down[...], ograd[...])
    sig = jax.nn.sigmoid(gate)
    silu = gate * sig
    hidden = (silu * up).astype(BF16)
    gate_grad = (hidden_grad * up * (sig * (1.0 + gate * (1.0 - sig)))).astype(BF16)
    up_grad = (hidden_grad * silu).astype(BF16)
    first = nn_dot(jnp.concatenate([gate_grad, up_grad], axis=0), keys[...])
    second = nn_dot(hidden, ograd[...])
    for idx in range(parts):
        at = idx * step
        out[idx, 0] = first[at : at + step].astype(out.dtype)
        out[idx, 1] = first[rows + at : rows + at + step].astype(out.dtype)
        out[idx, 2] = second[at : at + step].astype(out.dtype)


def key_side(grad_scale, k_own, v_own, k_near, v_near, rates, units, kind):
    _, tokens, width = k_own.shape
    parts = len(units)
    step = units[0].shape[1]
    rows = parts * step
    return pl.pallas_call(
        lambda *refs: key_kernel(grad_scale, *refs),
        out_shape=jax.ShapeDtypeStruct((parts, 3, step, width), kind),
        in_specs=[vmem()] * (5 + parts),
        out_specs=vmem(),
        scratch_shapes=[
            pltpu.VMEM((4 * tokens, width), BF16),
            pltpu.VMEM((4 * tokens, width), BF16),
            pltpu.VMEM((2 * rows, width), BF16),
            pltpu.VMEM((rows, width), BF16),
        ],
        cost_estimate=pl.CostEstimate(
            flops=12 * 4 * tokens * rows * width,
            bytes_accessed=16 * tokens * width,
            transcendentals=0,
        ),
    )(k_own, v_own, k_near, v_near, rates, *units)


def load_rows(pieces, weights):
    rows = pieces[0].shape[1]
    for idx, piece in enumerate(pieces):
        weights[:, idx * rows : (idx + 1) * rows, :] = piece[...]


def fast_product(quer_in, weights):
    quer = jnp.concatenate([quer_in[0], quer_in[1]], axis=0)
    gate = nt_dot(quer, weights[0])
    up = nt_dot(quer, weights[1])
    hidden = (gate * jax.nn.sigmoid(gate) * up).astype(BF16)
    return nn_dot(hidden, weights[2])


def query_first_kernel(count, *refs):
    quer_in = refs[0]
    out, weights = refs[1 + count :]
    load_rows(refs[1 : 1 + count], weights)
    out[...] = fast_product(quer_in, weights)


def query_first(quer_in, pieces):
    _, tokens, width = quer_in.shape
    count = len(pieces)
    rows = pieces[0].shape[1]
    return pl.pallas_call(
        lambda *refs: query_first_kernel(count, *refs),
        out_shape=jax.ShapeDtypeStruct((2 * tokens, width), F32),
        in_specs=[vmem()] * (1 + count),
        out_specs=vmem(),
        scratch_shapes=[pltpu.VMEM((3, count * rows, width), BF16)],
        cost_estimate=pl.CostEstimate(
            flops=12 * tokens * count * rows * width,
            bytes_accessed=6 * count * rows * width,
            transcendentals=0,
        ),
        name="query_first",
    )(quer_in, *pieces)


def query_last_kernel(count, *refs):
    where, quer_in = refs[:2]
    sums, gain, att_a, att_b, own, other, weights = refs[2 + count :]
    tokens, width = other.shape
    load_rows(refs[2 : 2 + count], weights)
    fast = sums[...] + fast_product(quer_in, weights)
    scale = lax.rsqrt(jnp.mean(fast * fast, axis=-1, keepdims=True) + EPS)
    normed = fast * scale * gain[...]
    here = pl.multiple_of(where[0] * width, ATT_DIM)
    at = [pl.multiple_of(core * tokens, tokens) for core in (where[0], 1 - where[0])]
    att = [
        jnp.concatenate([ref[pl.ds(base, tokens), :] for ref in (att_a, att_b)], axis=1)
        for base in at
    ]
    own[:, pl.ds(here, width)] = (normed[:tokens] + att[0]).astype(BF16)
    other[...] = (normed[tokens:] + att[1]).astype(BF16)


def query_last(where, quer_in, pieces, sums, gain, atts):
    _, tokens, width = quer_in.shape
    count = len(pieces)
    rows = pieces[0].shape[1]
    return pl.pallas_call(
        lambda *refs: query_last_kernel(count, *refs),
        out_shape=[
            jax.ShapeDtypeStruct((tokens, 2 * width), BF16),
            jax.ShapeDtypeStruct((tokens, width), BF16),
        ],
        in_specs=[pl.BlockSpec(memory_space=pltpu.SMEM)] + [vmem()] * (5 + count),
        out_specs=[vmem()] * 2,
        scratch_shapes=[pltpu.VMEM((3, count * rows, width), BF16)],
        cost_estimate=pl.CostEstimate(
            flops=12 * tokens * count * rows * width,
            bytes_accessed=6 * count * rows * width,
            transcendentals=0,
        ),
        name="query_last",
    )(where, quer_in, *pieces, sums, gain, *atts)


def att_kernel(low, where, quer_in, k_own, v_own, k_near, v_near, two, back, out,
               quer, keys, vals, bias):
    tokens = quer_in.shape[1]
    span = 2 * tokens
    reach = WINDOW + span
    wide = out.shape[1]
    cols = slice(low, low + wide)
    core, odd, chip = where[0], where[1], where[2]
    mine = core * tokens
    theirs = (1 - core) * tokens

    def put(dest, base, first, second):
        dest[pl.ds(pl.multiple_of(base + mine, tokens), tokens), :] = first
        dest[pl.ds(pl.multiple_of(base + theirs, tokens), tokens), :] = second

    put(quer, 0, quer_in[0, :, cols], quer_in[1, :, cols])
    for idx, (dest, own, near) in enumerate(((keys, k_own, k_near), (vals, v_own, v_near))):
        put(dest, 2 * span, own[0, :, cols], own[1, :, cols])
        put(dest, 0, two[2 * idx], two[2 * idx + 1])

        @pl.when(odd == 1)
        def _():
            put(dest, span, near[0, :, cols], near[1, :, cols])

        @pl.when(odd == 0)
        def _():
            put(dest, span, back[2 * idx], back[2 * idx + 1])

    scale = 1.0 / math.sqrt(ATT_DIM)
    row = lax.broadcasted_iota(jnp.int32, (span, reach), 0)
    col = lax.broadcasted_iota(jnp.int32, (span, reach), 1)
    seen = (col > row) & (col <= row + WINDOW) & (chip * span - WINDOW + col >= 0)
    bias[...] = jnp.where(seen, 0.0, MASKED)
    for head in range(wide // ATT_DIM):
        at = slice(head * ATT_DIM, (head + 1) * ATT_DIM)
        scores = nt_dot(quer[:, at], keys[:, at]) + bias[...]
        top = jnp.max(scores, axis=-1, keepdims=True)
        probs = jnp.exp((scores - top) * scale)
        norm = jnp.sum(probs, axis=-1, keepdims=True)
        att = nn_dot(probs.astype(BF16), vals[:, at]) / norm
        out[:, at] = att * lax.rsqrt(jnp.mean(att * att, axis=-1, keepdims=True) + EPS)


def attention(where, quer_in, k_own, v_own, k_near, v_near, two, back, low):
    _, tokens, _ = quer_in.shape
    wide = two.shape[2]
    span = 2 * tokens
    reach = WINDOW + span
    assert WINDOW == 2 * span
    return pl.pallas_call(
        lambda *refs: att_kernel(low, *refs),
        out_shape=jax.ShapeDtypeStruct((span, wide), F32),
        in_specs=[pl.BlockSpec(memory_space=pltpu.SMEM)] + [vmem()] * 7,
        out_specs=vmem(),
        scratch_shapes=[
            pltpu.VMEM((span, wide), BF16),
            pltpu.VMEM((reach, wide), BF16),
            pltpu.VMEM((reach, wide), BF16),
            pltpu.VMEM((span, reach), F32),
        ],
        cost_estimate=pl.CostEstimate(
            flops=4 * span * reach * wide,
            bytes_accessed=40 * tokens * wide,
            transcendentals=span * reach * wide // ATT_DIM,
        ),
    )(where, quer_in, k_own, v_own, k_near, v_near, two, back)


def updated(weights, momentum, grads):
    new_momentum = 0.9 * momentum + grads
    moved = weights - new_momentum
    keep_norm = jnp.sqrt(jnp.mean(weights * weights, axis=-1, keepdims=True))
    new_weights = (
        moved * keep_norm * lax.rsqrt(jnp.mean(moved * moved, axis=-1, keepdims=True) + EPS)
    )
    return new_weights, new_momentum


def layer(queries, key_rows, value_rows, step_rates, fast_weights, momentum, out_gain):
    count = lax.axis_size("seq")
    routes = Routes(count)
    local_tokens = queries.shape[0]
    heads, width = step_rates.shape[0], fast_weights.shape[2]
    owned = fast_weights.shape[1]
    assert heads == 2
    here = lax.axis_index("seq")
    core = here % 2
    chip = here // 2
    is_home = core == (2 * here) // count
    where = jnp.stack([core, chip % 2, chip]).astype(jnp.int32)

    my_rate = lax.dynamic_slice_in_dim(step_rates, core, 1, 0)
    their_rate = lax.dynamic_slice_in_dim(step_rates, 1 - core, 1, 0)
    rates = jnp.concatenate([my_rate, send(their_rate, routes.partner)], axis=0)
    rates = jnp.concatenate([rates, send(rates, routes.x_swap)], axis=0)

    def by_core(array):
        kept = lax.dynamic_slice_in_dim(array, core * width, width, 1)
        sent = lax.dynamic_slice_in_dim(array, (1 - core) * width, width, 1)
        return jnp.stack([kept, send(sent, routes.partner)])

    k_own = by_core(key_rows)
    v_own = by_core(value_rows)
    q_own = by_core(queries)

    pair_weights = jnp.concatenate([fast_weights, send(fast_weights, routes.pair_in)], axis=1)

    k_near = send(k_own, routes.x_swap)
    v_near = send(v_own, routes.x_swap)
    cut = 3 * ATT_DIM
    early = jnp.concatenate([k_own[:, :, :cut], v_own[:, :, :cut]], axis=0)
    late = jnp.concatenate([k_own[:, :, cut:], v_own[:, :, cut:]], axis=0)
    unit = pair_weights.astype(BF16)
    units = gather_z(unit, routes, is_home)
    side_units = [send(part, routes.y_swap) for part in units]
    grad_scale = 1.0 / math.sqrt(local_tokens * count)
    tokens_in = (k_own, v_own, k_near, v_near, rates)

    upper = chip // 2 % 2 == 1
    early_y = send(early, routes.y_swap)
    early_z = send(early_y, routes.z_up)
    early_two = jnp.where(upper, early_y, early_z)
    early_back = send(early_two, routes.back_x)
    late, _ = lax.optimization_barrier((late, side_units))
    late_y = send(late, routes.y_swap)
    late_z = send(late_y, routes.z_up)
    late_two = jnp.where(upper, late_y, late_z)
    late_back = send(late_two, routes.back_x)

    side_grads = key_side(grad_scale, *tokens_in, side_units, BF16)
    side_in = send(side_grads, routes.y_swap)
    own_grads = key_side(grad_scale, *tokens_in, units, F32)
    part, sent = fold(own_grads, side_in)
    for bit in reversed(routes.bits):
        part, sent = fold(part, send(sent, routes.z_swap[bit]))
    crossed = send(sent, routes.cross_back)
    their_momentum = send(momentum, routes.pair_in)
    pair_momentum = jnp.concatenate([momentum, their_momentum], axis=1)
    att_in = (where, q_own, k_own, v_own, k_near, v_near)
    early_att = attention(*att_in, early_two, early_back, 0)
    late_att = attention(*att_in, late_two, late_back, cut)

    total, pair_new = update_pair(part, crossed, pair_weights, pair_momentum)
    applied = gather_plane(gather_z(pair_new, routes, is_home), routes)
    partner_grads = send(total[:, owned:], routes.pair_out)
    grads = jnp.where(is_home, total[:, :owned], partner_grads)
    new_weights, new_momentum = updated(fast_weights, momentum, grads)
    gain = lax.dynamic_slice_in_dim(out_gain, core * width, width, 0).reshape(1, width)
    soon = [piece for idx, piece in enumerate(applied) if idx % 4 != 3]
    last = applied[3::4]
    sums = query_first(q_own, soon)
    own, other = query_last(where, q_own, last, sums, gain, (early_att, late_att))
    arrived = send(other, routes.partner)
    layer_out = lax.dynamic_update_slice_in_dim(own, arrived, (1 - core) * width, 1)
    return (layer_out, new_weights, new_momentum)


def solution(mesh):
    placed = (
        P(("groups", "seq"), None),
        P(("groups", "seq"), None),
        P(("groups", "seq"), None),
        P(None, ("groups", "seq")),
        P(None, "seq", None),
        P("groups", "seq", None),
        P(),
    )
    return jax.shard_map(
        layer,
        mesh=mesh,
        in_specs=placed,
        out_specs=(P(("groups", "seq"), None), P("groups", "seq", None), P("groups", "seq", None)),
        check_vma=False,
    )
```

```python
import math

import jax
import jax.numpy as jnp
from jax import lax
from jax.experimental import pallas as pl
from jax.experimental.pallas import tpu as pltpu
from jax.sharding import PartitionSpec as P


ATT_DIM = 128
WINDOW = 1024
EPS = 1e-06
MASKED = -1e30
BF16 = jnp.bfloat16
F32 = jnp.float32


class Routes:
    def __init__(self, count):
        self.count = count
        half = count // 16
        self.bits = [1 << b for b in range(half.bit_length() - 1)]
        assert count % 16 == 0 and half == 1 << len(self.bits)
        home = [dev for dev in range(count) if self.is_home(dev)]
        away = [dev for dev in range(count) if not self.is_home(dev)]
        self.partner = [(dev, dev ^ 1) for dev in range(count)]
        self.x_swap = [(dev, dev ^ 2) for dev in range(count)]
        self.y_swap = [(dev, dev ^ 4) for dev in range(count)]
        self.pair_in = [(dev ^ 1, dev) for dev in home]
        self.pair_out = [(dev, dev ^ 1) for dev in home]
        shift = half * 8
        self.cross_out = [(dev, (dev + shift) % count) for dev in home]
        self.home_swap = [[(dev, dev ^ (8 * k)) for dev in home] for k in range(half)]
        self.away_swap = [[(dev, dev ^ (8 * k)) for dev in away] for k in range(half)]
        self.z_swap = [[(dev, dev ^ (8 * k)) for dev in range(count)] for k in range(half)]
        self.cross_back = [(dev, (dev + shift) % count) for dev in away]
        self.z_up_near = [(dev, dev + 8) for dev in range(count - 8) if dev % 8 < 4]
        self.z_up_far = [(dev, dev + 8) for dev in range(count - 8) if dev % 8 >= 4]
        self.back_x = [(dev, dev - 2) for dev in range(count) if dev % 4 >= 2]

    def is_home(self, dev):
        return (dev % 2) == (2 * dev // self.count)


def send(array, route):
    return lax.ppermute(array, "seq", route)


def gather_z(unit, routes, is_home):
    home_list = [unit]
    away_list = [send(unit, routes.cross_out)]
    for bit in routes.bits:
        home_list = home_list + [send(part, routes.home_swap[bit]) for part in home_list]
        away_list = away_list + [send(part, routes.away_swap[bit]) for part in away_list]
    return [jnp.where(is_home, home, away) for home, away in zip(home_list, away_list)]


def gather_plane(units, routes):
    pieces = []
    for idx, own in enumerate(units):
        first, second = (
            (routes.x_swap, routes.y_swap) if idx % 2 == 0 else (routes.y_swap, routes.x_swap)
        )
        near = send(own, first)
        side = send(own, second)
        pieces += [own, near, side, send(near, second)]
    return pieces


def fold_kernel(keep_from, send_from, low, arrived, keep, sent):
    count = keep.shape[0]
    total = low[...] + arrived[...].astype(F32)
    keep[...] = total[keep_from : keep_from + count]
    sent[...] = total[send_from : send_from + count].astype(BF16)


def fold(low, arrived):
    count = low.shape[0]
    half = max(count // 2, 1)
    shape = (half,) + low.shape[1:]
    return pl.pallas_call(
        lambda *refs: fold_kernel(0, count - half, *refs),
        out_shape=[jax.ShapeDtypeStruct(shape, F32), jax.ShapeDtypeStruct(shape, BF16)],
        in_specs=[vmem(), vmem()],
        out_specs=[vmem(), vmem()],
        compiler_params=grant(10),
        cost_estimate=pl.CostEstimate(flops=low.size, bytes_accessed=12 * low.size, transcendentals=0),
    )(low, arrived)


def update_kernel(part, crossed, w_own, w_near, m_own, m_near, total, applied):
    owned = w_own.shape[1]
    for idx, (weights, momentum) in enumerate(((w_own, m_own), (w_near, m_near))):
        rows = slice(idx * owned, (idx + 1) * owned)
        grads = part[0, :, rows] + crossed[0, :, rows].astype(F32)
        total[idx] = grads
        applied[:, rows] = updated(weights[...], momentum[...], grads)[0].astype(BF16)


def update_pair(part, crossed, *pairs):
    shape = pairs[0].shape
    rows = (shape[0], 2 * shape[1], shape[2])
    return pl.pallas_call(
        update_kernel,
        out_shape=[
            jax.ShapeDtypeStruct((2,) + shape, F32),
            jax.ShapeDtypeStruct(rows, BF16),
        ],
        in_specs=[vmem()] * 6,
        out_specs=[vmem()] * 2,
        compiler_params=grant(10),
        cost_estimate=pl.CostEstimate(
            flops=20 * math.prod(shape), bytes_accessed=40 * math.prod(shape), transcendentals=0
        ),
        name="update",
    )(part, crossed, *pairs)


def nt_dot(left, right):
    return lax.dot_general(left, right, (((1,), (1,)), ((), ())), preferred_element_type=F32)


def nn_dot(left, right):
    return lax.dot_general(left, right, (((1,), (0,)), ((), ())), preferred_element_type=F32)


def vmem():
    return pl.BlockSpec(memory_space=pltpu.VMEM)


def grant(mebibytes):
    return pltpu.CompilerParams(vmem_limit_bytes=mebibytes << 20)


def key_kernel(grad_scale, *refs):
    k_own, v_own, k_near, v_near, r_own, r_near = refs[:6]
    units = refs[6:-5]
    out, keys, ograd, pair, down = refs[-5:]
    tokens = k_own.shape[1]
    parts = len(units)
    step = units[0].shape[1]
    rows = parts * step
    rates = jnp.concatenate([r_own[...], r_near[...]], axis=0)
    by_token = jnp.transpose(rates * (-grad_scale))
    for idx, (k_ref, v_ref) in enumerate(((k_own, v_own), (k_near, v_near))):
        for side in range(2):
            at = (2 * idx + side) * tokens
            keys[at : at + tokens, :] = k_ref[side]
            rate = by_token[:, 2 * idx + side : 2 * idx + side + 1]
            ograd[at : at + tokens, :] = (rate * v_ref[side].astype(F32)).astype(BF16)
    for idx in range(parts):
        pair[idx * step : (idx + 1) * step, :] = units[idx][0]
        pair[rows + idx * step : rows + (idx + 1) * step, :] = units[idx][1]
        down[idx * step : (idx + 1) * step, :] = units[idx][2]
    both = nt_dot(pair[...], keys[...])
    gate, up = both[:rows], both[rows:]
    hidden_grad = nt_dot(down[...], ograd[...])
    sig = jax.nn.sigmoid(gate)
    silu = gate * sig
    hidden = (silu * up).astype(BF16)
    gate_grad = (hidden_grad * up * (sig * (1.0 + gate * (1.0 - sig)))).astype(BF16)
    up_grad = (hidden_grad * silu).astype(BF16)
    first = nn_dot(jnp.concatenate([gate_grad, up_grad], axis=0), keys[...])
    second = nn_dot(hidden, ograd[...])
    for idx in range(parts):
        at = idx * step
        out[idx, 0] = first[at : at + step].astype(out.dtype)
        out[idx, 1] = first[rows + at : rows + at + step].astype(out.dtype)
        out[idx, 2] = second[at : at + step].astype(out.dtype)


def key_side(grad_scale, tokens_in, units, kind):
    _, tokens, width = tokens_in[0].shape
    parts = len(units)
    step = units[0].shape[1]
    rows = parts * step
    return pl.pallas_call(
        lambda *refs: key_kernel(grad_scale, *refs),
        out_shape=jax.ShapeDtypeStruct((parts, 3, step, width), kind),
        in_specs=[vmem()] * (6 + parts),
        out_specs=vmem(),
        scratch_shapes=[
            pltpu.VMEM((4 * tokens, width), BF16),
            pltpu.VMEM((4 * tokens, width), BF16),
            pltpu.VMEM((2 * rows, width), BF16),
            pltpu.VMEM((rows, width), BF16),
        ],
        compiler_params=grant(30),
        cost_estimate=pl.CostEstimate(
            flops=12 * 4 * tokens * rows * width,
            bytes_accessed=16 * tokens * width,
            transcendentals=0,
        ),
    )(*tokens_in, *units)


def load_rows(pieces, weights):
    rows = pieces[0].shape[1]
    for idx, piece in enumerate(pieces):
        weights[:, idx * rows : (idx + 1) * rows, :] = piece[...]


def fast_product(quer_in, weights):
    quer = jnp.concatenate([part[...] for part in quer_in], axis=0)
    gate = nt_dot(quer, weights[0])
    up = nt_dot(quer, weights[1])
    hidden = (gate * jax.nn.sigmoid(gate) * up).astype(BF16)
    return nn_dot(hidden, weights[2])


def query_first_kernel(count, *refs):
    quer_in = refs[:2]
    out, weights = refs[2 + count :]
    load_rows(refs[2 : 2 + count], weights)
    out[...] = fast_product(quer_in, weights)


def query_first(quer_in, pieces):
    tokens, width = quer_in[0].shape
    count = len(pieces)
    rows = pieces[0].shape[1]
    return pl.pallas_call(
        lambda *refs: query_first_kernel(count, *refs),
        out_shape=jax.ShapeDtypeStruct((2 * tokens, width), F32),
        in_specs=[vmem()] * (2 + count),
        out_specs=vmem(),
        scratch_shapes=[pltpu.VMEM((3, count * rows, width), BF16)],
        compiler_params=grant(24),
        cost_estimate=pl.CostEstimate(
            flops=12 * tokens * count * rows * width,
            bytes_accessed=6 * count * rows * width,
            transcendentals=0,
        ),
        name="query_first",
    )(*quer_in, *pieces)


def query_last_kernel(count, *refs):
    where, quer_in = refs[0], refs[1:3]
    sums, gain, att_a, att_b, own, other, weights = refs[3 + count :]
    tokens, width = other.shape
    load_rows(refs[3 : 3 + count], weights)
    fast = sums[...] + fast_product(quer_in, weights)
    scale = lax.rsqrt(jnp.mean(fast * fast, axis=-1, keepdims=True) + EPS)
    normed = fast * scale * gain[...]
    here = pl.multiple_of(where[0] * width, ATT_DIM)
    at = [pl.multiple_of(core * tokens, tokens) for core in (where[0], 1 - where[0])]
    att = [
        jnp.concatenate([ref[pl.ds(base, tokens), :] for ref in (att_a, att_b)], axis=1)
        for base in at
    ]
    own[:, pl.ds(here, width)] = (normed[:tokens] + att[0]).astype(BF16)
    other[...] = (normed[tokens:] + att[1]).astype(BF16)


def query_last(where, quer_in, pieces, sums, gain, atts):
    tokens, width = quer_in[0].shape
    count = len(pieces)
    rows = pieces[0].shape[1]
    return pl.pallas_call(
        lambda *refs: query_last_kernel(count, *refs),
        out_shape=[
            jax.ShapeDtypeStruct((tokens, 2 * width), BF16),
            jax.ShapeDtypeStruct((tokens, width), BF16),
        ],
        in_specs=[pl.BlockSpec(memory_space=pltpu.SMEM)] + [vmem()] * (6 + count),
        out_specs=[vmem()] * 2,
        scratch_shapes=[pltpu.VMEM((3, count * rows, width), BF16)],
        compiler_params=grant(24),
        cost_estimate=pl.CostEstimate(
            flops=12 * tokens * count * rows * width,
            bytes_accessed=6 * count * rows * width,
            transcendentals=0,
        ),
        name="query_last",
    )(where, *quer_in, *pieces, sums, gain, *atts)


def att_kernel(low, where, q_kept, q_came, k_own, v_own, k_near, v_near, two, back, out,
               quer, keys, vals, bias):
    tokens = q_kept.shape[0]
    span = 2 * tokens
    reach = WINDOW + span
    wide = out.shape[1]
    cols = slice(low, low + wide)
    core, odd, chip = where[0], where[1], where[2]
    mine = core * tokens
    theirs = (1 - core) * tokens

    def put(dest, base, first, second):
        dest[pl.ds(pl.multiple_of(base + mine, tokens), tokens), :] = first
        dest[pl.ds(pl.multiple_of(base + theirs, tokens), tokens), :] = second

    put(quer, 0, q_kept[:, cols], q_came[:, cols])
    for idx, (dest, own, near) in enumerate(((keys, k_own, k_near), (vals, v_own, v_near))):
        put(dest, 2 * span, own[0, :, cols], own[1, :, cols])
        put(dest, 0, two[2 * idx], two[2 * idx + 1])

        @pl.when(odd == 1)
        def _():
            put(dest, span, near[0, :, cols], near[1, :, cols])

        @pl.when(odd == 0)
        def _():
            put(dest, span, back[2 * idx], back[2 * idx + 1])

    scale = 1.0 / math.sqrt(ATT_DIM)
    row = lax.broadcasted_iota(jnp.int32, (span, reach), 0)
    col = lax.broadcasted_iota(jnp.int32, (span, reach), 1)
    seen = (col > row) & (col <= row + WINDOW) & (chip * span - WINDOW + col >= 0)
    bias[...] = jnp.where(seen, 0.0, MASKED)
    for head in range(wide // ATT_DIM):
        at = slice(head * ATT_DIM, (head + 1) * ATT_DIM)
        scores = nt_dot(quer[:, at], keys[:, at]) + bias[...]
        top = jnp.max(scores, axis=-1, keepdims=True)
        probs = jnp.exp((scores - top) * scale)
        norm = jnp.sum(probs, axis=-1, keepdims=True)
        att = nn_dot(probs.astype(BF16), vals[:, at]) / norm
        out[:, at] = att * lax.rsqrt(jnp.mean(att * att, axis=-1, keepdims=True) + EPS)


def attention(where, quer_in, k_own, v_own, k_near, v_near, two, back, low):
    tokens = quer_in[0].shape[0]
    wide = two.shape[2]
    span = 2 * tokens
    reach = WINDOW + span
    assert WINDOW == 2 * span
    return pl.pallas_call(
        lambda *refs: att_kernel(low, *refs),
        out_shape=jax.ShapeDtypeStruct((span, wide), F32),
        in_specs=[pl.BlockSpec(memory_space=pltpu.SMEM)] + [vmem()] * 8,
        out_specs=vmem(),
        scratch_shapes=[
            pltpu.VMEM((span, wide), BF16),
            pltpu.VMEM((reach, wide), BF16),
            pltpu.VMEM((reach, wide), BF16),
            pltpu.VMEM((span, reach), F32),
        ],
        compiler_params=grant(30),
        cost_estimate=pl.CostEstimate(
            flops=4 * span * reach * wide,
            bytes_accessed=40 * tokens * wide,
            transcendentals=span * reach * wide // ATT_DIM,
        ),
    )(where, *quer_in, k_own, v_own, k_near, v_near, two, back)


def updated(weights, momentum, grads):
    new_momentum = 0.9 * momentum + grads
    moved = weights - new_momentum
    keep_norm = jnp.sqrt(jnp.mean(weights * weights, axis=-1, keepdims=True))
    new_weights = (
        moved * keep_norm * lax.rsqrt(jnp.mean(moved * moved, axis=-1, keepdims=True) + EPS)
    )
    return new_weights, new_momentum


def layer(queries, key_rows, value_rows, step_rates, fast_weights, momentum, out_gain):
    count = lax.axis_size("seq")
    routes = Routes(count)
    local_tokens = queries.shape[0]
    heads, width = step_rates.shape[0], fast_weights.shape[2]
    assert heads == 2
    here = lax.axis_index("seq")
    core = here % 2
    chip = here // 2
    is_home = core == (2 * here) // count
    where = jnp.stack([core, chip % 2, chip]).astype(jnp.int32)

    my_rate = lax.dynamic_slice_in_dim(step_rates, core, 1, 0)
    their_rate = lax.dynamic_slice_in_dim(step_rates, 1 - core, 1, 0)
    r_own = jnp.concatenate([my_rate, send(their_rate, routes.partner)], axis=0)
    r_near = send(r_own, routes.x_swap)

    def by_core(array):
        kept = lax.dynamic_slice_in_dim(array, core * width, width, 1)
        sent = lax.dynamic_slice_in_dim(array, (1 - core) * width, width, 1)
        return kept, send(sent, routes.partner)

    k_own = jnp.stack(by_core(key_rows))
    v_own = jnp.stack(by_core(value_rows))
    q_own = by_core(queries)

    their_weights = send(fast_weights, routes.pair_in)
    their_momentum = send(momentum, routes.pair_in)

    k_near = send(k_own, routes.x_swap)
    v_near = send(v_own, routes.x_swap)
    cut = 2 * ATT_DIM
    early = jnp.concatenate([k_own[:, :, :cut], v_own[:, :, :cut]], axis=0)
    late = jnp.concatenate([k_own[:, :, cut:], v_own[:, :, cut:]], axis=0)
    unit = jnp.concatenate([fast_weights.astype(BF16), their_weights.astype(BF16)], axis=1)
    units = gather_z(unit, routes, is_home)
    side_units = [send(part, routes.y_swap) for part in units]
    grad_scale = 1.0 / math.sqrt(local_tokens * count)
    tokens_in = (k_own, v_own, k_near, v_near, r_own, r_near)

    upper = chip // 2 % 2 == 1
    early_y = send(early, routes.y_swap)
    early_z = send(early_y, routes.z_up_near)
    early_two = jnp.where(upper, early_y, early_z)
    early_back = send(early_two, routes.back_x)
    late_in, _ = lax.optimization_barrier((late, units))
    late_z = send(late_in, routes.z_up_far)

    side_grads = key_side(grad_scale, tokens_in, side_units, BF16)
    side_in = send(side_grads, routes.y_swap)
    own_grads = key_side(grad_scale, tokens_in, units, F32)
    late_turn = jnp.where(upper, late_z, late)
    side_in, late_turn = lax.optimization_barrier((side_in, late_turn))
    late_two = send(late_turn, routes.y_swap)
    late_back = send(late_two, routes.back_x)
    part, sent = fold(own_grads, side_in)
    for bit in reversed(routes.bits):
        part, sent = fold(part, send(sent, routes.z_swap[bit]))
    crossed = send(sent, routes.cross_back)
    att_in = (where, q_own, k_own, v_own, k_near, v_near)
    early_att = attention(*att_in, early_two, early_back, 0)
    late_att = attention(*att_in, late_two, late_back, cut)

    total, pair_new = update_pair(
        part, crossed, fast_weights, their_weights, momentum, their_momentum
    )
    applied = gather_plane(gather_z(pair_new, routes, is_home), routes)
    partner_grads = send(total[1], routes.pair_out)
    grads = jnp.where(is_home, total[0], partner_grads)
    new_weights, new_momentum = updated(fast_weights, momentum, grads)
    gain = lax.dynamic_slice_in_dim(out_gain, core * width, width, 0).reshape(1, width)
    soon = [piece for idx, piece in enumerate(applied) if idx % 4 < 2]
    last = [piece for idx, piece in enumerate(applied) if idx % 4 >= 2]
    new_weights, new_momentum, gain = lax.optimization_barrier((new_weights, new_momentum, gain))
    sums = query_first(q_own, soon)
    own, other = query_last(where, q_own, last, sums, gain, (early_att, late_att))
    arrived = send(other, routes.partner)
    layer_out = lax.dynamic_update_slice_in_dim(own, arrived, (1 - core) * width, 1)
    return (layer_out, new_weights, new_momentum)


def solution(mesh):
    placed = (
        P(("groups", "seq"), None),
        P(("groups", "seq"), None),
        P(("groups", "seq"), None),
        P(None, ("groups", "seq")),
        P(None, "seq", None),
        P("groups", "seq", None),
        P(),
    )
    return jax.shard_map(
        layer,
        mesh=mesh,
        in_specs=placed,
        out_specs=(P(("groups", "seq"), None), P("groups", "seq", None), P("groups", "seq", None)),
        check_vma=False,
    )
```

```python
import math

import jax
import jax.numpy as jnp
from jax import lax
from jax.experimental import pallas as pl
from jax.experimental.pallas import tpu as pltpu
from jax.sharding import PartitionSpec as P


ATT_DIM = 128
WINDOW = 1024
EPS = 1e-06
MASKED = -1e30
BF16 = jnp.bfloat16
F32 = jnp.float32


class Routes:
    def __init__(self, count):
        self.count = count
        half = count // 16
        self.bits = [1 << b for b in range(half.bit_length() - 1)]
        assert count % 16 == 0 and half == 1 << len(self.bits)
        home = [dev for dev in range(count) if self.is_home(dev)]
        away = [dev for dev in range(count) if not self.is_home(dev)]
        self.partner = [(dev, dev ^ 1) for dev in range(count)]
        self.x_swap = [(dev, dev ^ 2) for dev in range(count)]
        self.y_swap = [(dev, dev ^ 4) for dev in range(count)]
        self.pair_in = [(dev ^ 1, dev) for dev in home]
        self.pair_out = [(dev, dev ^ 1) for dev in home]
        shift = half * 8
        self.cross_out = [(dev, (dev + shift) % count) for dev in home]
        self.home_swap = [[(dev, dev ^ (8 * k)) for dev in home] for k in range(half)]
        self.away_swap = [[(dev, dev ^ (8 * k)) for dev in away] for k in range(half)]
        self.z_swap = [[(dev, dev ^ (8 * k)) for dev in range(count)] for k in range(half)]
        self.cross_back = [(dev, (dev + shift) % count) for dev in away]
        self.z_up_near = [(dev, dev + 8) for dev in range(count - 8) if dev % 8 < 4]
        self.z_up_far = [(dev, dev + 8) for dev in range(count - 8) if dev % 8 >= 4]
        self.back_x = [(dev, dev - 2) for dev in range(count) if dev % 4 >= 2]

    def is_home(self, dev):
        return (dev % 2) == (2 * dev // self.count)


def send(array, route):
    return lax.ppermute(array, "seq", route)


def gather_z(unit, routes, is_home):
    home_list = [unit]
    away_list = [send(unit, routes.cross_out)]
    for bit in routes.bits:
        home_list = home_list + [send(part, routes.home_swap[bit]) for part in home_list]
        away_list = away_list + [send(part, routes.away_swap[bit]) for part in away_list]
    return [jnp.where(is_home, home, away) for home, away in zip(home_list, away_list)]


def gather_plane(units, routes):
    pieces = []
    for idx, own in enumerate(units):
        first, second = (
            (routes.x_swap, routes.y_swap) if idx % 2 == 0 else (routes.y_swap, routes.x_swap)
        )
        near = send(own, first)
        side = send(own, second)
        pieces += [own, near, side, send(near, second)]
    return pieces


def fold_kernel(keep_from, send_from, low, arrived, keep, sent):
    count = keep.shape[0]
    total = low[...] + arrived[...].astype(F32)
    keep[...] = total[keep_from : keep_from + count]
    sent[...] = total[send_from : send_from + count].astype(BF16)


def fold(low, arrived):
    count = low.shape[0]
    half = max(count // 2, 1)
    shape = (half,) + low.shape[1:]
    return pl.pallas_call(
        lambda *refs: fold_kernel(0, count - half, *refs),
        out_shape=[jax.ShapeDtypeStruct(shape, F32), jax.ShapeDtypeStruct(shape, BF16)],
        in_specs=[vmem(), vmem()],
        out_specs=[vmem(), vmem()],
        compiler_params=grant(10),
        cost_estimate=pl.CostEstimate(flops=low.size, bytes_accessed=12 * low.size, transcendentals=0),
    )(low, arrived)


def update_kernel(part, crossed, w_own, w_near, m_own, m_near, total, applied):
    owned = w_own.shape[1]
    for idx, (weights, momentum) in enumerate(((w_own, m_own), (w_near, m_near))):
        rows = slice(idx * owned, (idx + 1) * owned)
        grads = part[0, :, rows] + crossed[0, :, rows].astype(F32)
        total[idx] = grads
        applied[:, rows] = updated(weights[...], momentum[...], grads)[0].astype(BF16)


def update_pair(part, crossed, *pairs):
    shape = pairs[0].shape
    rows = (shape[0], 2 * shape[1], shape[2])
    return pl.pallas_call(
        update_kernel,
        out_shape=[
            jax.ShapeDtypeStruct((2,) + shape, F32),
            jax.ShapeDtypeStruct(rows, BF16),
        ],
        in_specs=[vmem()] * 6,
        out_specs=[vmem()] * 2,
        compiler_params=grant(10),
        cost_estimate=pl.CostEstimate(
            flops=20 * math.prod(shape), bytes_accessed=40 * math.prod(shape), transcendentals=0
        ),
        name="update",
    )(part, crossed, *pairs)


def nt_dot(left, right):
    return lax.dot_general(left, right, (((1,), (1,)), ((), ())), preferred_element_type=F32)


def nn_dot(left, right):
    return lax.dot_general(left, right, (((1,), (0,)), ((), ())), preferred_element_type=F32)


def vmem():
    return pl.BlockSpec(memory_space=pltpu.VMEM)


def grant(mebibytes):
    return pltpu.CompilerParams(vmem_limit_bytes=mebibytes << 20)


def key_kernel(grad_scale, *refs):
    k_own, v_own, k_near, v_near, r_own, r_near = refs[:6]
    units = refs[6:-5]
    out, keys, ograd, pair, down = refs[-5:]
    tokens = k_own.shape[1]
    parts = len(units)
    step = units[0].shape[1]
    rows = parts * step
    rates = jnp.concatenate([r_own[...], r_near[...]], axis=0)
    by_token = jnp.transpose(rates * (-grad_scale))
    for idx, (k_ref, v_ref) in enumerate(((k_own, v_own), (k_near, v_near))):
        for side in range(2):
            at = (2 * idx + side) * tokens
            keys[at : at + tokens, :] = k_ref[side]
            rate = by_token[:, 2 * idx + side : 2 * idx + side + 1]
            ograd[at : at + tokens, :] = (rate * v_ref[side].astype(F32)).astype(BF16)
    for idx in range(parts):
        pair[idx * step : (idx + 1) * step, :] = units[idx][0]
        pair[rows + idx * step : rows + (idx + 1) * step, :] = units[idx][1]
        down[idx * step : (idx + 1) * step, :] = units[idx][2]
    both = nt_dot(pair[...], keys[...])
    gate, up = both[:rows], both[rows:]
    hidden_grad = nt_dot(down[...], ograd[...])
    sig = jax.nn.sigmoid(gate)
    silu = gate * sig
    hidden = (silu * up).astype(BF16)
    gate_grad = (hidden_grad * up * (sig * (1.0 + gate * (1.0 - sig)))).astype(BF16)
    up_grad = (hidden_grad * silu).astype(BF16)
    first = nn_dot(jnp.concatenate([gate_grad, up_grad], axis=0), keys[...])
    second = nn_dot(hidden, ograd[...])
    for idx in range(parts):
        at = idx * step
        out[idx, 0] = first[at : at + step].astype(out.dtype)
        out[idx, 1] = first[rows + at : rows + at + step].astype(out.dtype)
        out[idx, 2] = second[at : at + step].astype(out.dtype)


def key_side(grad_scale, tokens_in, units, kind):
    _, tokens, width = tokens_in[0].shape
    parts = len(units)
    step = units[0].shape[1]
    rows = parts * step
    return pl.pallas_call(
        lambda *refs: key_kernel(grad_scale, *refs),
        out_shape=jax.ShapeDtypeStruct((parts, 3, step, width), kind),
        in_specs=[vmem()] * (6 + parts),
        out_specs=vmem(),
        scratch_shapes=[
            pltpu.VMEM((4 * tokens, width), BF16),
            pltpu.VMEM((4 * tokens, width), BF16),
            pltpu.VMEM((2 * rows, width), BF16),
            pltpu.VMEM((rows, width), BF16),
        ],
        compiler_params=grant(30),
        cost_estimate=pl.CostEstimate(
            flops=12 * 4 * tokens * rows * width,
            bytes_accessed=16 * tokens * width,
            transcendentals=0,
        ),
    )(*tokens_in, *units)


def load_rows(pieces, weights):
    rows = pieces[0].shape[1]
    for idx, piece in enumerate(pieces):
        weights[:, idx * rows : (idx + 1) * rows, :] = piece[...]


def fast_product(quer_in, weights):
    quer = jnp.concatenate([part[...] for part in quer_in], axis=0)
    gate = nt_dot(quer, weights[0])
    up = nt_dot(quer, weights[1])
    hidden = (gate * jax.nn.sigmoid(gate) * up).astype(BF16)
    return nn_dot(hidden, weights[2])


def query_first_kernel(count, *refs):
    quer_in = refs[:2]
    out, weights = refs[2 + count :]
    load_rows(refs[2 : 2 + count], weights)
    out[...] = fast_product(quer_in, weights)


def query_first(quer_in, pieces):
    tokens, width = quer_in[0].shape
    count = len(pieces)
    rows = pieces[0].shape[1]
    return pl.pallas_call(
        lambda *refs: query_first_kernel(count, *refs),
        out_shape=jax.ShapeDtypeStruct((2 * tokens, width), F32),
        in_specs=[vmem()] * (2 + count),
        out_specs=vmem(),
        scratch_shapes=[pltpu.VMEM((3, count * rows, width), BF16)],
        compiler_params=grant(24),
        cost_estimate=pl.CostEstimate(
            flops=12 * tokens * count * rows * width,
            bytes_accessed=6 * count * rows * width,
            transcendentals=0,
        ),
        name="query_first",
    )(*quer_in, *pieces)


def query_last_kernel(count, *refs):
    where, quer_in = refs[0], refs[1:3]
    sums, gain, att_a, att_b, own, other, weights = refs[3 + count :]
    tokens, width = other.shape
    load_rows(refs[3 : 3 + count], weights)
    fast = sums[...] + fast_product(quer_in, weights)
    scale = lax.rsqrt(jnp.mean(fast * fast, axis=-1, keepdims=True) + EPS)
    normed = fast * scale * gain[...]
    here = pl.multiple_of(where[0] * width, ATT_DIM)
    at = [pl.multiple_of(core * tokens, tokens) for core in (where[0], 1 - where[0])]
    att = [
        jnp.concatenate([ref[pl.ds(base, tokens), :] for ref in (att_a, att_b)], axis=1)
        for base in at
    ]
    own[:, pl.ds(here, width)] = (normed[:tokens] + att[0]).astype(BF16)
    other[...] = (normed[tokens:] + att[1]).astype(BF16)


def query_last(where, quer_in, pieces, sums, gain, atts):
    tokens, width = quer_in[0].shape
    count = len(pieces)
    rows = pieces[0].shape[1]
    return pl.pallas_call(
        lambda *refs: query_last_kernel(count, *refs),
        out_shape=[
            jax.ShapeDtypeStruct((tokens, 2 * width), BF16),
            jax.ShapeDtypeStruct((tokens, width), BF16),
        ],
        in_specs=[pl.BlockSpec(memory_space=pltpu.SMEM)] + [vmem()] * (6 + count),
        out_specs=[vmem()] * 2,
        scratch_shapes=[pltpu.VMEM((3, count * rows, width), BF16)],
        compiler_params=grant(24),
        cost_estimate=pl.CostEstimate(
            flops=12 * tokens * count * rows * width,
            bytes_accessed=6 * count * rows * width,
            transcendentals=0,
        ),
        name="query_last",
    )(where, *quer_in, *pieces, sums, gain, *atts)


def att_kernel(low, where, q_kept, q_came, k_own, v_own, k_near, v_near, two, back, out,
               quer, keys, vals, bias):
    tokens = q_kept.shape[0]
    span = 2 * tokens
    reach = WINDOW + span
    wide = out.shape[1]
    cols = slice(low, low + wide)
    core, odd, chip = where[0], where[1], where[2]
    mine = core * tokens
    theirs = (1 - core) * tokens

    def put(dest, base, first, second):
        dest[pl.ds(pl.multiple_of(base + mine, tokens), tokens), :] = first
        dest[pl.ds(pl.multiple_of(base + theirs, tokens), tokens), :] = second

    put(quer, 0, q_kept[:, cols], q_came[:, cols])
    for idx, (dest, own, near) in enumerate(((keys, k_own, k_near), (vals, v_own, v_near))):
        put(dest, 2 * span, own[0, :, cols], own[1, :, cols])
        put(dest, 0, two[2 * idx], two[2 * idx + 1])

        @pl.when(odd == 1)
        def _():
            put(dest, span, near[0, :, cols], near[1, :, cols])

        @pl.when(odd == 0)
        def _():
            put(dest, span, back[2 * idx], back[2 * idx + 1])

    scale = 1.0 / math.sqrt(ATT_DIM)
    row = lax.broadcasted_iota(jnp.int32, (span, reach), 0)
    col = lax.broadcasted_iota(jnp.int32, (span, reach), 1)
    seen = (col > row) & (col <= row + WINDOW) & (chip * span - WINDOW + col >= 0)
    bias[...] = jnp.where(seen, 0.0, MASKED)
    for head in range(wide // ATT_DIM):
        at = slice(head * ATT_DIM, (head + 1) * ATT_DIM)
        scores = nt_dot(quer[:, at], keys[:, at]) + bias[...]
        top = jnp.max(scores, axis=-1, keepdims=True)
        probs = jnp.exp((scores - top) * scale)
        norm = jnp.sum(probs, axis=-1, keepdims=True)
        att = nn_dot(probs.astype(BF16), vals[:, at]) / norm
        out[:, at] = att * lax.rsqrt(jnp.mean(att * att, axis=-1, keepdims=True) + EPS)


def attention(where, quer_in, k_own, v_own, k_near, v_near, two, back, low):
    tokens = quer_in[0].shape[0]
    wide = two.shape[2]
    span = 2 * tokens
    reach = WINDOW + span
    assert WINDOW == 2 * span
    return pl.pallas_call(
        lambda *refs: att_kernel(low, *refs),
        out_shape=jax.ShapeDtypeStruct((span, wide), F32),
        in_specs=[pl.BlockSpec(memory_space=pltpu.SMEM)] + [vmem()] * 8,
        out_specs=vmem(),
        scratch_shapes=[
            pltpu.VMEM((span, wide), BF16),
            pltpu.VMEM((reach, wide), BF16),
            pltpu.VMEM((reach, wide), BF16),
            pltpu.VMEM((span, reach), F32),
        ],
        compiler_params=grant(30),
        cost_estimate=pl.CostEstimate(
            flops=4 * span * reach * wide,
            bytes_accessed=40 * tokens * wide,
            transcendentals=span * reach * wide // ATT_DIM,
        ),
    )(where, *quer_in, k_own, v_own, k_near, v_near, two, back)


def updated(weights, momentum, grads):
    new_momentum = 0.9 * momentum + grads
    moved = weights - new_momentum
    keep_norm = jnp.sqrt(jnp.mean(weights * weights, axis=-1, keepdims=True))
    new_weights = (
        moved * keep_norm * lax.rsqrt(jnp.mean(moved * moved, axis=-1, keepdims=True) + EPS)
    )
    return new_weights, new_momentum


def layer(queries, key_rows, value_rows, step_rates, fast_weights, momentum, out_gain):
    count = lax.axis_size("seq")
    routes = Routes(count)
    local_tokens = queries.shape[0]
    heads, width = step_rates.shape[0], fast_weights.shape[2]
    assert heads == 2
    here = lax.axis_index("seq")
    core = here % 2
    chip = here // 2
    is_home = core == (2 * here) // count
    where = jnp.stack([core, chip % 2, chip]).astype(jnp.int32)

    my_rate = lax.dynamic_slice_in_dim(step_rates, core, 1, 0)
    their_rate = lax.dynamic_slice_in_dim(step_rates, 1 - core, 1, 0)
    r_own = jnp.concatenate([my_rate, send(their_rate, routes.partner)], axis=0)
    r_near = send(r_own, routes.x_swap)

    def by_core(array):
        kept = lax.dynamic_slice_in_dim(array, core * width, width, 1)
        sent = lax.dynamic_slice_in_dim(array, (1 - core) * width, width, 1)
        return kept, send(sent, routes.partner)

    k_own = jnp.stack(by_core(key_rows))
    v_own = jnp.stack(by_core(value_rows))
    q_own = by_core(queries)

    their_weights = send(fast_weights, routes.pair_in)
    their_momentum = send(momentum, routes.pair_in)

    k_near = send(k_own, routes.x_swap)
    v_near = send(v_own, routes.x_swap)
    cut = 3 * ATT_DIM
    k_held, v_held = lax.optimization_barrier((k_own, v_own))
    early = jnp.concatenate([k_held[:, :, :cut], v_held[:, :, :cut]], axis=0)
    late = jnp.concatenate([k_held[:, :, cut:], v_held[:, :, cut:]], axis=0)
    unit = jnp.concatenate([fast_weights.astype(BF16), their_weights.astype(BF16)], axis=1)
    units = gather_z(unit, routes, is_home)
    side_units = [send(part, routes.y_swap) for part in units]
    grad_scale = 1.0 / math.sqrt(local_tokens * count)
    tokens_in = (k_own, v_own, k_near, v_near, r_own, r_near)

    upper = chip // 2 % 2 == 1
    early_y = send(early, routes.y_swap)
    early_z = send(early_y, routes.z_up_near)
    early_two = jnp.where(upper, early_y, early_z)
    early_back = send(early_two, routes.back_x)
    late_in, _ = lax.optimization_barrier((late, units))
    late_z = send(late_in, routes.z_up_far)

    side_grads = key_side(grad_scale, tokens_in, side_units, BF16)
    side_in = send(side_grads, routes.y_swap)
    own_grads = key_side(grad_scale, tokens_in, units, F32)
    late_turn = jnp.where(upper, late_z, late)
    side_in, late_turn = lax.optimization_barrier((side_in, late_turn))
    late_two = send(late_turn, routes.y_swap)
    late_back = send(late_two, routes.back_x)
    part, sent = fold(own_grads, side_in)
    for bit in reversed(routes.bits):
        part, sent = fold(part, send(sent, routes.z_swap[bit]))
    crossed = send(sent, routes.cross_back)
    att_in = (where, q_own, k_own, v_own, k_near, v_near)
    early_att = attention(*att_in, early_two, early_back, 0)
    late_att = attention(*att_in, late_two, late_back, cut)

    total, pair_new = update_pair(
        part, crossed, fast_weights, their_weights, momentum, their_momentum
    )
    applied = gather_plane(gather_z(pair_new, routes, is_home), routes)
    gain = lax.dynamic_slice_in_dim(out_gain, core * width, width, 0).reshape(1, width)
    soon = [piece for idx, piece in enumerate(applied) if idx % 4 < 2]
    last = [piece for idx, piece in enumerate(applied) if idx % 4 >= 2]
    sums = query_first(q_own, soon)
    total, sums, late_att = lax.optimization_barrier((total, sums, late_att))
    partner_grads = send(total[1], routes.pair_out)
    grads = jnp.where(is_home, total[0], partner_grads)
    new_weights, new_momentum = updated(fast_weights, momentum, grads)
    new_weights, new_momentum, gain = lax.optimization_barrier((new_weights, new_momentum, gain))
    own, other = query_last(where, q_own, last, sums, gain, (early_att, late_att))
    arrived = send(other, routes.partner)
    layer_out = lax.dynamic_update_slice_in_dim(own, arrived, (1 - core) * width, 1)
    return (layer_out, new_weights, new_momentum)


def solution(mesh):
    placed = (
        P(("groups", "seq"), None),
        P(("groups", "seq"), None),
        P(("groups", "seq"), None),
        P(None, ("groups", "seq")),
        P(None, "seq", None),
        P("groups", "seq", None),
        P(),
    )
    return jax.shard_map(
        layer,
        mesh=mesh,
        in_specs=placed,
        out_specs=(P(("groups", "seq"), None), P("groups", "seq", None), P("groups", "seq", None)),
        check_vma=False,
    )
```

```python
import math

import jax
import jax.numpy as jnp
from jax import lax
from jax.experimental import pallas as pl
from jax.experimental.pallas import tpu as pltpu
from jax.sharding import PartitionSpec as P


ATT_DIM = 128
WINDOW = 1024
EPS = 1e-06
MASKED = -1e30
BF16 = jnp.bfloat16
F32 = jnp.float32


class Routes:
    def __init__(self, count):
        self.count = count
        half = count // 16
        self.bits = [1 << b for b in range(half.bit_length() - 1)]
        assert count % 16 == 0 and half == 1 << len(self.bits)
        home = [dev for dev in range(count) if self.is_home(dev)]
        away = [dev for dev in range(count) if not self.is_home(dev)]
        self.partner = [(dev, dev ^ 1) for dev in range(count)]
        self.x_swap = [(dev, dev ^ 2) for dev in range(count)]
        self.y_swap = [(dev, dev ^ 4) for dev in range(count)]
        self.pair_in = [(dev ^ 1, dev) for dev in home]
        self.pair_out = [(dev, dev ^ 1) for dev in home]
        shift = half * 8
        self.cross_out = [(dev, (dev + shift) % count) for dev in home]
        self.home_swap = [[(dev, dev ^ (8 * k)) for dev in home] for k in range(half)]
        self.away_swap = [[(dev, dev ^ (8 * k)) for dev in away] for k in range(half)]
        self.cross_back = [
            [(dev, ((dev ^ (8 * k)) + shift) % count) for dev in away] for k in range(half)
        ]
        self.z_up_near = [(dev, dev + 8) for dev in range(count - 8) if dev % 8 < 4]
        self.z_up_far = [(dev, dev + 8) for dev in range(count - 8) if dev % 8 >= 4]
        self.back_x = [(dev, dev - 2) for dev in range(count) if dev % 4 >= 2]

    def is_home(self, dev):
        return (dev % 2) == (2 * dev // self.count)


def send(array, route):
    return lax.ppermute(array, "seq", route)


def gather_z(unit, routes, is_home):
    home_list = [unit]
    away_list = [send(unit, routes.cross_out)]
    for bit in routes.bits:
        home_list = home_list + [send(part, routes.home_swap[bit]) for part in home_list]
        away_list = away_list + [send(part, routes.away_swap[bit]) for part in away_list]
    return [jnp.where(is_home, home, away) for home, away in zip(home_list, away_list)]


def gather_plane(units, routes):
    pieces = []
    for idx, own in enumerate(units):
        first, second = (
            (routes.x_swap, routes.y_swap) if idx % 2 == 0 else (routes.y_swap, routes.x_swap)
        )
        near = send(own, first)
        side = send(own, second)
        pieces += [own, near, side, send(near, second)]
    return pieces


def fold_kernel(low, arrived, keep, *sent):
    for idx, ref in enumerate(sent):
        total = low[idx] + arrived[idx].astype(F32)
        ref[...] = total.astype(BF16)
        if idx == 0:
            keep[...] = total


def fold(low, arrived):
    shape = low.shape[1:]
    sent = [jax.ShapeDtypeStruct(shape, BF16)] * low.shape[0]
    return pl.pallas_call(
        fold_kernel,
        out_shape=[jax.ShapeDtypeStruct(shape, F32)] + sent,
        in_specs=[vmem(), vmem()],
        out_specs=[vmem()] * (1 + len(sent)),
        compiler_params=grant(10),
        cost_estimate=pl.CostEstimate(flops=low.size, bytes_accessed=12 * low.size, transcendentals=0),
        name="fold",
    )(low, arrived)


def update_kernel(part, *refs):
    arrived = refs[:-6]
    w_own, w_near, m_own, m_near, total, applied = refs[-6:]
    owned = w_own.shape[1]
    for idx, (weights, momentum) in enumerate(((w_own, m_own), (w_near, m_near))):
        rows = slice(idx * owned, (idx + 1) * owned)
        grads = part[:, rows]
        for came in arrived:
            grads = grads + came[:, rows].astype(F32)
        total[idx] = grads
        applied[:, rows] = updated(weights[...], momentum[...], grads)[0].astype(BF16)


def update_pair(part, arrived, *pairs):
    shape = pairs[0].shape
    rows = (shape[0], 2 * shape[1], shape[2])
    return pl.pallas_call(
        update_kernel,
        out_shape=[
            jax.ShapeDtypeStruct((2,) + shape, F32),
            jax.ShapeDtypeStruct(rows, BF16),
        ],
        in_specs=[vmem()] * (5 + len(arrived)),
        out_specs=[vmem()] * 2,
        compiler_params=grant(12),
        cost_estimate=pl.CostEstimate(
            flops=20 * math.prod(shape), bytes_accessed=40 * math.prod(shape), transcendentals=0
        ),
        name="update",
    )(part, *arrived, *pairs)


def nt_dot(left, right):
    return lax.dot_general(left, right, (((1,), (1,)), ((), ())), preferred_element_type=F32)


def nn_dot(left, right):
    return lax.dot_general(left, right, (((1,), (0,)), ((), ())), preferred_element_type=F32)


def vmem():
    return pl.BlockSpec(memory_space=pltpu.VMEM)


def grant(mebibytes):
    return pltpu.CompilerParams(vmem_limit_bytes=mebibytes << 20)


def key_kernel(grad_scale, *refs):
    k_own, v_own, k_near, v_near, r_own, r_near = refs[:6]
    units = refs[6:-5]
    out, keys, ograd, pair, down = refs[-5:]
    tokens = k_own.shape[1]
    parts = len(units)
    step = units[0].shape[1]
    rows = parts * step
    rates = jnp.concatenate([r_own[...], r_near[...]], axis=0)
    by_token = jnp.transpose(rates * (-grad_scale))
    for idx, (k_ref, v_ref) in enumerate(((k_own, v_own), (k_near, v_near))):
        for side in range(2):
            at = (2 * idx + side) * tokens
            keys[at : at + tokens, :] = k_ref[side]
            rate = by_token[:, 2 * idx + side : 2 * idx + side + 1]
            ograd[at : at + tokens, :] = (rate * v_ref[side].astype(F32)).astype(BF16)
    for idx in range(parts):
        pair[idx * step : (idx + 1) * step, :] = units[idx][0]
        pair[rows + idx * step : rows + (idx + 1) * step, :] = units[idx][1]
        down[idx * step : (idx + 1) * step, :] = units[idx][2]
    both = nt_dot(pair[...], keys[...])
    gate, up = both[:rows], both[rows:]
    hidden_grad = nt_dot(down[...], ograd[...])
    sig = jax.nn.sigmoid(gate)
    silu = gate * sig
    hidden = (silu * up).astype(BF16)
    gate_grad = (hidden_grad * up * (sig * (1.0 + gate * (1.0 - sig)))).astype(BF16)
    up_grad = (hidden_grad * silu).astype(BF16)
    first = nn_dot(jnp.concatenate([gate_grad, up_grad], axis=0), keys[...])
    second = nn_dot(hidden, ograd[...])
    for idx in range(parts):
        at = idx * step
        out[idx, 0] = first[at : at + step].astype(out.dtype)
        out[idx, 1] = first[rows + at : rows + at + step].astype(out.dtype)
        out[idx, 2] = second[at : at + step].astype(out.dtype)


def key_side(grad_scale, tokens_in, units, kind):
    _, tokens, width = tokens_in[0].shape
    parts = len(units)
    step = units[0].shape[1]
    rows = parts * step
    return pl.pallas_call(
        lambda *refs: key_kernel(grad_scale, *refs),
        out_shape=jax.ShapeDtypeStruct((parts, 3, step, width), kind),
        in_specs=[vmem()] * (6 + parts),
        out_specs=vmem(),
        scratch_shapes=[
            pltpu.VMEM((4 * tokens, width), BF16),
            pltpu.VMEM((4 * tokens, width), BF16),
            pltpu.VMEM((2 * rows, width), BF16),
            pltpu.VMEM((rows, width), BF16),
        ],
        compiler_params=grant(30),
        cost_estimate=pl.CostEstimate(
            flops=12 * 4 * tokens * rows * width,
            bytes_accessed=16 * tokens * width,
            transcendentals=0,
        ),
    )(*tokens_in, *units)


def load_rows(pieces, weights):
    rows = pieces[0].shape[1]
    for idx, piece in enumerate(pieces):
        weights[:, idx * rows : (idx + 1) * rows, :] = piece[...]


def fast_product(quer_in, weights):
    quer = jnp.concatenate([part[...] for part in quer_in], axis=0)
    gate = nt_dot(quer, weights[0])
    up = nt_dot(quer, weights[1])
    hidden = (gate * jax.nn.sigmoid(gate) * up).astype(BF16)
    return nn_dot(hidden, weights[2])


def query_first_kernel(count, *refs):
    quer_in = refs[:2]
    out, weights = refs[2 + count :]
    load_rows(refs[2 : 2 + count], weights)
    out[...] = fast_product(quer_in, weights)


def query_first(quer_in, pieces):
    tokens, width = quer_in[0].shape
    count = len(pieces)
    rows = pieces[0].shape[1]
    return pl.pallas_call(
        lambda *refs: query_first_kernel(count, *refs),
        out_shape=jax.ShapeDtypeStruct((2 * tokens, width), F32),
        in_specs=[vmem()] * (2 + count),
        out_specs=vmem(),
        scratch_shapes=[pltpu.VMEM((3, count * rows, width), BF16)],
        compiler_params=grant(24),
        cost_estimate=pl.CostEstimate(
            flops=12 * tokens * count * rows * width,
            bytes_accessed=6 * count * rows * width,
            transcendentals=0,
        ),
        name="query_first",
    )(*quer_in, *pieces)


def query_last_kernel(count, *refs):
    where, quer_in = refs[0], refs[1:3]
    sums, gain, att_a, att_b, own, other, weights = refs[3 + count :]
    tokens, width = other.shape
    load_rows(refs[3 : 3 + count], weights)
    fast = sums[...] + fast_product(quer_in, weights)
    scale = lax.rsqrt(jnp.mean(fast * fast, axis=-1, keepdims=True) + EPS)
    normed = fast * scale * gain[...]
    here = pl.multiple_of(where[0] * width, ATT_DIM)
    at = [pl.multiple_of(core * tokens, tokens) for core in (where[0], 1 - where[0])]
    att = [
        jnp.concatenate([ref[pl.ds(base, tokens), :] for ref in (att_a, att_b)], axis=1)
        for base in at
    ]
    own[:, pl.ds(here, width)] = (normed[:tokens] + att[0]).astype(BF16)
    other[...] = (normed[tokens:] + att[1]).astype(BF16)


def query_last(where, quer_in, pieces, sums, gain, atts):
    tokens, width = quer_in[0].shape
    count = len(pieces)
    rows = pieces[0].shape[1]
    return pl.pallas_call(
        lambda *refs: query_last_kernel(count, *refs),
        out_shape=[
            jax.ShapeDtypeStruct((tokens, 2 * width), BF16),
            jax.ShapeDtypeStruct((tokens, width), BF16),
        ],
        in_specs=[pl.BlockSpec(memory_space=pltpu.SMEM)] + [vmem()] * (6 + count),
        out_specs=[vmem()] * 2,
        scratch_shapes=[pltpu.VMEM((3, count * rows, width), BF16)],
        compiler_params=grant(24),
        cost_estimate=pl.CostEstimate(
            flops=12 * tokens * count * rows * width,
            bytes_accessed=6 * count * rows * width,
            transcendentals=0,
        ),
        name="query_last",
    )(where, *quer_in, *pieces, sums, gain, *atts)


def att_kernel(low, where, q_kept, q_came, k_own, v_own, k_near, v_near, two, back, out,
               quer, keys, vals, bias):
    tokens = q_kept.shape[0]
    span = 2 * tokens
    reach = WINDOW + span
    wide = out.shape[1]
    cols = slice(low, low + wide)
    core, odd, chip = where[0], where[1], where[2]
    mine = core * tokens
    theirs = (1 - core) * tokens

    def put(dest, base, first, second):
        dest[pl.ds(pl.multiple_of(base + mine, tokens), tokens), :] = first
        dest[pl.ds(pl.multiple_of(base + theirs, tokens), tokens), :] = second

    put(quer, 0, q_kept[:, cols], q_came[:, cols])
    for idx, (dest, own, near) in enumerate(((keys, k_own, k_near), (vals, v_own, v_near))):
        put(dest, 2 * span, own[0, :, cols], own[1, :, cols])
        put(dest, 0, two[2 * idx], two[2 * idx + 1])

        @pl.when(odd == 1)
        def _():
            put(dest, span, near[0, :, cols], near[1, :, cols])

        @pl.when(odd == 0)
        def _():
            put(dest, span, back[2 * idx], back[2 * idx + 1])

    scale = 1.0 / math.sqrt(ATT_DIM)
    row = lax.broadcasted_iota(jnp.int32, (span, reach), 0)
    col = lax.broadcasted_iota(jnp.int32, (span, reach), 1)
    seen = (col > row) & (col <= row + WINDOW) & (chip * span - WINDOW + col >= 0)
    bias[...] = jnp.where(seen, 0.0, MASKED)
    for head in range(wide // ATT_DIM):
        at = slice(head * ATT_DIM, (head + 1) * ATT_DIM)
        scores = nt_dot(quer[:, at], keys[:, at]) + bias[...]
        top = jnp.max(scores, axis=-1, keepdims=True)
        probs = jnp.exp((scores - top) * scale)
        norm = jnp.sum(probs, axis=-1, keepdims=True)
        att = nn_dot(probs.astype(BF16), vals[:, at]) / norm
        out[:, at] = att * lax.rsqrt(jnp.mean(att * att, axis=-1, keepdims=True) + EPS)


def attention(where, quer_in, k_own, v_own, k_near, v_near, two, back, low):
    tokens = quer_in[0].shape[0]
    wide = two.shape[2]
    span = 2 * tokens
    reach = WINDOW + span
    assert WINDOW == 2 * span
    return pl.pallas_call(
        lambda *refs: att_kernel(low, *refs),
        out_shape=jax.ShapeDtypeStruct((span, wide), F32),
        in_specs=[pl.BlockSpec(memory_space=pltpu.SMEM)] + [vmem()] * 8,
        out_specs=vmem(),
        scratch_shapes=[
            pltpu.VMEM((span, wide), BF16),
            pltpu.VMEM((reach, wide), BF16),
            pltpu.VMEM((reach, wide), BF16),
            pltpu.VMEM((span, reach), F32),
        ],
        compiler_params=grant(30),
        cost_estimate=pl.CostEstimate(
            flops=4 * span * reach * wide,
            bytes_accessed=40 * tokens * wide,
            transcendentals=span * reach * wide // ATT_DIM,
        ),
    )(where, *quer_in, k_own, v_own, k_near, v_near, two, back)


def updated(weights, momentum, grads):
    new_momentum = 0.9 * momentum + grads
    moved = weights - new_momentum
    keep_norm = jnp.sqrt(jnp.mean(weights * weights, axis=-1, keepdims=True))
    new_weights = (
        moved * keep_norm * lax.rsqrt(jnp.mean(moved * moved, axis=-1, keepdims=True) + EPS)
    )
    return new_weights, new_momentum


def layer(queries, key_rows, value_rows, step_rates, fast_weights, momentum, out_gain):
    count = lax.axis_size("seq")
    routes = Routes(count)
    local_tokens = queries.shape[0]
    heads, width = step_rates.shape[0], fast_weights.shape[2]
    assert heads == 2
    here = lax.axis_index("seq")
    core = here % 2
    chip = here // 2
    is_home = core == (2 * here) // count
    where = jnp.stack([core, chip % 2, chip]).astype(jnp.int32)

    my_rate = lax.dynamic_slice_in_dim(step_rates, core, 1, 0)
    their_rate = lax.dynamic_slice_in_dim(step_rates, 1 - core, 1, 0)
    r_own = jnp.concatenate([my_rate, send(their_rate, routes.partner)], axis=0)
    r_near = send(r_own, routes.x_swap)

    def by_core(array):
        kept = lax.dynamic_slice_in_dim(array, core * width, width, 1)
        sent = lax.dynamic_slice_in_dim(array, (1 - core) * width, width, 1)
        return kept, send(sent, routes.partner)

    k_own = jnp.stack(by_core(key_rows))
    v_own = jnp.stack(by_core(value_rows))
    q_own = by_core(queries)

    their_weights = send(fast_weights, routes.pair_in)
    their_momentum = send(momentum, routes.pair_in)

    k_near = send(k_own, routes.x_swap)
    v_near = send(v_own, routes.x_swap)
    cut = 3 * ATT_DIM
    k_held, v_held = lax.optimization_barrier((k_own, v_own))
    early = jnp.concatenate([k_held[:, :, :cut], v_held[:, :, :cut]], axis=0)
    late = jnp.concatenate([k_held[:, :, cut:], v_held[:, :, cut:]], axis=0)
    unit = jnp.concatenate([fast_weights.astype(BF16), their_weights.astype(BF16)], axis=1)
    units = gather_z(unit, routes, is_home)
    side_units = [send(part, routes.y_swap) for part in units]
    grad_scale = 1.0 / math.sqrt(local_tokens * count)
    tokens_in = (k_own, v_own, k_near, v_near, r_own, r_near)

    upper = chip // 2 % 2 == 1
    early_y = send(early, routes.y_swap)
    early_z = send(early_y, routes.z_up_near)
    early_two = jnp.where(upper, early_y, early_z)
    early_back = send(early_two, routes.back_x)
    late_in, _ = lax.optimization_barrier((late, units))
    late_z = send(late_in, routes.z_up_far)

    side_grads = key_side(grad_scale, tokens_in, side_units, BF16)
    side_in = send(side_grads, routes.y_swap)
    own_grads = key_side(grad_scale, tokens_in, units, F32)
    late_turn = jnp.where(upper, late_z, late)
    side_in, late_turn = lax.optimization_barrier((side_in, late_turn))
    late_two = send(late_turn, routes.y_swap)
    late_back = send(late_two, routes.back_x)
    part, *sent = fold(own_grads, side_in)
    arrived = []
    for k in range(len(sent)):
        arrived.append(send(sent[k], routes.cross_back[k]))
    for k in range(1, len(sent)):
        arrived.append(send(sent[k], routes.home_swap[k]))
    att_in = (where, q_own, k_own, v_own, k_near, v_near)
    early_att = attention(*att_in, early_two, early_back, 0)
    late_att = attention(*att_in, late_two, late_back, cut)

    total, pair_new = update_pair(
        part, arrived, fast_weights, their_weights, momentum, their_momentum
    )
    applied = gather_plane(gather_z(pair_new, routes, is_home), routes)
    partner_grads = send(total[1], routes.pair_out)
    gain = lax.dynamic_slice_in_dim(out_gain, core * width, width, 0).reshape(1, width)
    soon = [piece for idx, piece in enumerate(applied) if idx % 4 < 2]
    last = [piece for idx, piece in enumerate(applied) if idx % 4 >= 2]
    sums = query_first(q_own, soon)
    partner_grads, sums = lax.optimization_barrier((partner_grads, sums))
    grads = jnp.where(is_home, total[0], partner_grads)
    new_weights, new_momentum = updated(fast_weights, momentum, grads)
    new_weights, new_momentum, gain = lax.optimization_barrier((new_weights, new_momentum, gain))
    own, other = query_last(where, q_own, last, sums, gain, (early_att, late_att))
    arrived = send(other, routes.partner)
    layer_out = lax.dynamic_update_slice_in_dim(own, arrived, (1 - core) * width, 1)
    return (layer_out, new_weights, new_momentum)


def solution(mesh):
    placed = (
        P(("groups", "seq"), None),
        P(("groups", "seq"), None),
        P(("groups", "seq"), None),
        P(None, ("groups", "seq")),
        P(None, "seq", None),
        P("groups", "seq", None),
        P(),
    )
    return jax.shard_map(
        layer,
        mesh=mesh,
        in_specs=placed,
        out_specs=(P(("groups", "seq"), None), P("groups", "seq", None), P("groups", "seq", None)),
        check_vma=False,
    )
```

```python
import math

import jax
import jax.numpy as jnp
from jax import lax
from jax.experimental import pallas as pl
from jax.experimental.pallas import tpu as pltpu
from jax.sharding import PartitionSpec as P


ATT_DIM = 128
WINDOW = 1024
EPS = 1e-06
MASKED = -1e30
BF16 = jnp.bfloat16
F32 = jnp.float32


class Routes:
    def __init__(self, count):
        self.count = count
        half = count // 16
        self.bits = [1 << b for b in range(half.bit_length() - 1)]
        assert count % 16 == 0 and half == 1 << len(self.bits)
        home = [dev for dev in range(count) if self.is_home(dev)]
        away = [dev for dev in range(count) if not self.is_home(dev)]
        self.partner = [(dev, dev ^ 1) for dev in range(count)]
        self.x_swap = [(dev, dev ^ 2) for dev in range(count)]
        self.y_swap = [(dev, dev ^ 4) for dev in range(count)]
        self.pair_in = [(dev ^ 1, dev) for dev in home]
        self.pair_out = [(dev, dev ^ 1) for dev in home]
        shift = half * 8
        self.cross_out = [(dev, (dev + shift) % count) for dev in home]
        self.home_swap = [[(dev, dev ^ (8 * k)) for dev in home] for k in range(half)]
        self.away_swap = [[(dev, dev ^ (8 * k)) for dev in away] for k in range(half)]
        self.cross_back = [
            [(dev, ((dev ^ (8 * k)) + shift) % count) for dev in away] for k in range(half)
        ]
        self.z_up_near = [(dev, dev + 8) for dev in range(count - 8) if dev % 8 < 4]
        self.z_up_far = [(dev, dev + 8) for dev in range(count - 8) if dev % 8 >= 4]
        self.back_x = [(dev, dev - 2) for dev in range(count) if dev % 4 >= 2]

    def is_home(self, dev):
        return (dev % 2) == (2 * dev // self.count)


def send(array, route):
    return lax.ppermute(array, "seq", route)


def gather_z(unit, routes, is_home):
    home_list = [unit]
    away_list = [send(unit, routes.cross_out)]
    for bit in routes.bits:
        home_list = home_list + [send(part, routes.home_swap[bit]) for part in home_list]
        away_list = away_list + [send(part, routes.away_swap[bit]) for part in away_list]
    return [jnp.where(is_home, home, away) for home, away in zip(home_list, away_list)]


def gather_plane(units, routes):
    pieces = []
    for idx, own in enumerate(units):
        first, second = (
            (routes.x_swap, routes.y_swap) if idx % 2 == 0 else (routes.y_swap, routes.x_swap)
        )
        near = send(own, first)
        side = send(own, second)
        pieces += [own, near, side, send(near, second)]
    return pieces


def fold_kernel(low, arrived, keep, *sent):
    for idx, ref in enumerate(sent):
        total = low[idx] + arrived[idx].astype(F32)
        ref[...] = total.astype(BF16)
        if idx == 0:
            keep[...] = total


def fold(low, arrived):
    shape = low.shape[1:]
    sent = [jax.ShapeDtypeStruct(shape, BF16)] * low.shape[0]
    return pl.pallas_call(
        fold_kernel,
        out_shape=[jax.ShapeDtypeStruct(shape, F32)] + sent,
        in_specs=[vmem(), vmem()],
        out_specs=[vmem()] * (1 + len(sent)),
        compiler_params=grant(10),
        cost_estimate=pl.CostEstimate(flops=low.size, bytes_accessed=12 * low.size, transcendentals=0),
        name="fold",
    )(low, arrived)


def update_kernel(part, *refs):
    arrived = refs[:-6]
    w_own, w_near, m_own, m_near, total, applied = refs[-6:]
    owned = w_own.shape[1]
    for idx, (weights, momentum) in enumerate(((w_own, m_own), (w_near, m_near))):
        rows = slice(idx * owned, (idx + 1) * owned)
        grads = part[:, rows]
        for came in arrived:
            grads = grads + came[:, rows].astype(F32)
        total[idx] = grads
        applied[:, rows] = updated(weights[...], momentum[...], grads)[0].astype(BF16)


def update_pair(part, arrived, *pairs):
    shape = pairs[0].shape
    rows = (shape[0], 2 * shape[1], shape[2])
    return pl.pallas_call(
        update_kernel,
        out_shape=[
            jax.ShapeDtypeStruct((2,) + shape, F32),
            jax.ShapeDtypeStruct(rows, BF16),
        ],
        in_specs=[vmem()] * (5 + len(arrived)),
        out_specs=[vmem()] * 2,
        compiler_params=grant(12),
        cost_estimate=pl.CostEstimate(
            flops=20 * math.prod(shape), bytes_accessed=40 * math.prod(shape), transcendentals=0
        ),
        name="update",
    )(part, *arrived, *pairs)


def nt_dot(left, right):
    return lax.dot_general(left, right, (((1,), (1,)), ((), ())), preferred_element_type=F32)


def nn_dot(left, right):
    return lax.dot_general(left, right, (((1,), (0,)), ((), ())), preferred_element_type=F32)


def vmem():
    return pl.BlockSpec(memory_space=pltpu.VMEM)


def grant(mebibytes):
    return pltpu.CompilerParams(vmem_limit_bytes=mebibytes << 20)


def key_kernel(grad_scale, *refs):
    k_own, v_own, k_near, v_near, r_own, r_near = refs[:6]
    units = refs[6:-5]
    out, keys, ograd, pair, down = refs[-5:]
    tokens = k_own.shape[1]
    parts = len(units)
    step = units[0].shape[1]
    rows = parts * step
    rates = jnp.concatenate([r_own[...], r_near[...]], axis=0)
    by_token = jnp.transpose(rates * (-grad_scale))
    for idx, (k_ref, v_ref) in enumerate(((k_own, v_own), (k_near, v_near))):
        for side in range(2):
            at = (2 * idx + side) * tokens
            keys[at : at + tokens, :] = k_ref[side]
            rate = by_token[:, 2 * idx + side : 2 * idx + side + 1]
            ograd[at : at + tokens, :] = (rate * v_ref[side].astype(F32)).astype(BF16)
    for idx in range(parts):
        pair[idx * step : (idx + 1) * step, :] = units[idx][0]
        pair[rows + idx * step : rows + (idx + 1) * step, :] = units[idx][1]
        down[idx * step : (idx + 1) * step, :] = units[idx][2]
    both = nt_dot(pair[...], keys[...])
    gate, up = both[:rows], both[rows:]
    hidden_grad = nt_dot(down[...], ograd[...])
    sig = jax.nn.sigmoid(gate)
    silu = gate * sig
    hidden = (silu * up).astype(BF16)
    gate_grad = (hidden_grad * up * (sig * (1.0 + gate * (1.0 - sig)))).astype(BF16)
    up_grad = (hidden_grad * silu).astype(BF16)
    first = nn_dot(jnp.concatenate([gate_grad, up_grad], axis=0), keys[...])
    second = nn_dot(hidden, ograd[...])
    for idx in range(parts):
        at = idx * step
        out[idx, 0] = first[at : at + step].astype(out.dtype)
        out[idx, 1] = first[rows + at : rows + at + step].astype(out.dtype)
        out[idx, 2] = second[at : at + step].astype(out.dtype)


def key_side(grad_scale, tokens_in, units, kind):
    _, tokens, width = tokens_in[0].shape
    parts = len(units)
    step = units[0].shape[1]
    rows = parts * step
    return pl.pallas_call(
        lambda *refs: key_kernel(grad_scale, *refs),
        out_shape=jax.ShapeDtypeStruct((parts, 3, step, width), kind),
        in_specs=[vmem()] * (6 + parts),
        out_specs=vmem(),
        scratch_shapes=[
            pltpu.VMEM((4 * tokens, width), BF16),
            pltpu.VMEM((4 * tokens, width), BF16),
            pltpu.VMEM((2 * rows, width), BF16),
            pltpu.VMEM((rows, width), BF16),
        ],
        compiler_params=grant(30),
        cost_estimate=pl.CostEstimate(
            flops=12 * 4 * tokens * rows * width,
            bytes_accessed=16 * tokens * width,
            transcendentals=0,
        ),
    )(*tokens_in, *units)


def load_rows(pieces, weights):
    rows = pieces[0].shape[1]
    for idx, piece in enumerate(pieces):
        weights[:, idx * rows : (idx + 1) * rows, :] = piece[...]


def fast_product(quer_in, weights):
    quer = jnp.concatenate([part[...] for part in quer_in], axis=0)
    gate = nt_dot(quer, weights[0])
    up = nt_dot(quer, weights[1])
    hidden = (gate * jax.nn.sigmoid(gate) * up).astype(BF16)
    return nn_dot(hidden, weights[2])


def query_first_kernel(count, *refs):
    quer_in = refs[:2]
    out, weights = refs[2 + count :]
    load_rows(refs[2 : 2 + count], weights)
    out[...] = fast_product(quer_in, weights)


def query_first(quer_in, pieces):
    tokens, width = quer_in[0].shape
    count = len(pieces)
    rows = pieces[0].shape[1]
    return pl.pallas_call(
        lambda *refs: query_first_kernel(count, *refs),
        out_shape=jax.ShapeDtypeStruct((2 * tokens, width), F32),
        in_specs=[vmem()] * (2 + count),
        out_specs=vmem(),
        scratch_shapes=[pltpu.VMEM((3, count * rows, width), BF16)],
        compiler_params=grant(24),
        cost_estimate=pl.CostEstimate(
            flops=12 * tokens * count * rows * width,
            bytes_accessed=6 * count * rows * width,
            transcendentals=0,
        ),
        name="query_first",
    )(*quer_in, *pieces)


def query_last_kernel(count, *refs):
    where, quer_in = refs[0], refs[1:3]
    sums, gain, att_a, att_b, own, other, weights = refs[3 + count :]
    tokens, width = other.shape
    load_rows(refs[3 : 3 + count], weights)
    fast = sums[...] + fast_product(quer_in, weights)
    scale = lax.rsqrt(jnp.mean(fast * fast, axis=-1, keepdims=True) + EPS)
    normed = fast * scale * gain[...]
    here = pl.multiple_of(where[0] * width, ATT_DIM)
    at = [pl.multiple_of(core * tokens, tokens) for core in (where[0], 1 - where[0])]
    att = [
        jnp.concatenate([ref[pl.ds(base, tokens), :] for ref in (att_a, att_b)], axis=1)
        for base in at
    ]
    own[:, pl.ds(here, width)] = (normed[:tokens] + att[0]).astype(BF16)
    other[...] = (normed[tokens:] + att[1]).astype(BF16)


def query_last(where, quer_in, pieces, sums, gain, atts):
    tokens, width = quer_in[0].shape
    count = len(pieces)
    rows = pieces[0].shape[1]
    return pl.pallas_call(
        lambda *refs: query_last_kernel(count, *refs),
        out_shape=[
            jax.ShapeDtypeStruct((tokens, 2 * width), BF16),
            jax.ShapeDtypeStruct((tokens, width), BF16),
        ],
        in_specs=[pl.BlockSpec(memory_space=pltpu.SMEM)] + [vmem()] * (6 + count),
        out_specs=[vmem()] * 2,
        scratch_shapes=[pltpu.VMEM((3, count * rows, width), BF16)],
        compiler_params=grant(24),
        cost_estimate=pl.CostEstimate(
            flops=12 * tokens * count * rows * width,
            bytes_accessed=6 * count * rows * width,
            transcendentals=0,
        ),
        name="query_last",
    )(where, *quer_in, *pieces, sums, gain, *atts)


def att_kernel(low, where, q_kept, q_came, k_own, v_own, k_near, v_near, two, back, out,
               quer, keys, vals, bias, arrivals):
    tokens = q_kept.shape[0]
    span = 2 * tokens
    reach = WINDOW + span
    wide = out.shape[1]
    cols = slice(low, low + wide)
    core, odd, chip = where[0], where[1], where[2]
    mine = core * tokens
    theirs = (1 - core) * tokens

    copies = []
    for idx, (dest, near) in enumerate(((keys, k_near), (vals, v_near))):
        for side, at in enumerate((mine, theirs)):
            rows = pl.ds(pl.multiple_of(span + at, tokens), tokens)
            copies.append(
                pltpu.make_async_copy(
                    near.at[side, :, pl.ds(low, wide)], dest.at[rows], arrivals.at[2 * idx + side]
                )
            )

    @pl.when(odd == 1)
    def _():
        for copy in copies:
            copy.start()

    def put(dest, base, first, second):
        dest[pl.ds(pl.multiple_of(base + mine, tokens), tokens), :] = first
        dest[pl.ds(pl.multiple_of(base + theirs, tokens), tokens), :] = second

    put(quer, 0, q_kept[:, cols], q_came[:, cols])
    for idx, (dest, own) in enumerate(((keys, k_own), (vals, v_own))):
        put(dest, 2 * span, own[0, :, cols], own[1, :, cols])
        put(dest, 0, two[2 * idx], two[2 * idx + 1])

        @pl.when(odd == 0)
        def _():
            put(dest, span, back[2 * idx], back[2 * idx + 1])

    scale = 1.0 / math.sqrt(ATT_DIM)
    row = lax.broadcasted_iota(jnp.int32, (span, reach), 0)
    col = lax.broadcasted_iota(jnp.int32, (span, reach), 1)
    seen = (col > row) & (col <= row + WINDOW) & (chip * span - WINDOW + col >= 0)
    bias[...] = jnp.where(seen, 0.0, MASKED)

    @pl.when(odd == 1)
    def _():
        for copy in copies:
            copy.wait()

    for head in range(wide // ATT_DIM):
        at = slice(head * ATT_DIM, (head + 1) * ATT_DIM)
        scores = nt_dot(quer[:, at], keys[:, at]) + bias[...]
        top = jnp.max(scores, axis=-1, keepdims=True)
        probs = jnp.exp((scores - top) * scale)
        norm = jnp.sum(probs, axis=-1, keepdims=True)
        att = nn_dot(probs.astype(BF16), vals[:, at]) / norm
        out[:, at] = att * lax.rsqrt(jnp.mean(att * att, axis=-1, keepdims=True) + EPS)


def attention(where, quer_in, k_own, v_own, k_near, v_near, two, back, low):
    tokens = quer_in[0].shape[0]
    wide = two.shape[2]
    span = 2 * tokens
    reach = WINDOW + span
    assert WINDOW == 2 * span
    return pl.pallas_call(
        lambda *refs: att_kernel(low, *refs),
        out_shape=jax.ShapeDtypeStruct((span, wide), F32),
        in_specs=[pl.BlockSpec(memory_space=pltpu.SMEM)]
        + [vmem()] * 4
        + [pl.BlockSpec(memory_space=pl.ANY)] * 2
        + [vmem()] * 2,
        out_specs=vmem(),
        scratch_shapes=[
            pltpu.VMEM((span, wide), BF16),
            pltpu.VMEM((reach, wide), BF16),
            pltpu.VMEM((reach, wide), BF16),
            pltpu.VMEM((span, reach), F32),
            pltpu.SemaphoreType.DMA((4,)),
        ],
        compiler_params=grant(30),
        cost_estimate=pl.CostEstimate(
            flops=4 * span * reach * wide,
            bytes_accessed=40 * tokens * wide,
            transcendentals=span * reach * wide // ATT_DIM,
        ),
    )(where, *quer_in, k_own, v_own, k_near, v_near, two, back)


def updated(weights, momentum, grads):
    new_momentum = 0.9 * momentum + grads
    moved = weights - new_momentum
    keep_norm = jnp.sqrt(jnp.mean(weights * weights, axis=-1, keepdims=True))
    new_weights = (
        moved * keep_norm * lax.rsqrt(jnp.mean(moved * moved, axis=-1, keepdims=True) + EPS)
    )
    return new_weights, new_momentum


def layer(queries, key_rows, value_rows, step_rates, fast_weights, momentum, out_gain):
    count = lax.axis_size("seq")
    routes = Routes(count)
    local_tokens = queries.shape[0]
    heads, width = step_rates.shape[0], fast_weights.shape[2]
    assert heads == 2
    here = lax.axis_index("seq")
    core = here % 2
    chip = here // 2
    is_home = core == (2 * here) // count
    where = jnp.stack([core, chip % 2, chip]).astype(jnp.int32)

    my_rate = lax.dynamic_slice_in_dim(step_rates, core, 1, 0)
    their_rate = lax.dynamic_slice_in_dim(step_rates, 1 - core, 1, 0)
    r_own = jnp.concatenate([my_rate, send(their_rate, routes.partner)], axis=0)
    r_near = send(r_own, routes.x_swap)

    def by_core(array):
        kept = lax.dynamic_slice_in_dim(array, core * width, width, 1)
        sent = lax.dynamic_slice_in_dim(array, (1 - core) * width, width, 1)
        return kept, send(sent, routes.partner)

    k_own = jnp.stack(by_core(key_rows))
    v_own = jnp.stack(by_core(value_rows))
    q_own = by_core(queries)

    their_weights = send(fast_weights, routes.pair_in)
    their_momentum = send(momentum, routes.pair_in)

    k_near = send(k_own, routes.x_swap)
    v_near = send(v_own, routes.x_swap)
    cut = 3 * ATT_DIM
    k_held, v_held = lax.optimization_barrier((k_own, v_own))
    early = jnp.concatenate([k_held[:, :, :cut], v_held[:, :, :cut]], axis=0)
    late = jnp.concatenate([k_held[:, :, cut:], v_held[:, :, cut:]], axis=0)
    unit = jnp.concatenate([fast_weights.astype(BF16), their_weights.astype(BF16)], axis=1)
    units = gather_z(unit, routes, is_home)
    side_units = [send(part, routes.y_swap) for part in units]
    grad_scale = 1.0 / math.sqrt(local_tokens * count)
    tokens_in = (k_own, v_own, k_near, v_near, r_own, r_near)

    upper = chip // 2 % 2 == 1
    early_y = send(early, routes.y_swap)
    early_z = send(early_y, routes.z_up_near)
    early_two = jnp.where(upper, early_y, early_z)
    early_back = send(early_two, routes.back_x)
    late_in, _ = lax.optimization_barrier((late, units))
    late_z = send(late_in, routes.z_up_far)

    side_grads = key_side(grad_scale, tokens_in, side_units, BF16)
    side_in = send(side_grads, routes.y_swap)
    own_grads = key_side(grad_scale, tokens_in, units, F32)
    late_turn = jnp.where(upper, late_z, late)
    side_in, late_turn = lax.optimization_barrier((side_in, late_turn))
    late_two = send(late_turn, routes.y_swap)
    late_back = send(late_two, routes.back_x)
    part, *sent = fold(own_grads, side_in)
    arrived = []
    for k in range(len(sent)):
        arrived.append(send(sent[k], routes.cross_back[k]))
    for k in range(1, len(sent)):
        arrived.append(send(sent[k], routes.home_swap[k]))
    att_in = (where, q_own, k_own, v_own, k_near, v_near)
    early_att = attention(*att_in, early_two, early_back, 0)
    late_att = attention(*att_in, late_two, late_back, cut)

    total, pair_new = update_pair(
        part, arrived, fast_weights, their_weights, momentum, their_momentum
    )
    applied = gather_plane(gather_z(pair_new, routes, is_home), routes)
    partner_grads = send(total[1], routes.pair_out)
    gain = lax.dynamic_slice_in_dim(out_gain, core * width, width, 0).reshape(1, width)
    soon = [piece for idx, piece in enumerate(applied) if idx % 4 < 2]
    last = [piece for idx, piece in enumerate(applied) if idx % 4 >= 2]
    sums = query_first(q_own, soon)
    partner_grads, sums = lax.optimization_barrier((partner_grads, sums))
    grads = jnp.where(is_home, total[0], partner_grads)
    new_weights, new_momentum = updated(fast_weights, momentum, grads)
    new_weights, new_momentum, gain = lax.optimization_barrier((new_weights, new_momentum, gain))
    own, other = query_last(where, q_own, last, sums, gain, (early_att, late_att))
    arrived = send(other, routes.partner)
    layer_out = lax.dynamic_update_slice_in_dim(own, arrived, (1 - core) * width, 1)
    return (layer_out, new_weights, new_momentum)


def solution(mesh):
    placed = (
        P(("groups", "seq"), None),
        P(("groups", "seq"), None),
        P(("groups", "seq"), None),
        P(None, ("groups", "seq")),
        P(None, "seq", None),
        P("groups", "seq", None),
        P(),
    )
    return jax.shard_map(
        layer,
        mesh=mesh,
        in_specs=placed,
        out_specs=(P(("groups", "seq"), None), P("groups", "seq", None), P("groups", "seq", None)),
        check_vma=False,
    )
```

```python
import math

import jax
import jax.numpy as jnp
from jax import lax
from jax.experimental import pallas as pl
from jax.experimental.pallas import tpu as pltpu
from jax.sharding import PartitionSpec as P


ATT_DIM = 128
WINDOW = 1024
EPS = 1e-06
MASKED = -1e30
BF16 = jnp.bfloat16
F32 = jnp.float32


class Routes:
    def __init__(self, count):
        self.count = count
        half = count // 16
        self.bits = [1 << b for b in range(half.bit_length() - 1)]
        assert count % 16 == 0 and half == 1 << len(self.bits)
        home = [dev for dev in range(count) if self.is_home(dev)]
        away = [dev for dev in range(count) if not self.is_home(dev)]
        self.partner = [(dev, dev ^ 1) for dev in range(count)]
        self.x_swap = [(dev, dev ^ 2) for dev in range(count)]
        self.y_swap = [(dev, dev ^ 4) for dev in range(count)]
        self.pair_in = [(dev ^ 1, dev) for dev in home]
        self.pair_out = [(dev, dev ^ 1) for dev in home]
        shift = half * 8
        self.cross_out = [(dev, (dev + shift) % count) for dev in home]
        self.home_swap = [[(dev, dev ^ (8 * k)) for dev in home] for k in range(half)]
        self.away_swap = [[(dev, dev ^ (8 * k)) for dev in away] for k in range(half)]
        self.cross_back = [
            [(dev, ((dev ^ (8 * k)) + shift) % count) for dev in away] for k in range(half)
        ]
        self.z_up_near = [(dev, dev + 8) for dev in range(count - 8) if dev % 8 < 4]
        self.z_up_far = [(dev, dev + 8) for dev in range(count - 8) if dev % 8 >= 4]
        self.back_x = [(dev, dev - 2) for dev in range(count) if dev % 4 >= 2]

    def is_home(self, dev):
        return (dev % 2) == (2 * dev // self.count)


def send(array, route):
    return lax.ppermute(array, "seq", route)


def gather_z(unit, routes, is_home):
    home_list = [unit]
    away_list = [send(unit, routes.cross_out)]
    for bit in routes.bits:
        home_list = home_list + [send(part, routes.home_swap[bit]) for part in home_list]
        away_list = away_list + [send(part, routes.away_swap[bit]) for part in away_list]
    return [jnp.where(is_home, home, away) for home, away in zip(home_list, away_list)]


def gather_plane(units, routes):
    pieces = []
    for idx, own in enumerate(units):
        first, second = (
            (routes.x_swap, routes.y_swap) if idx % 2 == 0 else (routes.y_swap, routes.x_swap)
        )
        near = send(own, first)
        side = send(own, second)
        pieces += [own, near, side, send(near, second)]
    return pieces


def fold_kernel(low, arrived, keep, *sent):
    for idx, ref in enumerate(sent):
        total = low[idx] + arrived[idx].astype(F32)
        ref[...] = total.astype(BF16)
        if idx == 0:
            keep[...] = total


def fold(low, arrived):
    shape = low.shape[1:]
    sent = [jax.ShapeDtypeStruct(shape, BF16)] * low.shape[0]
    return pl.pallas_call(
        fold_kernel,
        out_shape=[jax.ShapeDtypeStruct(shape, F32)] + sent,
        in_specs=[vmem(), vmem()],
        out_specs=[vmem()] * (1 + len(sent)),
        compiler_params=grant(10),
        cost_estimate=pl.CostEstimate(flops=low.size, bytes_accessed=12 * low.size, transcendentals=0),
        name="fold",
    )(low, arrived)


def update_kernel(where, part, *refs):
    arrived = refs[:-6]
    w_own, w_near, m_own, m_near, total, applied = refs[-6:]
    owned = w_own.shape[1]

    @pl.when(where[3] == 1)
    def _():
        for idx, (weights, momentum) in enumerate(((w_own, m_own), (w_near, m_near))):
            rows = slice(idx * owned, (idx + 1) * owned)
            grads = part[:, rows]
            for came in arrived:
                grads = grads + came[:, rows].astype(F32)
            total[idx] = grads
            applied[:, rows] = updated(weights[...], momentum[...], grads)[0].astype(BF16)


def update_pair(where, part, arrived, *pairs):
    shape = pairs[0].shape
    rows = (shape[0], 2 * shape[1], shape[2])
    return pl.pallas_call(
        update_kernel,
        out_shape=[
            jax.ShapeDtypeStruct((2,) + shape, F32),
            jax.ShapeDtypeStruct(rows, BF16),
        ],
        in_specs=[pl.BlockSpec(memory_space=pltpu.SMEM)] + [vmem()] * (5 + len(arrived)),
        out_specs=[vmem()] * 2,
        compiler_params=grant(12),
        cost_estimate=pl.CostEstimate(
            flops=20 * math.prod(shape), bytes_accessed=40 * math.prod(shape), transcendentals=0
        ),
        name="update",
    )(where, part, *arrived, *pairs)


def nt_dot(left, right):
    return lax.dot_general(left, right, (((1,), (1,)), ((), ())), preferred_element_type=F32)


def nn_dot(left, right):
    return lax.dot_general(left, right, (((1,), (0,)), ((), ())), preferred_element_type=F32)


def vmem():
    return pl.BlockSpec(memory_space=pltpu.VMEM)


def grant(mebibytes):
    return pltpu.CompilerParams(vmem_limit_bytes=mebibytes << 20)


def key_kernel(grad_scale, *refs):
    k_own, v_own, k_near, v_near, r_own, r_near = refs[:6]
    units = refs[6:-5]
    out, keys, ograd, pair, down = refs[-5:]
    tokens = k_own.shape[1]
    parts = len(units)
    step = units[0].shape[1]
    rows = parts * step
    rates = jnp.concatenate([r_own[...], r_near[...]], axis=0)
    by_token = jnp.transpose(rates * (-grad_scale))
    for idx, (k_ref, v_ref) in enumerate(((k_own, v_own), (k_near, v_near))):
        for side in range(2):
            at = (2 * idx + side) * tokens
            keys[at : at + tokens, :] = k_ref[side]
            rate = by_token[:, 2 * idx + side : 2 * idx + side + 1]
            ograd[at : at + tokens, :] = (rate * v_ref[side].astype(F32)).astype(BF16)
    for idx in range(parts):
        pair[idx * step : (idx + 1) * step, :] = units[idx][0]
        pair[rows + idx * step : rows + (idx + 1) * step, :] = units[idx][1]
        down[idx * step : (idx + 1) * step, :] = units[idx][2]
    both = nt_dot(pair[...], keys[...])
    gate, up = both[:rows], both[rows:]
    hidden_grad = nt_dot(down[...], ograd[...])
    sig = jax.nn.sigmoid(gate)
    silu = gate * sig
    hidden = (silu * up).astype(BF16)
    gate_grad = (hidden_grad * up * (sig * (1.0 + gate * (1.0 - sig)))).astype(BF16)
    up_grad = (hidden_grad * silu).astype(BF16)
    first = nn_dot(jnp.concatenate([gate_grad, up_grad], axis=0), keys[...])
    second = nn_dot(hidden, ograd[...])
    for idx in range(parts):
        at = idx * step
        out[idx, 0] = first[at : at + step].astype(out.dtype)
        out[idx, 1] = first[rows + at : rows + at + step].astype(out.dtype)
        out[idx, 2] = second[at : at + step].astype(out.dtype)


def key_side(grad_scale, tokens_in, units, kind):
    _, tokens, width = tokens_in[0].shape
    parts = len(units)
    step = units[0].shape[1]
    rows = parts * step
    return pl.pallas_call(
        lambda *refs: key_kernel(grad_scale, *refs),
        out_shape=jax.ShapeDtypeStruct((parts, 3, step, width), kind),
        in_specs=[vmem()] * (6 + parts),
        out_specs=vmem(),
        scratch_shapes=[
            pltpu.VMEM((4 * tokens, width), BF16),
            pltpu.VMEM((4 * tokens, width), BF16),
            pltpu.VMEM((2 * rows, width), BF16),
            pltpu.VMEM((rows, width), BF16),
        ],
        compiler_params=grant(30),
        cost_estimate=pl.CostEstimate(
            flops=12 * 4 * tokens * rows * width,
            bytes_accessed=16 * tokens * width,
            transcendentals=0,
        ),
    )(*tokens_in, *units)


def load_rows(pieces, weights):
    rows = pieces[0].shape[1]
    for idx, piece in enumerate(pieces):
        weights[:, idx * rows : (idx + 1) * rows, :] = piece[...]


def fast_product(quer_in, weights):
    quer = jnp.concatenate([part[...] for part in quer_in], axis=0)
    gate = nt_dot(quer, weights[0])
    up = nt_dot(quer, weights[1])
    hidden = (gate * jax.nn.sigmoid(gate) * up).astype(BF16)
    return nn_dot(hidden, weights[2])


def query_first_kernel(count, *refs):
    quer_in = refs[:2]
    out, weights = refs[2 + count :]
    load_rows(refs[2 : 2 + count], weights)
    out[...] = fast_product(quer_in, weights)


def query_first(quer_in, pieces):
    tokens, width = quer_in[0].shape
    count = len(pieces)
    rows = pieces[0].shape[1]
    return pl.pallas_call(
        lambda *refs: query_first_kernel(count, *refs),
        out_shape=jax.ShapeDtypeStruct((2 * tokens, width), F32),
        in_specs=[vmem()] * (2 + count),
        out_specs=vmem(),
        scratch_shapes=[pltpu.VMEM((3, count * rows, width), BF16)],
        compiler_params=grant(24),
        cost_estimate=pl.CostEstimate(
            flops=12 * tokens * count * rows * width,
            bytes_accessed=6 * count * rows * width,
            transcendentals=0,
        ),
        name="query_first",
    )(*quer_in, *pieces)


def query_last_kernel(count, *refs):
    where, quer_in = refs[0], refs[1:3]
    sums, gain, att_a, att_b, own, other, weights = refs[3 + count :]
    tokens, width = other.shape
    load_rows(refs[3 : 3 + count], weights)
    fast = sums[...] + fast_product(quer_in, weights)
    scale = lax.rsqrt(jnp.mean(fast * fast, axis=-1, keepdims=True) + EPS)
    normed = fast * scale * gain[...]
    here = pl.multiple_of(where[0] * width, ATT_DIM)
    at = [pl.multiple_of(core * tokens, tokens) for core in (where[0], 1 - where[0])]
    att = [
        jnp.concatenate([ref[pl.ds(base, tokens), :] for ref in (att_a, att_b)], axis=1)
        for base in at
    ]
    own[:, pl.ds(here, width)] = (normed[:tokens] + att[0]).astype(BF16)
    other[...] = (normed[tokens:] + att[1]).astype(BF16)


def query_last(where, quer_in, pieces, sums, gain, atts):
    tokens, width = quer_in[0].shape
    count = len(pieces)
    rows = pieces[0].shape[1]
    return pl.pallas_call(
        lambda *refs: query_last_kernel(count, *refs),
        out_shape=[
            jax.ShapeDtypeStruct((tokens, 2 * width), BF16),
            jax.ShapeDtypeStruct((tokens, width), BF16),
        ],
        in_specs=[pl.BlockSpec(memory_space=pltpu.SMEM)] + [vmem()] * (6 + count),
        out_specs=[vmem()] * 2,
        scratch_shapes=[pltpu.VMEM((3, count * rows, width), BF16)],
        compiler_params=grant(24),
        cost_estimate=pl.CostEstimate(
            flops=12 * tokens * count * rows * width,
            bytes_accessed=6 * count * rows * width,
            transcendentals=0,
        ),
        name="query_last",
    )(where, *quer_in, *pieces, sums, gain, *atts)


def att_kernel(low, where, q_kept, q_came, k_own, v_own, k_near, v_near, two, back, out,
               quer, keys, vals, bias, arrivals):
    tokens = q_kept.shape[0]
    span = 2 * tokens
    reach = WINDOW + span
    wide = out.shape[1]
    cols = slice(low, low + wide)
    core, odd, chip = where[0], where[1], where[2]
    mine = core * tokens
    theirs = (1 - core) * tokens

    copies = []
    for idx, (dest, near) in enumerate(((keys, k_near), (vals, v_near))):
        for side, at in enumerate((mine, theirs)):
            rows = pl.ds(pl.multiple_of(span + at, tokens), tokens)
            copies.append(
                pltpu.make_async_copy(
                    near.at[side, :, pl.ds(low, wide)], dest.at[rows], arrivals.at[2 * idx + side]
                )
            )

    @pl.when(odd == 1)
    def _():
        for copy in copies:
            copy.start()

    def put(dest, base, first, second):
        dest[pl.ds(pl.multiple_of(base + mine, tokens), tokens), :] = first
        dest[pl.ds(pl.multiple_of(base + theirs, tokens), tokens), :] = second

    put(quer, 0, q_kept[:, cols], q_came[:, cols])
    for idx, (dest, own) in enumerate(((keys, k_own), (vals, v_own))):
        put(dest, 2 * span, own[0, :, cols], own[1, :, cols])
        put(dest, 0, two[2 * idx], two[2 * idx + 1])

        @pl.when(odd == 0)
        def _():
            put(dest, span, back[2 * idx], back[2 * idx + 1])

    scale = 1.0 / math.sqrt(ATT_DIM)
    row = lax.broadcasted_iota(jnp.int32, (span, reach), 0)
    col = lax.broadcasted_iota(jnp.int32, (span, reach), 1)
    seen = (col > row) & (col <= row + WINDOW) & (chip * span - WINDOW + col >= 0)
    bias[...] = jnp.where(seen, 0.0, MASKED)

    @pl.when(odd == 1)
    def _():
        for copy in copies:
            copy.wait()

    for head in range(wide // ATT_DIM):
        at = slice(head * ATT_DIM, (head + 1) * ATT_DIM)
        scores = nt_dot(quer[:, at], keys[:, at]) + bias[...]
        top = jnp.max(scores, axis=-1, keepdims=True)
        probs = jnp.exp((scores - top) * scale)
        norm = jnp.sum(probs, axis=-1, keepdims=True)
        att = nn_dot(probs.astype(BF16), vals[:, at]) / norm
        out[:, at] = att * lax.rsqrt(jnp.mean(att * att, axis=-1, keepdims=True) + EPS)


def attention(where, quer_in, k_own, v_own, k_near, v_near, two, back, low, space):
    tokens = quer_in[0].shape[0]
    wide = two.shape[2]
    span = 2 * tokens
    reach = WINDOW + span
    assert WINDOW == 2 * span
    return pl.pallas_call(
        lambda *refs: att_kernel(low, *refs),
        out_shape=jax.ShapeDtypeStruct((span, wide), F32),
        in_specs=[pl.BlockSpec(memory_space=pltpu.SMEM)]
        + [vmem()] * 4
        + [pl.BlockSpec(memory_space=space)] * 2
        + [vmem()] * 2,
        out_specs=vmem(),
        scratch_shapes=[
            pltpu.VMEM((span, wide), BF16),
            pltpu.VMEM((reach, wide), BF16),
            pltpu.VMEM((reach, wide), BF16),
            pltpu.VMEM((span, reach), F32),
            pltpu.SemaphoreType.DMA((4,)),
        ],
        compiler_params=grant(30),
        cost_estimate=pl.CostEstimate(
            flops=4 * span * reach * wide,
            bytes_accessed=40 * tokens * wide,
            transcendentals=span * reach * wide // ATT_DIM,
        ),
    )(where, *quer_in, k_own, v_own, k_near, v_near, two, back)


def updated(weights, momentum, grads):
    new_momentum = 0.9 * momentum + grads
    moved = weights - new_momentum
    keep_norm = jnp.sqrt(jnp.mean(weights * weights, axis=-1, keepdims=True))
    new_weights = (
        moved * keep_norm * lax.rsqrt(jnp.mean(moved * moved, axis=-1, keepdims=True) + EPS)
    )
    return new_weights, new_momentum


def layer(queries, key_rows, value_rows, step_rates, fast_weights, momentum, out_gain):
    count = lax.axis_size("seq")
    routes = Routes(count)
    local_tokens = queries.shape[0]
    heads, width = step_rates.shape[0], fast_weights.shape[2]
    assert heads == 2
    here = lax.axis_index("seq")
    core = here % 2
    chip = here // 2
    is_home = core == (2 * here) // count
    where = jnp.stack([core, chip % 2, chip, is_home.astype(jnp.int32)]).astype(jnp.int32)

    my_rate = lax.dynamic_slice_in_dim(step_rates, core, 1, 0)
    their_rate = lax.dynamic_slice_in_dim(step_rates, 1 - core, 1, 0)
    r_own = jnp.concatenate([my_rate, send(their_rate, routes.partner)], axis=0)
    r_near = send(r_own, routes.x_swap)

    def by_core(array):
        kept = lax.dynamic_slice_in_dim(array, core * width, width, 1)
        sent = lax.dynamic_slice_in_dim(array, (1 - core) * width, width, 1)
        return kept, send(sent, routes.partner)

    k_own = jnp.stack(by_core(key_rows))
    v_own = jnp.stack(by_core(value_rows))
    q_own = by_core(queries)

    their_weights = send(fast_weights, routes.pair_in)
    their_momentum = send(momentum, routes.pair_in)

    k_near = send(k_own, routes.x_swap)
    v_near = send(v_own, routes.x_swap)
    cut = 3 * ATT_DIM
    k_held, v_held = lax.optimization_barrier((k_own, v_own))
    early = jnp.concatenate([k_held[:, :, :cut], v_held[:, :, :cut]], axis=0)
    late = jnp.concatenate([k_held[:, :, cut:], v_held[:, :, cut:]], axis=0)
    unit = jnp.concatenate([fast_weights.astype(BF16), their_weights.astype(BF16)], axis=1)
    units = gather_z(unit, routes, is_home)
    side_units = [send(part, routes.y_swap) for part in units]
    grad_scale = 1.0 / math.sqrt(local_tokens * count)
    tokens_in = (k_own, v_own, k_near, v_near, r_own, r_near)

    upper = chip // 2 % 2 == 1
    early_y = send(early, routes.y_swap)
    early_z = send(early_y, routes.z_up_near)
    early_two = jnp.where(upper, early_y, early_z)
    early_back = send(early_two, routes.back_x)
    late_in, _ = lax.optimization_barrier((late, units))
    late_z = send(late_in, routes.z_up_far)

    side_grads = key_side(grad_scale, tokens_in, side_units, BF16)
    side_in = send(side_grads, routes.y_swap)
    own_grads = key_side(grad_scale, tokens_in, units, F32)
    late_turn = jnp.where(upper, late_z, late)
    side_in, late_turn = lax.optimization_barrier((side_in, late_turn))
    late_two = send(late_turn, routes.y_swap)
    late_back = send(late_two, routes.back_x)
    part, *sent = fold(own_grads, side_in)
    arrived = []
    for k in range(len(sent)):
        arrived.append(send(sent[k], routes.cross_back[k]))
    for k in range(1, len(sent)):
        arrived.append(send(sent[k], routes.home_swap[k]))
    att_in = (where, q_own, k_own, v_own, k_near, v_near)
    early_att = attention(*att_in, early_two, early_back, 0, pl.ANY)
    late_att = attention(*att_in, late_two, late_back, cut, pltpu.VMEM)

    total, pair_new = update_pair(
        where, part, arrived, fast_weights, their_weights, momentum, their_momentum
    )
    applied = gather_plane(gather_z(pair_new, routes, is_home), routes)
    partner_grads = send(total[1], routes.pair_out)
    gain = lax.dynamic_slice_in_dim(out_gain, core * width, width, 0).reshape(1, width)
    soon = [piece for idx, piece in enumerate(applied) if idx % 4 < 2]
    last = [piece for idx, piece in enumerate(applied) if idx % 4 >= 2]
    sums = query_first(q_own, soon)
    partner_grads, sums = lax.optimization_barrier((partner_grads, sums))
    grads = jnp.where(is_home, total[0], partner_grads)
    new_weights, new_momentum = updated(fast_weights, momentum, grads)
    new_weights, new_momentum, gain = lax.optimization_barrier((new_weights, new_momentum, gain))
    own, other = query_last(where, q_own, last, sums, gain, (early_att, late_att))
    arrived = send(other, routes.partner)
    layer_out = lax.dynamic_update_slice_in_dim(own, arrived, (1 - core) * width, 1)
    return (layer_out, new_weights, new_momentum)


def solution(mesh):
    placed = (
        P(("groups", "seq"), None),
        P(("groups", "seq"), None),
        P(("groups", "seq"), None),
        P(None, ("groups", "seq")),
        P(None, "seq", None),
        P("groups", "seq", None),
        P(),
    )
    return jax.shard_map(
        layer,
        mesh=mesh,
        in_specs=placed,
        out_specs=(P(("groups", "seq"), None), P("groups", "seq", None), P("groups", "seq", None)),
        check_vma=False,
    )
```

```python
import math

import jax
import jax.numpy as jnp
from jax import lax
from jax.experimental import pallas as pl
from jax.experimental.pallas import tpu as pltpu
from jax.sharding import PartitionSpec as P


ATT_DIM = 128
WINDOW = 1024
EPS = 1e-06
MASKED = -1e30
BF16 = jnp.bfloat16
F32 = jnp.float32


class Routes:
    def __init__(self, count):
        self.count = count
        half = count // 16
        self.bits = [1 << b for b in range(half.bit_length() - 1)]
        assert count % 16 == 0 and half == 1 << len(self.bits)
        home = [dev for dev in range(count) if self.is_home(dev)]
        away = [dev for dev in range(count) if not self.is_home(dev)]
        self.partner = [(dev, dev ^ 1) for dev in range(count)]
        self.x_swap = [(dev, dev ^ 2) for dev in range(count)]
        self.y_swap = [(dev, dev ^ 4) for dev in range(count)]
        self.pair_in = [(dev ^ 1, dev) for dev in home]
        self.pair_out = [(dev, dev ^ 1) for dev in home]
        shift = half * 8
        self.cross_out = [(dev, (dev + shift) % count) for dev in home]
        self.home_swap = [[(dev, dev ^ (8 * k)) for dev in home] for k in range(half)]
        self.away_swap = [[(dev, dev ^ (8 * k)) for dev in away] for k in range(half)]
        self.cross_back = [
            [(dev, ((dev ^ (8 * k)) + shift) % count) for dev in away] for k in range(half)
        ]
        self.z_up_near = [(dev, dev + 8) for dev in range(count - 8) if dev % 8 < 4]
        self.z_up_far = [(dev, dev + 8) for dev in range(count - 8) if dev % 8 >= 4]
        self.back_x = [(dev, dev - 2) for dev in range(count) if dev % 4 >= 2]

    def is_home(self, dev):
        return (dev % 2) == (2 * dev // self.count)


def send(array, route):
    return lax.ppermute(array, "seq", route)


def gather_z(unit, routes, is_home):
    home_list = [unit]
    away_list = [send(unit, routes.cross_out)]
    for bit in routes.bits:
        home_list = home_list + [send(part, routes.home_swap[bit]) for part in home_list]
        away_list = away_list + [send(part, routes.away_swap[bit]) for part in away_list]
    return [jnp.where(is_home, home, away) for home, away in zip(home_list, away_list)]


def gather_plane(units, routes):
    pieces = []
    for idx, own in enumerate(units):
        first, second = (
            (routes.x_swap, routes.y_swap) if idx % 2 == 0 else (routes.y_swap, routes.x_swap)
        )
        near = send(own, first)
        side = send(own, second)
        pieces += [own, near, side, send(near, second)]
    return pieces


def fold_kernel(low, arrived, keep, *sent):
    for idx, ref in enumerate(sent):
        total = low[idx] + arrived[idx].astype(F32)
        ref[...] = total.astype(BF16)
        if idx == 0:
            keep[...] = total


def fold(low, arrived):
    shape = low.shape[1:]
    sent = [jax.ShapeDtypeStruct(shape, BF16)] * low.shape[0]
    return pl.pallas_call(
        fold_kernel,
        out_shape=[jax.ShapeDtypeStruct(shape, F32)] + sent,
        in_specs=[vmem(), vmem()],
        out_specs=[vmem()] * (1 + len(sent)),
        compiler_params=grant(10),
        cost_estimate=pl.CostEstimate(flops=low.size, bytes_accessed=12 * low.size, transcendentals=0),
        name="fold",
    )(low, arrived)


def update_kernel(where, part, *refs):
    arrived = refs[:-6]
    w_own, w_near, m_own, m_near, total, applied = refs[-6:]
    owned = w_own.shape[1]

    @pl.when(where[3] == 1)
    def _():
        for idx, (weights, momentum) in enumerate(((w_own, m_own), (w_near, m_near))):
            rows = slice(idx * owned, (idx + 1) * owned)
            grads = part[:, rows]
            for came in arrived:
                grads = grads + came[:, rows].astype(F32)
            total[idx] = grads
            applied[:, rows] = updated(weights[...], momentum[...], grads)[0].astype(BF16)


def update_pair(where, part, arrived, *pairs):
    shape = pairs[0].shape
    rows = (shape[0], 2 * shape[1], shape[2])
    return pl.pallas_call(
        update_kernel,
        out_shape=[
            jax.ShapeDtypeStruct((2,) + shape, F32),
            jax.ShapeDtypeStruct(rows, BF16),
        ],
        in_specs=[pl.BlockSpec(memory_space=pltpu.SMEM)] + [vmem()] * (5 + len(arrived)),
        out_specs=[vmem()] * 2,
        compiler_params=grant(12),
        cost_estimate=pl.CostEstimate(
            flops=20 * math.prod(shape), bytes_accessed=40 * math.prod(shape), transcendentals=0
        ),
        name="update",
    )(where, part, *arrived, *pairs)


def nt_dot(left, right):
    return lax.dot_general(left, right, (((1,), (1,)), ((), ())), preferred_element_type=F32)


def nn_dot(left, right):
    return lax.dot_general(left, right, (((1,), (0,)), ((), ())), preferred_element_type=F32)


def vmem():
    return pl.BlockSpec(memory_space=pltpu.VMEM)


def grant(mebibytes):
    return pltpu.CompilerParams(vmem_limit_bytes=mebibytes << 20)


def key_kernel(grad_scale, *refs):
    k_own, v_own, k_near, v_near, r_own, r_near = refs[:6]
    units = refs[6:-5]
    out, keys, ograd, pair, down = refs[-5:]
    tokens = k_own.shape[1]
    parts = len(units)
    step = units[0].shape[1]
    rows = parts * step
    rates = jnp.concatenate([r_own[...], r_near[...]], axis=0)
    by_token = jnp.transpose(rates * (-grad_scale))
    for idx, (k_ref, v_ref) in enumerate(((k_own, v_own), (k_near, v_near))):
        for side in range(2):
            at = (2 * idx + side) * tokens
            keys[at : at + tokens, :] = k_ref[side]
            rate = by_token[:, 2 * idx + side : 2 * idx + side + 1]
            ograd[at : at + tokens, :] = (rate * v_ref[side].astype(F32)).astype(BF16)
    for idx in range(parts):
        pair[idx * step : (idx + 1) * step, :] = units[idx][0]
        pair[rows + idx * step : rows + (idx + 1) * step, :] = units[idx][1]
        down[idx * step : (idx + 1) * step, :] = units[idx][2]
    both = nt_dot(pair[...], keys[...])
    gate, up = both[:rows], both[rows:]
    hidden_grad = nt_dot(down[...], ograd[...])
    sig = jax.nn.sigmoid(gate)
    silu = gate * sig
    hidden = (silu * up).astype(BF16)
    gate_grad = (hidden_grad * up * (sig * (1.0 + gate * (1.0 - sig)))).astype(BF16)
    up_grad = (hidden_grad * silu).astype(BF16)
    first = nn_dot(jnp.concatenate([gate_grad, up_grad], axis=0), keys[...])
    second = nn_dot(hidden, ograd[...])
    for idx in range(parts):
        at = idx * step
        out[idx, 0] = first[at : at + step].astype(out.dtype)
        out[idx, 1] = first[rows + at : rows + at + step].astype(out.dtype)
        out[idx, 2] = second[at : at + step].astype(out.dtype)


def key_side(grad_scale, tokens_in, units, kind):
    _, tokens, width = tokens_in[0].shape
    parts = len(units)
    step = units[0].shape[1]
    rows = parts * step
    return pl.pallas_call(
        lambda *refs: key_kernel(grad_scale, *refs),
        out_shape=jax.ShapeDtypeStruct((parts, 3, step, width), kind),
        in_specs=[vmem()] * (6 + parts),
        out_specs=vmem(),
        scratch_shapes=[
            pltpu.VMEM((4 * tokens, width), BF16),
            pltpu.VMEM((4 * tokens, width), BF16),
            pltpu.VMEM((2 * rows, width), BF16),
            pltpu.VMEM((rows, width), BF16),
        ],
        compiler_params=grant(30),
        cost_estimate=pl.CostEstimate(
            flops=12 * 4 * tokens * rows * width,
            bytes_accessed=16 * tokens * width,
            transcendentals=0,
        ),
    )(*tokens_in, *units)


def load_rows(pieces, weights):
    rows = pieces[0].shape[1]
    for idx, piece in enumerate(pieces):
        weights[:, idx * rows : (idx + 1) * rows, :] = piece[...]


def fast_product(quer_in, weights):
    quer = jnp.concatenate([part[...] for part in quer_in], axis=0)
    gate = nt_dot(quer, weights[0])
    up = nt_dot(quer, weights[1])
    hidden = (gate * jax.nn.sigmoid(gate) * up).astype(BF16)
    return nn_dot(hidden, weights[2])


def query_first_kernel(count, *refs):
    quer_in = refs[:2]
    out, weights = refs[2 + count :]
    load_rows(refs[2 : 2 + count], weights)
    out[...] = fast_product(quer_in, weights)


def query_first(quer_in, pieces):
    tokens, width = quer_in[0].shape
    count = len(pieces)
    rows = pieces[0].shape[1]
    return pl.pallas_call(
        lambda *refs: query_first_kernel(count, *refs),
        out_shape=jax.ShapeDtypeStruct((2 * tokens, width), F32),
        in_specs=[vmem()] * (2 + count),
        out_specs=vmem(),
        scratch_shapes=[pltpu.VMEM((3, count * rows, width), BF16)],
        compiler_params=grant(24),
        cost_estimate=pl.CostEstimate(
            flops=12 * tokens * count * rows * width,
            bytes_accessed=6 * count * rows * width,
            transcendentals=0,
        ),
        name="query_first",
    )(*quer_in, *pieces)


def query_last_kernel(count, side, where, quer_in, *refs):
    sums, gain, att_a, att_b, out, weights = refs[count:]
    tokens, width = quer_in.shape
    load_rows(refs[:count], weights)
    fast = sums[side * tokens : (side + 1) * tokens, :] + fast_product([quer_in], weights)
    scale = lax.rsqrt(jnp.mean(fast * fast, axis=-1, keepdims=True) + EPS)
    core = where[0] if side == 0 else 1 - where[0]
    rows = pl.ds(pl.multiple_of(core * tokens, tokens), tokens)
    att = jnp.concatenate([att_a[rows, :], att_b[rows, :]], axis=1)
    result = (fast * scale * gain[...] + att).astype(BF16)
    if side == 0:
        out[:, pl.ds(pl.multiple_of(where[0] * width, ATT_DIM), width)] = result
    else:
        out[...] = result


def query_last(where, quer_in, pieces, sums, gain, atts, side):
    tokens, width = quer_in.shape
    count = len(pieces)
    rows = pieces[0].shape[1]
    return pl.pallas_call(
        lambda *refs: query_last_kernel(count, side, *refs),
        out_shape=jax.ShapeDtypeStruct((tokens, (2 - side) * width), BF16),
        in_specs=[pl.BlockSpec(memory_space=pltpu.SMEM)] + [vmem()] * (5 + count),
        out_specs=vmem(),
        scratch_shapes=[pltpu.VMEM((3, count * rows, width), BF16)],
        compiler_params=grant(24),
        cost_estimate=pl.CostEstimate(
            flops=6 * tokens * count * rows * width,
            bytes_accessed=6 * count * rows * width,
            transcendentals=0,
        ),
    )(where, quer_in, *pieces, sums, gain, *atts)


def att_kernel(low, where, q_kept, q_came, k_own, v_own, k_near, v_near, two, back, out,
               quer, keys, vals, bias, arrivals):
    tokens = q_kept.shape[0]
    span = 2 * tokens
    wide = out.shape[1]
    cols = slice(low, low + wide)
    core, odd, chip = where[0], where[1], where[2]
    mine = core * tokens
    theirs = (1 - core) * tokens

    copies = []
    for idx, (dest, near) in enumerate(((keys, k_near), (vals, v_near))):
        for side, at in enumerate((mine, theirs)):
            rows = pl.ds(pl.multiple_of(span + at, tokens), tokens)
            copies.append(
                pltpu.make_async_copy(
                    near.at[side, :, pl.ds(low, wide)], dest.at[rows], arrivals.at[2 * idx + side]
                )
            )

    @pl.when(odd == 1)
    def _():
        for copy in copies:
            copy.start()

    def put(dest, base, first, second):
        dest[pl.ds(pl.multiple_of(base + mine, tokens), tokens), :] = first
        dest[pl.ds(pl.multiple_of(base + theirs, tokens), tokens), :] = second

    put(quer, 0, q_kept[:, cols], q_came[:, cols])
    for idx, (dest, own) in enumerate(((keys, k_own), (vals, v_own))):
        put(dest, 2 * span, own[0, :, cols], own[1, :, cols])
        put(dest, 0, two[2 * idx], two[2 * idx + 1])

        @pl.when(odd == 0)
        def _():
            put(dest, span, back[2 * idx], back[2 * idx + 1])

    scale = 1.0 / math.sqrt(ATT_DIM)
    row = lax.broadcasted_iota(jnp.int32, (span, span), 0)
    col = lax.broadcasted_iota(jnp.int32, (span, span), 1)
    bias[0] = jnp.where((col > row) & (chip >= 2), 0.0, MASKED)
    bias[1] = jnp.where(col <= row, 0.0, MASKED)
    middle = jnp.where(chip >= 1, 0.0, MASKED)

    @pl.when(odd == 1)
    def _():
        for copy in copies:
            copy.wait()

    for head in range(wide // ATT_DIM):
        at = slice(head * ATT_DIM, (head + 1) * ATT_DIM)
        blocks = [slice(idx * span, (idx + 1) * span) for idx in range(3)]
        scores = [nt_dot(quer[:, at], keys[rows, at]) for rows in blocks]
        scores = [scores[0] + bias[0], scores[1] + middle, scores[2] + bias[1]]
        tops = [jnp.max(part, axis=-1, keepdims=True) for part in scores]
        top = jnp.maximum(jnp.maximum(tops[0], tops[1]), tops[2])
        probs = [jnp.exp((part - top) * scale) for part in scores]
        norm = sum(jnp.sum(part, axis=-1, keepdims=True) for part in probs)
        att = sum(nn_dot(part.astype(BF16), vals[rows, at]) for part, rows in zip(probs, blocks))
        att = att / norm
        out[:, at] = att * lax.rsqrt(jnp.mean(att * att, axis=-1, keepdims=True) + EPS)


def attention(where, quer_in, k_own, v_own, k_near, v_near, two, back, low, space):
    tokens = quer_in[0].shape[0]
    wide = two.shape[2]
    span = 2 * tokens
    reach = WINDOW + span
    assert WINDOW == 2 * span
    return pl.pallas_call(
        lambda *refs: att_kernel(low, *refs),
        out_shape=jax.ShapeDtypeStruct((span, wide), F32),
        in_specs=[pl.BlockSpec(memory_space=pltpu.SMEM)]
        + [vmem()] * 4
        + [pl.BlockSpec(memory_space=space)] * 2
        + [vmem()] * 2,
        out_specs=vmem(),
        scratch_shapes=[
            pltpu.VMEM((span, wide), BF16),
            pltpu.VMEM((reach, wide), BF16),
            pltpu.VMEM((reach, wide), BF16),
            pltpu.VMEM((2, span, span), F32),
            pltpu.SemaphoreType.DMA((4,)),
        ],
        compiler_params=grant(30),
        cost_estimate=pl.CostEstimate(
            flops=4 * span * reach * wide,
            bytes_accessed=40 * tokens * wide,
            transcendentals=span * reach * wide // ATT_DIM,
        ),
    )(where, *quer_in, k_own, v_own, k_near, v_near, two, back)


def updated(weights, momentum, grads):
    new_momentum = 0.9 * momentum + grads
    moved = weights - new_momentum
    keep_norm = jnp.sqrt(jnp.mean(weights * weights, axis=-1, keepdims=True))
    new_weights = (
        moved * keep_norm * lax.rsqrt(jnp.mean(moved * moved, axis=-1, keepdims=True) + EPS)
    )
    return new_weights, new_momentum


def layer(queries, key_rows, value_rows, step_rates, fast_weights, momentum, out_gain):
    count = lax.axis_size("seq")
    routes = Routes(count)
    local_tokens = queries.shape[0]
    heads, width = step_rates.shape[0], fast_weights.shape[2]
    assert heads == 2
    here = lax.axis_index("seq")
    core = here % 2
    chip = here // 2
    is_home = core == (2 * here) // count
    where = jnp.stack([core, chip % 2, chip, is_home.astype(jnp.int32)]).astype(jnp.int32)

    my_rate = lax.dynamic_slice_in_dim(step_rates, core, 1, 0)
    their_rate = lax.dynamic_slice_in_dim(step_rates, 1 - core, 1, 0)
    r_own = jnp.concatenate([my_rate, send(their_rate, routes.partner)], axis=0)
    r_near = send(r_own, routes.x_swap)

    def by_core(array):
        kept = lax.dynamic_slice_in_dim(array, core * width, width, 1)
        sent = lax.dynamic_slice_in_dim(array, (1 - core) * width, width, 1)
        return kept, send(sent, routes.partner)

    k_own = jnp.stack(by_core(key_rows))
    v_own = jnp.stack(by_core(value_rows))

    their_weights = send(fast_weights, routes.pair_in)
    their_momentum = send(momentum, routes.pair_in)

    k_near = send(k_own, routes.x_swap)
    v_near = send(v_own, routes.x_swap)
    cut = 2 * ATT_DIM
    k_held, v_held = lax.optimization_barrier((k_own, v_own))
    early = jnp.concatenate([k_held[:, :, :cut], v_held[:, :, :cut]], axis=0)
    late = jnp.concatenate([k_held[:, :, cut:], v_held[:, :, cut:]], axis=0)
    unit = jnp.concatenate([fast_weights.astype(BF16), their_weights.astype(BF16)], axis=1)
    units = gather_z(unit, routes, is_home)
    side_units = [send(part, routes.y_swap) for part in units]
    grad_scale = 1.0 / math.sqrt(local_tokens * count)
    tokens_in = (k_own, v_own, k_near, v_near, r_own, r_near)

    upper = chip // 2 % 2 == 1
    early_y = send(early, routes.y_swap)
    early_z = send(early_y, routes.z_up_near)
    early_two = jnp.where(upper, early_y, early_z)
    early_back = send(early_two, routes.back_x)
    late_in, _ = lax.optimization_barrier((late, units))
    late_z = send(late_in, routes.z_up_far)

    side_grads = key_side(grad_scale, tokens_in, side_units, BF16)
    queries, side_grads = lax.optimization_barrier((queries, side_grads))
    q_own = by_core(queries)
    side_in = send(side_grads, routes.y_swap)
    own_grads = key_side(grad_scale, tokens_in, units, F32)
    late_turn = jnp.where(upper, late_z, late)
    side_in, late_turn = lax.optimization_barrier((side_in, late_turn))
    late_two = send(late_turn, routes.y_swap)
    late_back = send(late_two, routes.back_x)
    part, *sent = fold(own_grads, side_in)
    arrived = []
    for k in range(len(sent)):
        arrived.append(send(sent[k], routes.cross_back[k]))
    for k in range(1, len(sent)):
        arrived.append(send(sent[k], routes.home_swap[k]))
    att_in = (where, q_own, k_own, v_own, k_near, v_near)
    early_att = attention(*att_in, early_two, early_back, 0, pl.ANY)
    late_att = attention(*att_in, late_two, late_back, cut, pltpu.VMEM)

    total, pair_new = update_pair(
        where, part, arrived, fast_weights, their_weights, momentum, their_momentum
    )
    applied = gather_plane(gather_z(pair_new, routes, is_home), routes)
    partner_grads = send(total[1], routes.pair_out)
    gain = lax.dynamic_slice_in_dim(out_gain, core * width, width, 0).reshape(1, width)
    soon = [piece for idx, piece in enumerate(applied) if idx % 4 < 2]
    last = [piece for idx, piece in enumerate(applied) if idx % 4 >= 2]
    sums = query_first(q_own, soon)
    partner_grads, sums = lax.optimization_barrier((partner_grads, sums))
    grads = jnp.where(is_home, total[0], partner_grads)
    new_weights, new_momentum = updated(fast_weights, momentum, grads)
    new_weights, new_momentum, gain = lax.optimization_barrier((new_weights, new_momentum, gain))
    last_in = (last, sums, gain, (early_att, late_att))
    other = query_last(where, q_own[1], *last_in, 1)
    arrived = send(other, routes.partner)
    own = query_last(where, q_own[0], *last_in, 0)
    layer_out = lax.dynamic_update_slice_in_dim(own, arrived, (1 - core) * width, 1)
    return (layer_out, new_weights, new_momentum)


def solution(mesh):
    placed = (
        P(("groups", "seq"), None),
        P(("groups", "seq"), None),
        P(("groups", "seq"), None),
        P(None, ("groups", "seq")),
        P(None, "seq", None),
        P("groups", "seq", None),
        P(),
    )
    return jax.shard_map(
        layer,
        mesh=mesh,
        in_specs=placed,
        out_specs=(P(("groups", "seq"), None), P("groups", "seq", None), P("groups", "seq", None)),
        check_vma=False,
    )
```
